32 devices in a mesh: seq: 4 (over x, core), fsdp: 8 (over z, y).
Axes of the slice: x: 2, y: 2, z: 4, core: 2. Of those that a mesh axis runs over, the one named last changes fastest.
Arguments:
- tokens: bfloat16 [2048, 8, 768], P(('seq', 'fsdp')), may hold values from -6 to 6
- pass_index: int32 [2048, 8], P(('seq', 'fsdp')), may hold values from 0 to 4
- lengths: int32 [8], replicated, may hold values from 1 to 2048, 12288 in all
- table: bfloat16 [5, 768], replicated, may hold values from -3 to 3
- gain_attn: bfloat16 [768], P('fsdp'), may hold values from 0.5 to 1.5
- w_qkv: bfloat16 [768, 2304], P('fsdp'), may hold values from -0.21875 to 0.21875
- w_out: bfloat16 [768, 768], P('fsdp'), may hold values from -1.25 to 1.25
- gain_mlp: bfloat16 [768], P('fsdp'), may hold values from 0.5 to 1.5
- w_up: bfloat16 [768, 3072], P('fsdp'), may hold values from -0.21875 to 0.21875
- w_down: bfloat16 [3072, 768], P('fsdp'), may hold values from -0.109375 to 0.109375
- cotangent: bfloat16 [2048, 8, 768], P(('seq', 'fsdp')), may hold values from -6 to 6
Outputs:
- output: bfloat16 [2048, 8, 768], P(('seq', 'fsdp'))
- d_tokens: bfloat16 [2048, 8, 768], P(('seq', 'fsdp'))
- d_table: float32 [5, 768], replicated
- d_gain_attn: float32 [768], P('fsdp')
- d_w_qkv: float32 [768, 2304], P('fsdp')
- d_w_out: float32 [768, 768], P('fsdp')
- d_gain_mlp: float32 [768], P('fsdp')
- d_w_up: float32 [768, 3072], P('fsdp')
- d_w_down: float32 [3072, 768], P('fsdp')
The draws below stay inside these ranges and needn't reach their ends.
Inputs may be any that keep to these rules, and one draw needn't show every extreme that they name: The longest sequence is exactly 2048 long; all lengths add up to 12288.
All inputs are finite; a program needn't handle non-finite values.
Results may differ from the reference program's by a relative error of at most 0.013.
Values may be sent and summed in bfloat16 or wider, within the bound.
No kernel may reach another device: no remote copies, remote signals or barrier semaphores. Data moves between devices by JAX's collectives and lax.ppermute only.
A program may use at most 192 MiB of HBM per device.

```python
import math
import jax
import jax.numpy as jnp
import numpy as np
from jax import lax

D = 768
HEADS = 12
FF = 3072
PASSES = 5
SLOT = 2048
HEAD_DIM = 64
NSEQ = 8


def place_ends(values, stream_key, low, largest):
    shape = values.shape
    index_at = [jax.random.randint(jax.random.fold_in(stream_key, axis), (), 0, shape[axis]) for axis in range(len(shape))]
    values = values.at[tuple(index_at)].set(low)
    longest = shape.index(max(shape))
    index_at[longest] = (index_at[longest] + 1) % shape[longest]
    return values.at[tuple(index_at)].set(largest)


def levels(own_key, shape, shards, least, high):
    def one(axis_at, parts):
        steps = jax.random.uniform(jax.random.fold_in(jax.random.fold_in(own_key, 6), axis_at), (parts,), jnp.float32, least / len(shards), high / len(shards))
        return jnp.repeat(jnp.exp(steps), shape[axis_at] // parts).reshape((-1,) + (1,) * (len(shape) - axis_at - 1))

    loudness = one(*shards[0])
    for cut in shards[1:]:
        loudness = loudness * one(*cut)
    return loudness


def length_profile(count, total, reach, skew):
    weights = [(1 << 20) // math.isqrt(rank ** skew) + 1 for rank in range(2, count + 1)]
    rest, counts = total - reach - (count - 1), [1] * (count - 1)
    while rest > 0:
        free = [i for i in range(count - 1) if counts[i] < reach]
        pool, left = sum([weights[i] for i in free]), rest
        for i in free:
            more = min(reach - counts[i], max(1, left * weights[i] // pool), rest)
            counts[i] = counts[i] + more
            rest = rest - more
    return np.array([reach] + counts)


def uneven(rng, amount, total, limit, skew):
    if amount == 2:
        one = jax.random.randint(rng, (), max(1, total - limit), min(limit, total - 1) + 1)
        return jnp.stack([one, total - one])
    tallies = jnp.asarray(length_profile(amount, total, limit, skew), jnp.int32)
    couples = (amount - 1) // 2
    source_of, taker = tallies[1:1 + 2 * couples:2], tallies[2:2 + 2 * couples:2]
    margin = jnp.minimum(source_of - 1, limit - taker)
    passed = jax.random.randint(jax.random.fold_in(rng, 1), (couples,), 0, 1 << 20) % (margin + 1)
    tallies = tallies.at[1:1 + 2 * couples:2].set(source_of - passed).at[2:2 + 2 * couples:2].set(taker + passed)
    return tallies[jax.random.permutation(jax.random.fold_in(rng, 2), amount)]


def normal_values(stream_key, shape, width, reach, shards=(), kind=jnp.bfloat16):
    drawn = width * jax.random.normal(stream_key, shape, jnp.float32)
    if shards:
        drawn = drawn * levels(stream_key, shape, shards, -0.22, 0.18)
    return jnp.clip(drawn, -reach, reach).astype(kind)


def setup_inputs(seed: int = 0) -> dict:
    key_of = jax.random.split(jax.random.key(seed), 12)
    return {
        "tokens": normal_values(key_of[0], (SLOT, NSEQ, D), 1.0, 6.0, ((0, 32),)),
        "pass_index": place_ends(jax.random.randint(key_of[1], (SLOT, NSEQ), 0, PASSES), jax.random.fold_in(key_of[1], 1), 0, PASSES - 1).astype(jnp.int32),
        "lengths": uneven(key_of[2], NSEQ, NSEQ * SLOT * 3 // 4, SLOT, 1).astype(jnp.int32),
        "table": normal_values(key_of[3], (PASSES, D), 0.5, 3.0),
        "gain_attn": jnp.clip(1.0 + 0.1 * jax.random.normal(key_of[4], (D,), jnp.float32), 0.5, 1.5).astype(jnp.bfloat16),
        "w_qkv": normal_values(key_of[5], (D, 3 * D), D ** -0.5, 0.21875, ((0, 8),)),
        "w_out": normal_values(key_of[6], (D, D), (D // 32) ** -0.5, 1.25, ((0, 8),)),
        "gain_mlp": jnp.clip(1.0 + 0.1 * jax.random.normal(key_of[7], (D,), jnp.float32), 0.5, 1.5).astype(jnp.bfloat16),
        "w_up": normal_values(key_of[8], (D, FF), D ** -0.5, 0.21875, ((0, 8),)),
        "w_down": normal_values(key_of[9], (FF, D), FF ** -0.5, 0.109375, ((0, 8),)),
        "cotangent": normal_values(key_of[10], (SLOT, NSEQ, D), 1.0, 6.0, ((0, 32),)),
    }


HIGHEST = lax.Precision.HIGHEST
EPSILON = 1e-05
MASKED = -1e+30

@jax.custom_vjp
def low(v):
    return lax.optimization_barrier(v.astype(jnp.bfloat16)).astype(jnp.float32)

@jax.custom_vjp
def low_back(v):
    return v

def low_keep(v):
    return (low(v), None)

def low_pass(kept, grad):
    return (grad,)

def back_keep(v):
    return (v, None)

def back_low(kept, grad):
    return (low(grad),)
low.defvjp(low_keep, low_pass)
low_back.defvjp(back_keep, back_low)

def norm_rows(values, gain_vec):
    centre = lax.optimization_barrier(jnp.mean(values, axis=-1, keepdims=True))
    shifted = values - centre
    spread = lax.optimization_barrier(jnp.mean(shifted * shifted, axis=-1, keepdims=True))
    return shifted * lax.rsqrt(spread + EPSILON) * gain_vec

def gelu_tanh(values):
    return jax.nn.gelu(values, approximate=True)

def one_sequence(seq_rows, length, gain_one, mat_qkv, mat_out, gain_two, mat_up, mat_down):
    normed = low(norm_rows(seq_rows, gain_one))
    projected = jnp.dot(normed, mat_qkv, precision=HIGHEST)
    queries = low_back(low(projected[:, :D])).reshape(SLOT, HEADS, HEAD_DIM)
    keys_all = low_back(low(projected[:, D:2 * D])).reshape(SLOT, HEADS, HEAD_DIM)
    values_all = low_back(low(projected[:, 2 * D:])).reshape(SLOT, HEADS, HEAD_DIM)
    scores = low_back(jnp.einsum('qhd,khd->hqk', queries, keys_all, precision=HIGHEST) * HEAD_DIM ** (-0.5))
    places = jnp.arange(SLOT, dtype=jnp.int32)
    allowed = (places[:, None] >= places[None, :]) & (places[None, :] < length)
    scores = jnp.where(allowed[None], scores, MASKED)
    weights = low(jax.nn.softmax(scores, axis=-1))
    mixed = jnp.einsum('hqk,khd->qhd', weights, values_all, precision=HIGHEST).reshape(SLOT, D)
    attended = low_back(low(mixed))
    residual = seq_rows + low_back(jnp.dot(attended, mat_out, precision=HIGHEST))
    normed_mlp = low(norm_rows(residual, gain_two))
    upper = low_back(jnp.dot(normed_mlp, mat_up, precision=HIGHEST))
    activation = low(gelu_tanh(upper))
    return residual + low_back(jnp.dot(activation, mat_down, precision=HIGHEST))

def reference(tokens, pass_index, lengths, table, gain_attn, w_qkv, w_out, gain_mlp, w_up, w_down, cotangent):
    token_f = jnp.transpose(tokens.astype(jnp.float32), (1, 0, 2))
    cot_f = jnp.transpose(cotangent.astype(jnp.float32), (1, 0, 2))
    chooser = (jnp.transpose(pass_index)[..., None] == jnp.arange(PASSES, dtype=jnp.int32)).astype(jnp.float32)
    primals = tuple((array_in.astype(jnp.float32) for array_in in (table, gain_attn, w_qkv, w_out, gain_mlp, w_up, w_down)))

    def forward(token_in, table_in, gain_one, mat_qkv, mat_out, gain_two, mat_up, mat_down):
        summed_in = low_back(low(token_in + jnp.einsum('nsc,cd->nsd', chooser, table_in, precision=HIGHEST)))
        checked = jax.checkpoint(one_sequence)

        def visit(carried, bundle):
            return (carried, checked(bundle[0], bundle[1], gain_one, mat_qkv, mat_out, gain_two, mat_up, mat_down))
        _, outcome = lax.scan(visit, jnp.float32(0.0), (summed_in, lengths))
        return outcome
    outcome, backward = jax.vjp(forward, token_f, *primals)
    grads = backward(cot_f)
    output = jnp.transpose(outcome, (1, 0, 2)).astype(jnp.bfloat16)
    d_tokens = jnp.transpose(grads[0], (1, 0, 2)).astype(jnp.bfloat16)
    return (output, d_tokens, grads[1], grads[2], grads[3], grads[4], grads[5], grads[6], grads[7])
```

```python
import functools

import jax
import jax.numpy as jnp
from jax import lax
from jax.experimental import pallas as pl
from jax.experimental.pallas import tpu as pltpu
from jax.sharding import PartitionSpec as P

HEADS = 12
EPSILON = 1e-05
LOG2E = 1.4426950408889634
LN2 = 0.6931471805599453
MASKED = -1e30
DH = 64


def dotg(a, b, ca, cb):
    return lax.dot_general(a, b, (((ca,), (cb,)), ((), ())), preferred_element_type=jnp.float32)


def attend_body(info, qkv, out, lse, acc, *, heads, blk):
    h = pl.program_id(0)
    i = pl.program_id(1)
    me = info[0]
    length = info[1]
    qt = qkv[i ^ me, pl.ds(pl.multiple_of(h * DH, DH), DH), :]
    scale = DH ** -0.5 * LOG2E

    def step(j, carry, masked):
        top, tot = carry
        kt = qkv[j ^ me, pl.ds(pl.multiple_of((heads + h) * DH, DH), DH), :]
        vt = qkv[j ^ me, pl.ds(pl.multiple_of((2 * heads + h) * DH, DH), DH), :]
        st = dotg(kt, qt, 0, 0) * scale
        if masked:
            key_at = j * blk + lax.broadcasted_iota(jnp.int32, st.shape, 0)
            query_at = i * blk + lax.broadcasted_iota(jnp.int32, st.shape, 1)
            st = jnp.where((query_at >= key_at) & (key_at < length), st, MASKED)
        new_top = jnp.maximum(top, jnp.max(st, axis=0, keepdims=True))
        fade = jnp.exp2(top - new_top)
        pt = jnp.exp2(st - new_top)
        tot = tot * fade + jnp.sum(pt, axis=0, keepdims=True)
        acc[...] = acc[...] * fade + dotg(vt, pt.astype(jnp.bfloat16), 1, 0)
        return new_top, tot

    acc[...] = jnp.zeros_like(acc)
    carry = (jnp.full((1, blk), MASKED, jnp.float32), jnp.zeros((1, blk), jnp.float32))
    plain = jnp.minimum(i, length // blk)
    stop = jnp.minimum(i + 1, (length + blk - 1) // blk)
    carry = lax.fori_loop(0, plain, functools.partial(step, masked=False), carry)
    top, tot = lax.fori_loop(plain, stop, functools.partial(step, masked=True), carry)
    out[0] = (acc[...] / tot).astype(jnp.bfloat16)
    lse[0, 0] = top + jnp.log2(tot)


def attend(info, qkv, heads):
    blocks, _, blk = qkv.shape
    flops = 2 * 2 * heads * DH * (blocks * blk) ** 2 // 2
    return pl.pallas_call(
        functools.partial(attend_body, heads=heads, blk=blk),
        grid_spec=pltpu.PrefetchScalarGridSpec(
            num_scalar_prefetch=1,
            grid=(heads, blocks),
            in_specs=[pl.BlockSpec(qkv.shape, lambda h, i, info: (0, 0, 0))],
            out_specs=[
                pl.BlockSpec((1, DH, blk), lambda h, i, info: (i, h, 0)),
                pl.BlockSpec((1, 1, 1, blk), lambda h, i, info: (h, i, 0, 0)),
            ],
            scratch_shapes=[pltpu.VMEM((DH, blk), jnp.float32)],
        ),
        out_shape=[
            jax.ShapeDtypeStruct((blocks, heads * DH, blk), jnp.bfloat16),
            jax.ShapeDtypeStruct((heads, blocks, 1, blk), jnp.float32),
        ],
        cost_estimate=pl.CostEstimate(flops=4 * flops, bytes_accessed=4 * qkv.size, transcendentals=0),
        name="attend",
    )(info, qkv)


def attend_back_body(info, qkv, att, datt, lse, dqkv, dq, q_rows, do_rows, delta, *, heads, blocks, blk):
    h = pl.program_id(0)
    j = pl.program_id(1)
    me = info[0]
    length = info[1]
    scale = DH ** -0.5
    at_q = pl.ds(pl.multiple_of(h * DH, DH), DH)
    at_k = pl.ds(pl.multiple_of((heads + h) * DH, DH), DH)
    at_v = pl.ds(pl.multiple_of((2 * heads + h) * DH, DH), DH)

    @pl.when(j == 0)
    def _():
        dq[...] = jnp.zeros_like(dq)
        for b in range(blocks):
            dt = datt[b, at_q, :]
            q_rows[b] = qkv[b ^ me, at_q, :].T
            do_rows[b] = dt.T
            delta[b] = jnp.sum(dt.astype(jnp.float32) * att[b, at_q, :].astype(jnp.float32), axis=0, keepdims=True)

    kt = qkv[j ^ me, at_k, :]
    vt = qkv[j ^ me, at_v, :]
    k_rows = kt.T
    v_rows = vt.T

    def step(i, carry, masked):
        dk, dv = carry
        qt = qkv[i ^ me, at_q, :]
        st = jnp.dot(k_rows, qt, preferred_element_type=jnp.float32)
        pt = jnp.exp2(st * (scale * LOG2E) - lse[0, i])
        if masked:
            key_at = j * blk + lax.broadcasted_iota(jnp.int32, st.shape, 0)
            query_at = i * blk + lax.broadcasted_iota(jnp.int32, st.shape, 1)
            pt = jnp.where((query_at >= key_at) & (key_at < length), pt, 0.0)
        dpt = jnp.dot(v_rows, datt[i, at_q, :], preferred_element_type=jnp.float32)
        dst = (pt * (dpt - delta[i])).astype(jnp.bfloat16)
        dv = dv + jnp.dot(pt.astype(jnp.bfloat16), do_rows[i], preferred_element_type=jnp.float32)
        dk = dk + jnp.dot(dst, q_rows[i], preferred_element_type=jnp.float32)
        dq[i] = dq[i] + jnp.dot(kt, dst, preferred_element_type=jnp.float32)
        return dk, dv

    zero = jnp.zeros((blk, DH), jnp.float32)
    whole = (j + 1) * blk <= length
    some = j * blk < length
    masked_end = jnp.where(some, jnp.where(whole, j + 1, blocks), j)
    carry = lax.fori_loop(j, masked_end, functools.partial(step, masked=True), (zero, zero))
    dk, dv = lax.fori_loop(
        jnp.where(whole, j + 1, blocks), blocks, functools.partial(step, masked=False), carry
    )
    dqkv[j ^ me, at_k, :] = (dk * scale).astype(jnp.bfloat16).T
    dqkv[j ^ me, at_v, :] = dv.astype(jnp.bfloat16).T
    dqkv[j ^ me, at_q, :] = (dq[j] * scale).astype(jnp.bfloat16)


def attend_back(info, qkv, att, datt, lse, heads):
    blocks, _, blk = qkv.shape
    flops = 5 * 2 * heads * DH * (blocks * blk) ** 2 // 2
    whole = lambda a: pl.BlockSpec(a.shape, lambda h, j, info: (0,) * a.ndim)
    return pl.pallas_call(
        functools.partial(attend_back_body, heads=heads, blocks=blocks, blk=blk),
        grid_spec=pltpu.PrefetchScalarGridSpec(
            num_scalar_prefetch=1,
            grid=(heads, blocks),
            in_specs=[
                whole(qkv),
                whole(att),
                whole(datt),
                pl.BlockSpec((1, blocks, 1, blk), lambda h, j, info: (h, 0, 0, 0)),
            ],
            out_specs=whole(qkv),
            scratch_shapes=[
                pltpu.VMEM((blocks, DH, blk), jnp.float32),
                pltpu.VMEM((blocks, blk, DH), jnp.bfloat16),
                pltpu.VMEM((blocks, blk, DH), jnp.bfloat16),
                pltpu.VMEM((blocks, 1, blk), jnp.float32),
            ],
        ),
        out_shape=jax.ShapeDtypeStruct(qkv.shape, jnp.bfloat16),
        cost_estimate=pl.CostEstimate(flops=4 * flops, bytes_accessed=8 * qkv.size, transcendentals=0),
        name="attend_back",
    )(info, qkv, att, datt, lse)


GELU_A = 0.7978845608028654
GELU_B = 0.044715


def mlp_body(nm, cot, wu, wd, acc_in, dnm_in, acc, dnm, dwu, dwd):
    @pl.when(pl.program_id(0) == 0)
    def _():
        acc[...] = acc_in[...]
        dnm[...] = dnm_in[...]

    x = nm[...]
    g = cot[...]
    u = jnp.dot(x, wu[...], preferred_element_type=jnp.float32)
    da = dotg(g, wd[...], 1, 1)
    square = u * u
    th = jnp.tanh(GELU_A * u * (1.0 + GELU_B * square))
    half = 0.5 * (1.0 + th)
    a = (u * half).astype(jnp.bfloat16)
    slope = half + 0.5 * u * (1.0 - th * th) * (GELU_A * (1.0 + 3.0 * GELU_B * square))
    du = (da * slope).astype(jnp.bfloat16)
    acc[...] += jnp.dot(a, wd[...], preferred_element_type=jnp.float32)
    dnm[...] += dotg(du, wu[...], 1, 1)
    dwd[...] = dotg(a, g, 0, 0).astype(jnp.bfloat16)
    dwu[...] = dotg(x, du, 0, 0).astype(jnp.bfloat16)


def mlp_part(nm, cot, wu, wd, acc, dnm, step=256):
    rows, width = nm.shape
    ff = wu.shape[1]
    whole = pl.BlockSpec((rows, width), lambda i: (0, 0))
    up = pl.BlockSpec((width, step), lambda i: (0, i))
    down = pl.BlockSpec((step, width), lambda i: (i, 0))
    return pl.pallas_call(
        mlp_body,
        grid=(ff // step,),
        in_specs=[whole, whole, up, down, whole, whole],
        out_specs=[whole, whole, up, down],
        out_shape=[
            jax.ShapeDtypeStruct((rows, width), jnp.float32),
            jax.ShapeDtypeStruct((rows, width), jnp.float32),
            jax.ShapeDtypeStruct(wu.shape, jnp.bfloat16),
            jax.ShapeDtypeStruct(wd.shape, jnp.bfloat16),
        ],
        input_output_aliases={4: 0, 5: 1},
        cost_estimate=pl.CostEstimate(flops=12 * rows * width * ff, bytes_accessed=8 * width * ff, transcendentals=0),
        name="mlp_part",
    )(nm, cot, wu, wd, acc, dnm)


def swap(value, axis, bit):
    count = lax.axis_size(axis)
    return lax.ppermute(value, axis, [(i, i ^ bit) for i in range(count)])


def bits_of(axis):
    count = lax.axis_size(axis)
    assert count & (count - 1) == 0, "axis size"
    return [1 << b for b in reversed(range(count.bit_length() - 1))]


def is_set(axis, bit):
    return (lax.axis_index(axis) & bit) != 0


def join(own, came, axis, bit, at):
    high = is_set(axis, bit)
    return jnp.stack((jnp.where(high, came, own), jnp.where(high, own, came)), axis=at)


def gather(value, axis, bits, at=0):
    for k, bit in enumerate(bits):
        value = join(value, swap(value, axis, bit), axis, bit, at + k)
    return value


def spread(blocks, bit):
    return blocks | {r ^ bit: swap(b, "seq", bit) for r, b in blocks.items()}


def add(a, b):
    return (a.astype(jnp.float32) + b.astype(jnp.float32)).astype(a.dtype)


def fold(blocks, bit):
    return {r: add(b, swap(blocks[r ^ bit], "seq", bit)) for r, b in blocks.items() if not r & bit}


def halve(value, axis, bit, at):
    mine = is_set(axis, bit).astype(jnp.int32)
    keep = lax.dynamic_index_in_dim(value, mine, at, keepdims=False)
    give = lax.dynamic_index_in_dim(value, 1 - mine, at, keepdims=False)
    return add(keep, swap(give, axis, bit))


def norm_stats(values):
    centre = jnp.mean(values, axis=-1, keepdims=True)
    shifted = values - centre
    spread_of = jnp.mean(shifted * shifted, axis=-1, keepdims=True)
    inverse = lax.rsqrt(spread_of + EPSILON)
    return shifted * inverse, inverse


def norm_back(z, inverse, gain, grad):
    e = grad * gain
    back = (e - jnp.mean(e, axis=-1, keepdims=True) - z * jnp.mean(e * z, axis=-1, keepdims=True)) * inverse
    return back, jnp.sum(grad * z, axis=0, keepdims=True)


def per_device(
    tokens, pass_index, lengths, table, gain_attn, w_qkv, w_out, gain_mlp, w_up, w_down, cotangent
):
    bf16, f32 = jnp.bfloat16, jnp.float32
    groups, parts = lax.axis_size("fsdp"), lax.axis_size("seq")
    local_len, seq_total, width = tokens.shape
    assert seq_total == groups
    heads = HEADS // parts
    part = width // parts
    ff = w_up.shape[1]
    own_rows = width // groups
    me, group = lax.axis_index("seq"), lax.axis_index("fsdp")
    f_bits, s_bits = bits_of("fsdp"), bits_of("seq")
    span = local_len * groups
    pick = lambda a, at: lax.dynamic_index_in_dim(a, me, at, keepdims=False)

    qkv_slice = pick(w_qkv.reshape(own_rows, 3, parts, part), 2).reshape(own_rows, 3 * part)
    gains = jnp.stack((gain_attn, gain_mlp), axis=1)
    qkv_slice = jnp.concatenate(
        (qkv_slice, gains, jnp.zeros((own_rows, -(3 * part + 2) % 128), bf16)), axis=1
    )
    ff_each = ff // groups // parts
    up_slice = pick(w_up.reshape(own_rows, groups, parts, ff_each), 2).reshape(own_rows, ff // parts)
    down_slice = pick(w_down.reshape(parts, ff_each, width), 0)
    out_slice = pick(w_out.reshape(parts, own_rows // parts, width), 0)

    chooser = (pass_index[..., None] == jnp.arange(table.shape[0], dtype=jnp.int32)).astype(bf16)
    embedded = jnp.einsum("pnc,cd->npd", chooser, table, preferred_element_type=f32)
    summed = (jnp.swapaxes(tokens, 0, 1).astype(f32) + embedded).astype(bf16)
    deal = lambda a: lax.all_to_all(a, "fsdp", split_axis=0, concat_axis=0, tiled=True)
    inputs = deal(summed).reshape(span, width)
    qkv_full = gather(qkv_slice, "fsdp", f_bits).reshape(width, -1)
    wq = qkv_full[:, : 3 * part]
    gain_one = qkv_full[:, 3 * part].astype(f32)
    gain_two = qkv_full[:, 3 * part + 1].astype(f32)
    cot = deal(jnp.swapaxes(cotangent, 0, 1)).reshape(span, width)
    passes = lax.dynamic_index_in_dim(gather(pass_index, "fsdp", f_bits), group, -1, keepdims=False).reshape(span)

    up_all = {0: gather(up_slice, "fsdp", f_bits).reshape(width, ff // parts)}
    for bit in s_bits:
        up_all = spread(up_all, bit)
    down_all = {0: gather(down_slice, "fsdp", f_bits[:-1])}
    for bit in s_bits[:-1]:
        down_all = spread(down_all, bit)
    down_all = {
        r: join(b, swap(b, "fsdp", f_bits[-1]), "fsdp", f_bits[-1], len(f_bits) - 1).reshape(ff // parts, width)
        for r, b in down_all.items()
    }
    down_all = spread(down_all, s_bits[-1])
    w_out_full = gather(gather(out_slice, "fsdp", f_bits), "seq", s_bits, len(f_bits)).reshape(width, width)

    rows = {0: inputs}
    for bit in s_bits:
        rows = spread(rows, bit)
    normed, inverse_one, z_one = {}, None, None
    pieces = []
    for r in range(parts):
        z, inverse = norm_stats(rows[r].astype(f32))
        normed[r] = (z * gain_one).astype(bf16)
        pieces.append(dotg(wq, normed[r], 0, 1).astype(bf16))
    qkv = jnp.stack(pieces)
    info = jnp.stack((me, lax.dynamic_index_in_dim(lengths, group, 0, keepdims=False))).astype(jnp.int32)
    att_heads, lse = attend(info, qkv, heads)
    across = lambda a: lax.all_to_all(a, "seq", split_axis=0, concat_axis=0, tiled=True)
    att = across(att_heads).reshape(width, span)

    residual = inputs.astype(f32) + dotg(att, w_out_full, 0, 0)
    z_two, inverse_two = norm_stats(residual)
    normed_mlp = (z_two * gain_two).astype(bf16)
    result = residual
    d_normed_mlp = jnp.zeros_like(residual)
    d_up, d_down = {}, {}
    for r in reversed(range(parts)):
        result, d_normed_mlp, d_up[r], d_down[r] = mlp_part(
            normed_mlp, cot, up_all[r], down_all[r], result, d_normed_mlp
        )
    out_back = deal(result.astype(bf16).reshape(groups, local_len, width))
    d_res_norm, d_gain_mlp = norm_back(z_two, inverse_two, gain_two, d_normed_mlp)
    d_residual = cot.astype(f32) + d_res_norm
    d_branch = d_residual.astype(bf16)
    d_att = dotg(w_out_full, d_branch, 1, 1).astype(bf16)
    d_heads = across(d_att.reshape(parts, part, span))

    sizes = (2,) * len(f_bits)
    for bit in reversed(s_bits):
        d_up = fold(d_up, bit)
    d_up = d_up[0].reshape(*sizes, own_rows, ff // parts)
    for k in reversed(range(len(f_bits))):
        d_up = halve(d_up, "fsdp", f_bits[k], k)
    d_down = {r: b.reshape(*sizes, ff_each, width) for r, b in fold(d_down, s_bits[-1]).items()}
    last = len(f_bits) - 1
    d_down = {r: halve(b, "fsdp", f_bits[last], last) for r, b in d_down.items()}
    for bit in reversed(s_bits[:-1]):
        d_down = fold(d_down, bit)
    d_down = d_down[0]
    for k in reversed(range(last)):
        d_down = halve(d_down, "fsdp", f_bits[k], k)
    d_out = dotg(att, d_branch, 0 + 1, 0).astype(bf16)
    d_out = d_out.reshape(*sizes, *(2,) * len(s_bits), own_rows // parts, width)
    for k in reversed(range(len(s_bits))):
        d_out = halve(d_out, "seq", s_bits[k], len(f_bits) + k)
    for k in reversed(range(len(f_bits))):
        d_out = halve(d_out, "fsdp", f_bits[k], k)

    d_qkv = attend_back(info, qkv, att_heads, d_heads, lse, heads)
    d_rows = {r: dotg(d_qkv[r], wq, 0, 1).astype(bf16) for r in range(parts)}
    for bit in reversed(s_bits[1:]):
        d_rows = fold(d_rows, bit)
    d_normed = d_rows[0].astype(f32) + swap(d_rows[s_bits[0]], "seq", s_bits[0]).astype(f32)
    z_one, inverse_one = norm_stats(inputs.astype(f32))
    d_in_norm, d_gain_attn = norm_back(z_one, inverse_one, gain_one, d_normed)
    d_inputs = (d_residual + d_in_norm).astype(bf16)
    d_back = deal(d_inputs.reshape(groups, local_len, width))
    d_wq = sum(dotg(normed[r], d_qkv[r], 0, 1) for r in range(parts)).astype(bf16)
    d_wq = d_wq.reshape(*sizes, own_rows, 3 * part)
    for k in reversed(range(len(f_bits))):
        d_wq = halve(d_wq, "fsdp", f_bits[k], k)

    picks = (passes[None, :] == jnp.arange(table.shape[0], dtype=jnp.int32)[:, None]).astype(bf16)
    d_table = jnp.dot(picks, d_inputs, preferred_element_type=f32)
    small = jnp.concatenate((d_table, d_gain_attn, d_gain_mlp, jnp.zeros_like(d_gain_mlp)), axis=0)
    for bit in reversed(s_bits):
        small = small + swap(small, "seq", bit)
    for bit in reversed(f_bits):
        small = small + swap(small, "fsdp", bit)
    owned_gain = lambda row: lax.dynamic_slice_in_dim(small[row], group * own_rows, own_rows)

    whole = lambda a: gather(a, "seq", s_bits).reshape(parts, *a.shape).astype(f32)
    g_qkv = whole(d_wq).reshape(parts, own_rows, 3, part).transpose(1, 2, 0, 3).reshape(own_rows, 3 * width)
    g_up = whole(d_up).reshape(parts, own_rows, groups, ff_each).transpose(1, 2, 0, 3).reshape(own_rows, ff)
    g_down = whole(d_down).reshape(ff // groups, width)
    g_out = whole(d_out).reshape(own_rows, width)
    count = table.shape[0]
    return (
        jnp.swapaxes(out_back, 0, 1),
        jnp.swapaxes(d_back, 0, 1),
        small[:count],
        owned_gain(count),
        g_qkv,
        g_out,
        owned_gain(count + 1),
        g_up,
        g_down,
    )


def solution(mesh):
    return jax.shard_map(
        per_device,
        mesh=mesh,
        in_specs=(
            P(("seq", "fsdp"), None, None),
            P(("seq", "fsdp"), None),
            P(),
            P(),
            P("fsdp"),
            P("fsdp", None),
            P("fsdp", None),
            P("fsdp"),
            P("fsdp", None),
            P("fsdp", None),
            P(("seq", "fsdp"), None, None),
        ),
        out_specs=(
            P(("seq", "fsdp"), None, None),
            P(("seq", "fsdp"), None, None),
            P(),
            P("fsdp"),
            P("fsdp", None),
            P("fsdp", None),
            P("fsdp"),
            P("fsdp", None),
            P("fsdp", None),
        ),
        check_vma=False,
    )
```

```python
import functools

import jax
import jax.numpy as jnp
from jax import lax
from jax.experimental import pallas as pl
from jax.experimental.pallas import tpu as pltpu
from jax.sharding import PartitionSpec as P

HEADS = 12
EPSILON = 1e-05
LOG2E = 1.4426950408889634
LN2 = 0.6931471805599453
MASKED = -1e30
DH = 64


def dotg(a, b, ca, cb):
    return lax.dot_general(a, b, (((ca,), (cb,)), ((), ())), preferred_element_type=jnp.float32)


def attend_body(info, qkv, *refs, blk):
    out, lse, acc = refs[-3:]
    i = pl.program_id(0)
    me = info[0]
    length = info[1]
    qt = qkv[i ^ me, 0:DH, :]
    scale = DH ** -0.5 * LOG2E

    def step(j, carry, masked):
        top, tot = carry
        kt = qkv[j ^ me, DH : 2 * DH, :]
        vt = qkv[j ^ me, 2 * DH : 3 * DH, :]
        st = dotg(kt, qt, 0, 0) * scale
        if masked:
            key_at = j * blk + lax.broadcasted_iota(jnp.int32, st.shape, 0)
            query_at = i * blk + lax.broadcasted_iota(jnp.int32, st.shape, 1)
            st = jnp.where((query_at >= key_at) & (key_at < length), st, MASKED)
        new_top = jnp.maximum(top, jnp.max(st, axis=0, keepdims=True))
        fade = jnp.exp2(top - new_top)
        pt = jnp.exp2(st - new_top)
        tot = tot * fade + jnp.sum(pt, axis=0, keepdims=True)
        acc[...] = acc[...] * fade + dotg(vt, pt.astype(jnp.bfloat16), 1, 0)
        return new_top, tot

    acc[...] = jnp.zeros_like(acc)
    carry = (jnp.full((1, blk), MASKED, jnp.float32), jnp.zeros((1, blk), jnp.float32))
    plain = jnp.minimum(i, length // blk)
    stop = jnp.minimum(i + 1, (length + blk - 1) // blk)
    carry = lax.fori_loop(0, plain, functools.partial(step, masked=False), carry)
    top, tot = lax.fori_loop(plain, stop, functools.partial(step, masked=True), carry)
    out[0] = (acc[...] / tot).astype(jnp.bfloat16)
    lse[0] = top + jnp.log2(tot)


def attend(info, qkv, heads, h, before=None):
    blocks, _, blk = qkv.shape
    flops = 2 * 2 * DH * (blocks * blk) ** 2 // 2
    given = () if before is None else (before,)
    return pl.pallas_call(
        functools.partial(attend_body, blk=blk),
        grid_spec=pltpu.PrefetchScalarGridSpec(
            num_scalar_prefetch=1,
            grid=(blocks,),
            in_specs=[pl.BlockSpec((blocks, 3 * DH, blk), lambda i, info: (0, h, 0))]
            + [pl.BlockSpec(memory_space=pl.ANY)] * len(given),
            out_specs=[
                pl.BlockSpec((1, DH, blk), lambda i, info: (i, h, 0)),
                pl.BlockSpec((1, 1, blk), lambda i, info: (i, 0, 0)),
            ],
            scratch_shapes=[pltpu.VMEM((DH, blk), jnp.float32)],
        ),
        out_shape=[
            jax.ShapeDtypeStruct((blocks, heads * DH, blk), jnp.bfloat16),
            jax.ShapeDtypeStruct((blocks, 1, blk), jnp.float32),
        ],
        input_output_aliases={2: 0} if given else {},
        cost_estimate=pl.CostEstimate(flops=4 * flops, bytes_accessed=4 * qkv.size // heads, transcendentals=0),
        name="attend",
    )(info, qkv, *given)


def attend_back_body(info, qkv, att, datt, lse, *refs, blocks, blk):
    dqkv, dq, q_rows, do_rows, delta = refs[-5:]
    j = pl.program_id(0)
    me = info[0]
    length = info[1]
    scale = DH ** -0.5
    at_q, at_k, at_v = slice(0, DH), slice(DH, 2 * DH), slice(2 * DH, 3 * DH)

    @pl.when(j == 0)
    def _():
        dq[...] = jnp.zeros_like(dq)
        for b in range(blocks):
            dt = datt[b]
            q_rows[b] = qkv[b ^ me, at_q, :].T
            do_rows[b] = dt.T
            delta[b] = jnp.sum(dt.astype(jnp.float32) * att[b].astype(jnp.float32), axis=0, keepdims=True)

    kt = qkv[j ^ me, at_k, :]
    vt = qkv[j ^ me, at_v, :]
    k_rows = kt.T
    v_rows = vt.T

    def step(i, carry, masked):
        dk, dv = carry
        qt = qkv[i ^ me, at_q, :]
        st = jnp.dot(k_rows, qt, preferred_element_type=jnp.float32)
        pt = jnp.exp2(st * (scale * LOG2E) - lse[i])
        if masked:
            key_at = j * blk + lax.broadcasted_iota(jnp.int32, st.shape, 0)
            query_at = i * blk + lax.broadcasted_iota(jnp.int32, st.shape, 1)
            pt = jnp.where((query_at >= key_at) & (key_at < length), pt, 0.0)
        dpt = jnp.dot(v_rows, datt[i], preferred_element_type=jnp.float32)
        dst = (pt * (dpt - delta[i])).astype(jnp.bfloat16)
        dv = dv + jnp.dot(pt.astype(jnp.bfloat16), do_rows[i], preferred_element_type=jnp.float32)
        dk = dk + jnp.dot(dst, q_rows[i], preferred_element_type=jnp.float32)
        dq[i] = dq[i] + jnp.dot(kt, dst, preferred_element_type=jnp.float32)
        return dk, dv

    zero = jnp.zeros((blk, DH), jnp.float32)
    whole = (j + 1) * blk <= length
    some = j * blk < length
    masked_end = jnp.where(some, jnp.where(whole, j + 1, blocks), j)
    carry = lax.fori_loop(j, masked_end, functools.partial(step, masked=True), (zero, zero))
    dk, dv = lax.fori_loop(
        jnp.where(whole, j + 1, blocks), blocks, functools.partial(step, masked=False), carry
    )
    dqkv[j ^ me, at_k, :] = (dk * scale).astype(jnp.bfloat16).T
    dqkv[j ^ me, at_v, :] = dv.astype(jnp.bfloat16).T
    dqkv[j ^ me, at_q, :] = (dq[j] * scale).astype(jnp.bfloat16)


def attend_back(info, qkv, att, datt, lse, heads, h, before=None):
    blocks, _, blk = qkv.shape
    flops = 5 * 2 * DH * (blocks * blk) ** 2 // 2
    given = () if before is None else (before,)
    third = pl.BlockSpec((blocks, 3 * DH, blk), lambda j, info: (0, h, 0))
    head = pl.BlockSpec((blocks, DH, blk), lambda j, info: (0, h, 0))
    return pl.pallas_call(
        functools.partial(attend_back_body, blocks=blocks, blk=blk),
        grid_spec=pltpu.PrefetchScalarGridSpec(
            num_scalar_prefetch=1,
            grid=(blocks,),
            in_specs=[third, head, head, pl.BlockSpec((blocks, 1, blk), lambda j, info: (0, 0, 0))]
            + [pl.BlockSpec(memory_space=pl.ANY)] * len(given),
            out_specs=third,
            scratch_shapes=[
                pltpu.VMEM((blocks, DH, blk), jnp.float32),
                pltpu.VMEM((blocks, blk, DH), jnp.bfloat16),
                pltpu.VMEM((blocks, blk, DH), jnp.bfloat16),
                pltpu.VMEM((blocks, 1, blk), jnp.float32),
            ],
        ),
        out_shape=jax.ShapeDtypeStruct(qkv.shape, jnp.bfloat16),
        input_output_aliases={5: 0} if given else {},
        cost_estimate=pl.CostEstimate(flops=4 * flops, bytes_accessed=8 * qkv.size // heads, transcendentals=0),
        name="attend_back",
    )(info, qkv, att, datt, lse, *given)


GELU_A = 0.7978845608028654
GELU_B = 0.044715


def mlp_body(nm, cot, wu, wd, acc_in, dnm_in, acc, dnm, dwu, dwd):
    @pl.when(pl.program_id(0) == 0)
    def _():
        acc[...] = acc_in[...]
        dnm[...] = dnm_in[...]

    x = nm[...]
    g = cot[...]
    u = jnp.dot(x, wu[...], preferred_element_type=jnp.float32)
    da = dotg(g, wd[...], 1, 1)
    square = u * u
    th = jnp.tanh(GELU_A * u * (1.0 + GELU_B * square))
    half = 0.5 * (1.0 + th)
    a = (u * half).astype(jnp.bfloat16)
    slope = half + 0.5 * u * (1.0 - th * th) * (GELU_A * (1.0 + 3.0 * GELU_B * square))
    du = (da * slope).astype(jnp.bfloat16)
    acc[...] += jnp.dot(a, wd[...], preferred_element_type=jnp.float32)
    dnm[...] += dotg(du, wu[...], 1, 1)
    dwd[...] = dotg(a, g, 0, 0).astype(jnp.bfloat16)
    dwu[...] = dotg(x, du, 0, 0).astype(jnp.bfloat16)


def mlp_part(nm, cot, wu, wd, acc, dnm, step=256):
    rows, width = nm.shape
    ff = wu.shape[1]
    whole = pl.BlockSpec((rows, width), lambda i: (0, 0))
    up = pl.BlockSpec((width, step), lambda i: (0, i))
    down = pl.BlockSpec((step, width), lambda i: (i, 0))
    return pl.pallas_call(
        mlp_body,
        grid=(ff // step,),
        in_specs=[whole, whole, up, down, whole, whole],
        out_specs=[whole, whole, up, down],
        out_shape=[
            jax.ShapeDtypeStruct((rows, width), jnp.float32),
            jax.ShapeDtypeStruct((rows, width), jnp.float32),
            jax.ShapeDtypeStruct(wu.shape, jnp.bfloat16),
            jax.ShapeDtypeStruct(wd.shape, jnp.bfloat16),
        ],
        input_output_aliases={4: 0, 5: 1},
        cost_estimate=pl.CostEstimate(flops=12 * rows * width * ff, bytes_accessed=8 * width * ff, transcendentals=0),
        name="mlp_part",
    )(nm, cot, wu, wd, acc, dnm)


def swap(value, axis, bit):
    count = lax.axis_size(axis)
    return lax.ppermute(value, axis, [(i, i ^ bit) for i in range(count)])


def bits_of(axis):
    count = lax.axis_size(axis)
    assert count & (count - 1) == 0, "axis size"
    return [1 << b for b in reversed(range(count.bit_length() - 1))]


def is_set(axis, bit):
    return (lax.axis_index(axis) & bit) != 0


def join(own, came, axis, bit, at):
    high = is_set(axis, bit)
    return jnp.stack((jnp.where(high, came, own), jnp.where(high, own, came)), axis=at)


def gather(value, axis, bits, at=0):
    for k, bit in enumerate(bits):
        value = join(value, swap(value, axis, bit), axis, bit, at + k)
    return value


def spread(blocks, bit):
    return blocks | {r ^ bit: swap(b, "seq", bit) for r, b in blocks.items()}


def add(a, b):
    return (a.astype(jnp.float32) + b.astype(jnp.float32)).astype(a.dtype)


def fold(blocks, bit):
    return {r: add(b, swap(blocks[r ^ bit], "seq", bit)) for r, b in blocks.items() if not r & bit}


def halve(value, axis, bit, at):
    mine = is_set(axis, bit).astype(jnp.int32)
    keep = lax.dynamic_index_in_dim(value, mine, at, keepdims=False)
    give = lax.dynamic_index_in_dim(value, 1 - mine, at, keepdims=False)
    return add(keep, swap(give, axis, bit))


def norm_stats(values):
    centre = jnp.mean(values, axis=-1, keepdims=True)
    shifted = values - centre
    spread_of = jnp.mean(shifted * shifted, axis=-1, keepdims=True)
    inverse = lax.rsqrt(spread_of + EPSILON)
    return shifted * inverse, inverse


def norm_back(z, inverse, gain, grad):
    e = grad * gain
    back = (e - jnp.mean(e, axis=-1, keepdims=True) - z * jnp.mean(e * z, axis=-1, keepdims=True)) * inverse
    return back, jnp.sum(grad * z, axis=0, keepdims=True)


def pick_at(value, at):
    return lax.dynamic_index_in_dim(value, at, 1, keepdims=False)


def tie(*values):
    return lax.optimization_barrier(values)


def per_device(
    tokens, pass_index, lengths, table, gain_attn, w_qkv, w_out, gain_mlp, w_up, w_down, cotangent
):
    bf16, f32 = jnp.bfloat16, jnp.float32
    groups, parts = lax.axis_size("fsdp"), lax.axis_size("seq")
    local_len, seq_total, width = tokens.shape
    assert seq_total == groups and parts == 4
    heads = HEADS // parts
    part = width // parts
    ff = w_up.shape[1]
    own_rows = width // groups
    ff_each = ff // groups // parts
    me, group = lax.axis_index("seq"), lax.axis_index("fsdp")
    f_bits = bits_of("fsdp")
    last = len(f_bits) - 1
    sizes = (2,) * len(f_bits)
    span = local_len * groups
    pick = lambda a, at: lax.dynamic_index_in_dim(a, me, at, keepdims=False)
    deal = lambda a: lax.all_to_all(a, "fsdp", split_axis=0, concat_axis=0, tiled=True)
    across = lambda a: lax.all_to_all(a, "seq", split_axis=0, concat_axis=0, tiled=True)

    chooser = (pass_index[..., None] == jnp.arange(table.shape[0], dtype=jnp.int32)).astype(bf16)
    embedded = jnp.einsum("pnc,cd->npd", chooser, table, preferred_element_type=f32)
    summed = (jnp.swapaxes(tokens, 0, 1).astype(f32) + embedded).astype(bf16)
    inputs = deal(summed).reshape(span, width)
    qkv_slice = pick(w_qkv.reshape(own_rows, 3, parts, heads, DH), 2)
    qkv_slice = jnp.swapaxes(qkv_slice, 1, 2).reshape(own_rows, 3 * part)
    out_slice = pick(w_out.reshape(own_rows, parts, part), 1)
    gains = jnp.stack((gain_attn, gain_mlp), axis=1)
    packet = jnp.concatenate((qkv_slice, out_slice, gains, jnp.zeros((own_rows, 126), bf16)), axis=1)
    packet = gather(packet, "fsdp", f_bits).reshape(width, -1)
    wq = packet[:, : 3 * part]
    out_cols = packet[:, 3 * part : width]
    gain_one = packet[:, width].astype(f32)
    gain_two = packet[:, width + 1].astype(f32)

    up_slice = pick(w_up.reshape(own_rows, groups, parts, ff_each), 2).reshape(own_rows, ff // parts)
    down_slice = pick(w_down.reshape(parts, ff_each, width), 0)
    inputs, up_slice, down_slice = tie(inputs, up_slice, down_slice)
    up = gather(up_slice, "fsdp", f_bits[:-1])
    down = gather(down_slice, "fsdp", f_bits[:-1])

    rows = {0: inputs, 2: swap(inputs, "seq", 2), 1: swap(inputs, "seq", 1)}
    rows[3] = swap(rows[2], "seq", 1)
    normed, pieces = {}, []
    for r in range(parts):
        z, _ = norm_stats(rows[r].astype(f32))
        normed[r] = (z * gain_one).astype(bf16)
        pieces.append(dotg(wq, normed[r], 0, 1).astype(bf16))
    qkv = jnp.stack(pieces)
    info = jnp.stack((me, lax.dynamic_index_in_dim(lengths, group, 0, keepdims=False))).astype(jnp.int32)

    marks = jnp.swapaxes(pass_index, 0, 1)[..., None].astype(bf16)
    cot_packet = jnp.concatenate(
        (jnp.swapaxes(cotangent, 0, 1), jnp.broadcast_to(marks, marks.shape[:2] + (128,))), axis=2
    )
    qkv, up, down, cot_packet = tie(qkv, up, down, cot_packet)
    cot_packet = deal(cot_packet).reshape(span, -1)
    up_next = swap(up, "fsdp", f_bits[-1])
    down_next = swap(down, "seq", 2)
    out_two = swap(out_cols, "seq", 2)
    lse = [None] * heads
    att_heads, lse[0] = attend(info, qkv, heads, 0)
    att_heads, lse[1] = attend(info, qkv, heads, 1, att_heads)
    up = join(up, up_next, "fsdp", f_bits[-1], last).reshape(width, ff // parts)
    qkv, up, down, down_next, out_cols, out_two = tie(qkv, up, down, down_next, out_cols, out_two)
    up_all = {0: up, 2: swap(up, "seq", 2)}
    down_all = {
        r: join(b, swap(b, "fsdp", f_bits[-1]), "fsdp", f_bits[-1], last).reshape(ff // parts, width)
        for r, b in {0: down, 2: down_next}.items()
    }
    for h in range(2, heads):
        att_heads, lse[h] = attend(info, qkv, heads, h, att_heads)
    out_all = spread({0: out_cols, 2: out_two}, 1)
    up_all = spread(up_all, 1)
    down_all = spread(down_all, 1)
    w_out_full = jnp.stack([out_all[r] for r in range(parts)])
    w_out_full = jnp.concatenate(
        [lax.dynamic_index_in_dim(w_out_full, r ^ me, 0, keepdims=False) for r in range(parts)], axis=1
    )
    att = across(att_heads).reshape(width, span)

    cot = cot_packet[:, :width]
    passes = cot_packet[:, width]
    residual = inputs.astype(f32) + dotg(att, w_out_full, 0, 0)
    z_two, inverse_two = norm_stats(residual)
    normed_mlp = (z_two * gain_two).astype(bf16)
    result = residual
    d_normed_mlp = jnp.zeros_like(residual)
    d_up, d_down = {}, {}
    for r in (3, 2, 1, 0):
        result, d_normed_mlp, d_up[r], d_down[r] = mlp_part(
            normed_mlp, cot, up_all[r], down_all[r], result, d_normed_mlp
        )
        if r == 2:
            up_2 = add(d_up[2], swap(d_up[3], "seq", 1))
            down_2 = add(d_down[2], swap(d_down[3], "seq", 1))
            d_normed_mlp, up_2, down_2 = tie(d_normed_mlp, up_2, down_2)
    up_0 = add(d_up[0], swap(d_up[1], "seq", 1))
    down_0 = add(d_down[0], swap(d_down[1], "seq", 1))
    d_normed_mlp, up_0, down_0 = tie(d_normed_mlp, up_0, down_0)
    d_res_norm, d_gain_mlp = norm_back(z_two, inverse_two, gain_two, d_normed_mlp)
    d_residual = cot.astype(f32) + d_res_norm
    d_branch = d_residual.astype(bf16)
    d_att = dotg(w_out_full, d_branch, 1, 1).astype(bf16)
    d_heads = across(d_att.reshape(parts, part, span))

    up_0 = add(up_0, swap(up_2, "seq", 2)).reshape(*sizes, own_rows, ff // parts)
    down_0, down_2 = (
        halve(b.reshape(*sizes, ff_each, width), "fsdp", f_bits[-1], last) for b in (down_0, down_2)
    )
    d_cols = d_branch.reshape(span, parts, part)
    d_out = {r: dotg(att, pick_at(d_cols, me ^ r), 1, 0).astype(bf16) for r in range(parts)}
    d_out = fold(d_out, 1)
    back = result.astype(bf16).reshape(groups, local_len, width)
    d_heads, up_0, down_0, down_2, back, d_out = tie(d_heads, up_0, down_0, down_2, back, d_out)
    out_back = deal(back)
    up_0 = halve(up_0, "fsdp", f_bits[-1], last)
    down_0 = add(down_0, swap(down_2, "seq", 2))
    d_out = fold(d_out, 2)[0]
    d_qkv = attend_back(info, qkv, att_heads, d_heads, lse[0], heads, 0)
    d_qkv = attend_back(info, qkv, att_heads, d_heads, lse[1], heads, 1, d_qkv)
    d_qkv, up_0, down_0, d_out = tie(d_qkv, up_0, down_0, d_out)
    grads = jnp.stack((up_0, down_0), axis=last)
    grads = halve(grads, "fsdp", f_bits[-2], last - 1)
    for h in range(2, heads):
        d_qkv = attend_back(info, qkv, att_heads, d_heads, lse[h], heads, h, d_qkv)
    d_qkv, grads = tie(d_qkv, grads)
    for k in reversed(range(last - 1)):
        grads = halve(grads, "fsdp", f_bits[k], k)

    d_rows = {r: dotg(d_qkv[r], wq, 0, 1).astype(bf16) for r in range(parts)}
    d_rows = fold(d_rows, 1)
    d_wq = sum(dotg(normed[r], d_qkv[r], 0, 1) for r in range(parts)).astype(bf16)
    d_wq = jnp.concatenate((d_wq, d_out), axis=1).reshape(*sizes, own_rows, width)
    for k in reversed(range(len(f_bits))):
        d_wq = halve(d_wq, "fsdp", f_bits[k], k)
    d_normed = d_rows[0].astype(f32) + swap(d_rows[2], "seq", 2).astype(f32)
    z_one, inverse_one = norm_stats(inputs.astype(f32))
    d_in_norm, d_gain_attn = norm_back(z_one, inverse_one, gain_one, d_normed)
    d_inputs = (d_residual + d_in_norm).astype(bf16)
    d_back = deal(d_inputs.reshape(groups, local_len, width))

    count = table.shape[0]
    picks = (passes[None, :] == jnp.arange(count, dtype=jnp.int32)[:, None].astype(bf16)).astype(bf16)
    d_table = jnp.dot(picks, d_inputs, preferred_element_type=f32)
    small = jnp.concatenate((d_table, d_gain_attn, d_gain_mlp, jnp.zeros_like(d_gain_mlp)), axis=0)
    for bit in (1, 2):
        small = small + swap(small, "seq", bit)
    for bit in reversed(f_bits):
        small = small + swap(small, "fsdp", bit)
    owned_gain = lambda row: lax.dynamic_slice_in_dim(small[row], group * own_rows, own_rows)

    whole = lambda a: gather(a, "seq", (2, 1)).reshape(parts, *a.shape).astype(f32)
    grads = whole(grads)
    g_up = grads[:, 0].reshape(parts, own_rows, groups, ff_each).transpose(1, 2, 0, 3).reshape(own_rows, ff)
    g_down = grads[:, 1].reshape(ff // groups, width)
    d_wq = whole(d_wq)
    g_qkv = d_wq[..., : 3 * part].reshape(parts, own_rows, heads, 3, DH).transpose(1, 3, 0, 2, 4)
    g_out = jnp.swapaxes(d_wq[..., 3 * part :], 0, 1)
    return (
        jnp.swapaxes(out_back, 0, 1),
        jnp.swapaxes(d_back, 0, 1),
        small[:count],
        owned_gain(count),
        g_qkv.reshape(own_rows, 3 * width),
        g_out.reshape(own_rows, width),
        owned_gain(count + 1),
        g_up,
        g_down,
    )


def solution(mesh):
    return jax.shard_map(
        per_device,
        mesh=mesh,
        in_specs=(
            P(("seq", "fsdp"), None, None),
            P(("seq", "fsdp"), None),
            P(),
            P(),
            P("fsdp"),
            P("fsdp", None),
            P("fsdp", None),
            P("fsdp"),
            P("fsdp", None),
            P("fsdp", None),
            P(("seq", "fsdp"), None, None),
        ),
        out_specs=(
            P(("seq", "fsdp"), None, None),
            P(("seq", "fsdp"), None, None),
            P(),
            P("fsdp"),
            P("fsdp", None),
            P("fsdp", None),
            P("fsdp"),
            P("fsdp", None),
            P("fsdp", None),
        ),
        check_vma=False,
    )
```

```python
import functools

import jax
import jax.numpy as jnp
from jax import lax
from jax.experimental import pallas as pl
from jax.experimental.pallas import tpu as pltpu
from jax.sharding import PartitionSpec as P

HEADS = 12
EPSILON = 1e-05
LOG2E = 1.4426950408889634
LN2 = 0.6931471805599453
MASKED = -1e30
DH = 64


def dotg(a, b, ca, cb):
    return lax.dot_general(a, b, (((ca,), (cb,)), ((), ())), preferred_element_type=jnp.float32)


def slot_of(block, info):
    return (((block & 1) << 1) | (block >> 1)) ^ info[0]


def attend_body(info, qkv, before, out, lse, acc, *, blk):
    i = pl.program_id(0)
    length = info[1]
    qt = qkv[slot_of(i, info), 0:DH, :]
    scale = DH ** -0.5 * LOG2E

    def step(j, carry, masked):
        top, tot = carry
        kt = qkv[slot_of(j, info), DH : 2 * DH, :]
        vt = qkv[slot_of(j, info), 2 * DH : 3 * DH, :]
        st = dotg(kt, qt, 0, 0) * scale
        if masked:
            key_at = j * blk + lax.broadcasted_iota(jnp.int32, st.shape, 0)
            query_at = i * blk + lax.broadcasted_iota(jnp.int32, st.shape, 1)
            st = jnp.where((query_at >= key_at) & (key_at < length), st, MASKED)
        new_top = jnp.maximum(top, jnp.max(st, axis=0, keepdims=True))
        fade = jnp.exp2(top - new_top)
        pt = jnp.exp2(st - new_top)
        tot = tot * fade + jnp.sum(pt, axis=0, keepdims=True)
        acc[...] = acc[...] * fade + dotg(vt, pt.astype(jnp.bfloat16), 1, 0)
        return new_top, tot

    acc[...] = jnp.zeros_like(acc)
    carry = (jnp.full((1, blk), MASKED, jnp.float32), jnp.zeros((1, blk), jnp.float32))
    plain = jnp.minimum(i, length // blk)
    stop = jnp.minimum(i + 1, (length + blk - 1) // blk)
    carry = lax.fori_loop(0, plain, functools.partial(step, masked=False), carry)
    top, tot = lax.fori_loop(plain, stop, functools.partial(step, masked=True), carry)
    out[0] = (acc[...] / tot).astype(jnp.bfloat16)
    lse[0] = top + jnp.log2(tot)


def attend(info, qkv, before):
    blocks, rows, blk = qkv.shape
    heads = rows // (3 * DH)
    return pl.pallas_call(
        functools.partial(attend_body, blk=blk),
        grid_spec=pltpu.PrefetchScalarGridSpec(
            num_scalar_prefetch=1,
            grid=(blocks,),
            in_specs=[
                pl.BlockSpec((blocks, 3 * DH, blk), lambda i, info: (0, info[2], 0)),
                pl.BlockSpec(memory_space=pl.ANY),
            ],
            out_specs=[
                pl.BlockSpec((1, DH, blk), lambda i, info: (i, info[2], 0)),
                pl.BlockSpec((1, 1, blk), lambda i, info: (i, 0, 0)),
            ],
            scratch_shapes=[pltpu.VMEM((DH, blk), jnp.float32)],
        ),
        out_shape=[
            jax.ShapeDtypeStruct((blocks, heads * DH, blk), jnp.bfloat16),
            jax.ShapeDtypeStruct((blocks, 1, blk), jnp.float32),
        ],
        input_output_aliases={2: 0},
        compiler_params=pltpu.CompilerParams(vmem_limit_bytes=24 << 20),
        cost_estimate=SMALL,
        name="attend",
    )(info, qkv, before)


def attend_back_body(info, qkv, att, datt, lse, before, dqkv, dq, q_rows, do_rows, delta, *, blocks, blk):
    j = pl.program_id(0)
    length = info[1]
    scale = DH ** -0.5
    at_q, at_k, at_v = slice(0, DH), slice(DH, 2 * DH), slice(2 * DH, 3 * DH)

    @pl.when(j == 0)
    def _():
        dq[...] = jnp.zeros_like(dq)
        for b in range(blocks):
            dt = datt[b]
            q_rows[b] = qkv[slot_of(b, info), at_q, :].T
            do_rows[b] = dt.T
            delta[b] = jnp.sum(dt.astype(jnp.float32) * att[b].astype(jnp.float32), axis=0, keepdims=True)

    kt = qkv[slot_of(j, info), at_k, :]
    vt = qkv[slot_of(j, info), at_v, :]
    k_rows = kt.T
    v_rows = vt.T

    def step(i, carry, masked):
        dk, dv = carry
        qt = qkv[slot_of(i, info), at_q, :]
        st = jnp.dot(k_rows, qt, preferred_element_type=jnp.float32)
        pt = jnp.exp2(st * (scale * LOG2E) - lse[i])
        if masked:
            key_at = j * blk + lax.broadcasted_iota(jnp.int32, st.shape, 0)
            query_at = i * blk + lax.broadcasted_iota(jnp.int32, st.shape, 1)
            pt = jnp.where((query_at >= key_at) & (key_at < length), pt, 0.0)
        dpt = jnp.dot(v_rows, datt[i], preferred_element_type=jnp.float32)
        dst = (pt * (dpt - delta[i])).astype(jnp.bfloat16)
        dv = dv + jnp.dot(pt.astype(jnp.bfloat16), do_rows[i], preferred_element_type=jnp.float32)
        dk = dk + jnp.dot(dst, q_rows[i], preferred_element_type=jnp.float32)
        dq[i] = dq[i] + jnp.dot(kt, dst, preferred_element_type=jnp.float32)
        return dk, dv

    zero = jnp.zeros((blk, DH), jnp.float32)
    whole = (j + 1) * blk <= length
    some = j * blk < length
    masked_end = jnp.where(some, jnp.where(whole, j + 1, blocks), j)
    carry = lax.fori_loop(j, masked_end, functools.partial(step, masked=True), (zero, zero))
    dk, dv = lax.fori_loop(
        jnp.where(whole, j + 1, blocks), blocks, functools.partial(step, masked=False), carry
    )
    dqkv[slot_of(j, info), at_k, :] = (dk * scale).astype(jnp.bfloat16).T
    dqkv[slot_of(j, info), at_v, :] = dv.astype(jnp.bfloat16).T
    dqkv[slot_of(j, info), at_q, :] = (dq[j] * scale).astype(jnp.bfloat16)


def attend_back(info, qkv, att, datt, lse, before):
    blocks, rows, blk = qkv.shape
    third = pl.BlockSpec((blocks, 3 * DH, blk), lambda j, info: (0, info[2], 0))
    head = pl.BlockSpec((blocks, DH, blk), lambda j, info: (0, info[2], 0))
    return pl.pallas_call(
        functools.partial(attend_back_body, blocks=blocks, blk=blk),
        grid_spec=pltpu.PrefetchScalarGridSpec(
            num_scalar_prefetch=1,
            grid=(blocks,),
            in_specs=[
                third,
                head,
                head,
                pl.BlockSpec((blocks, 1, blk), lambda j, info: (0, 0, 0)),
                pl.BlockSpec(memory_space=pl.ANY),
            ],
            out_specs=third,
            scratch_shapes=[
                pltpu.VMEM((blocks, DH, blk), jnp.float32),
                pltpu.VMEM((blocks, blk, DH), jnp.bfloat16),
                pltpu.VMEM((blocks, blk, DH), jnp.bfloat16),
                pltpu.VMEM((blocks, 1, blk), jnp.float32),
            ],
        ),
        out_shape=jax.ShapeDtypeStruct(qkv.shape, jnp.bfloat16),
        input_output_aliases={5: 0},
        compiler_params=pltpu.CompilerParams(vmem_limit_bytes=24 << 20),
        cost_estimate=SMALL,
        name="attend_back",
    )(info, qkv, att, datt, lse, before)


SMALL = pl.CostEstimate(flops=1 << 20, bytes_accessed=1 << 20, transcendentals=0)
GELU_A = 0.7978845608028654
GELU_B = 0.044715


def mlp_body(nm, cot, wu, wd, *refs, begun, added):
    acc, dnm, dwu, dwd = refs[-4:]

    @pl.when(pl.program_id(0) == 0)
    def _():
        acc[...] = refs[0][...] if begun else jnp.zeros_like(acc)
        dnm[...] = refs[1][...] if begun else jnp.zeros_like(dnm)

    x = nm[...]
    g = cot[...]
    u = jnp.dot(x, wu[...], preferred_element_type=jnp.float32)
    da = dotg(g, wd[...], 1, 1)
    square = u * u
    th = jnp.tanh(GELU_A * u * (1.0 + GELU_B * square))
    half = 0.5 * (1.0 + th)
    a = (u * half).astype(jnp.bfloat16)
    slope = half + 0.5 * u * (1.0 - th * th) * (GELU_A * (1.0 + 3.0 * GELU_B * square))
    du = (da * slope).astype(jnp.bfloat16)
    acc[...] += jnp.dot(a, wd[...], preferred_element_type=jnp.float32)
    dnm[...] += dotg(du, wu[...], 1, 1)
    up = dotg(x, du, 0, 0)
    down = dotg(a, g, 0, 0)
    if added:
        up += refs[-6][...].astype(jnp.float32)
        down += refs[-5][...].astype(jnp.float32)
    dwu[...] = up.astype(jnp.bfloat16)
    dwd[...] = down.astype(jnp.bfloat16)


def mlp_part(nm, cot, wu, wd, sums=(), more=(), step=256):
    rows, width = nm.shape
    ff = wu.shape[1]
    whole = pl.BlockSpec((rows, width), lambda i: (0, 0))
    up = pl.BlockSpec((width, step), lambda i: (0, i))
    down = pl.BlockSpec((step, width), lambda i: (i, 0))
    return pl.pallas_call(
        functools.partial(mlp_body, begun=bool(sums), added=bool(more)),
        grid=(ff // step,),
        in_specs=[whole, whole, up, down] + [whole, whole][: len(sums)] + [up, down][: len(more)],
        out_specs=[whole, whole, up, down],
        out_shape=[
            jax.ShapeDtypeStruct((rows, width), jnp.float32),
            jax.ShapeDtypeStruct((rows, width), jnp.float32),
            jax.ShapeDtypeStruct(wu.shape, jnp.bfloat16),
            jax.ShapeDtypeStruct(wd.shape, jnp.bfloat16),
        ],
        input_output_aliases={4: 0, 5: 1} if sums else {},
        compiler_params=pltpu.CompilerParams(vmem_limit_bytes=36 << 20),
        cost_estimate=SMALL,
        name="mlp_part",
    )(nm, cot, wu, wd, *sums, *more)


def swap(value, axis, bit):
    count = lax.axis_size(axis)
    return lax.ppermute(value, axis, [(i, i ^ bit) for i in range(count)])


def bits_of(axis):
    count = lax.axis_size(axis)
    assert count & (count - 1) == 0, "axis size"
    return [1 << b for b in reversed(range(count.bit_length() - 1))]


def is_set(axis, bit):
    return (lax.axis_index(axis) & bit) != 0


def join(own, came, axis, bit, at):
    own, came = (jnp.expand_dims(a, at) for a in (own, came))
    shape = own.shape[:at] + (2,) + own.shape[at + 1 :]
    place = lax.broadcasted_iota(jnp.int32, shape, at)
    return jnp.where(place == is_set(axis, bit).astype(jnp.int32), own, came)


def gather(value, axis, bits, at=0):
    for k, bit in enumerate(bits):
        value = join(value, swap(value, axis, bit), axis, bit, at + k)
    return value


def spread(blocks, bit):
    return blocks | {r ^ bit: swap(b, "seq", bit) for r, b in blocks.items()}


def add(a, b):
    return (a.astype(jnp.float32) + b.astype(jnp.float32)).astype(a.dtype)


def fold(blocks, bit):
    return {r: add(b, swap(blocks[r ^ bit], "seq", bit)) for r, b in blocks.items() if not r & bit}


def halve(value, axis, bit, at, *more):
    mine = is_set(axis, bit).astype(jnp.int32)
    part = lambda which: functools.reduce(
        add, [lax.dynamic_index_in_dim(v, which, at, keepdims=False) for v in (value, *more)]
    )
    return part(mine), swap(part(1 - mine), axis, bit)


def norm_stats(values):
    centre = jnp.mean(values, axis=-1, keepdims=True)
    shifted = values - centre
    spread_of = jnp.mean(shifted * shifted, axis=-1, keepdims=True)
    inverse = lax.rsqrt(spread_of + EPSILON)
    return shifted * inverse, inverse


def norm_back(z, inverse, gain, grad):
    e = grad * gain
    back = (e - jnp.mean(e, axis=-1, keepdims=True) - z * jnp.mean(e * z, axis=-1, keepdims=True)) * inverse
    return back, jnp.sum(grad * z, axis=0, keepdims=True)


def pick_at(value, at):
    return lax.dynamic_index_in_dim(value, at, 1, keepdims=False)


def after(first, *values):
    return lax.optimization_barrier((first, values))[1]


def per_device(
    tokens, pass_index, lengths, table, gain_attn, w_qkv, w_out, gain_mlp, w_up, w_down, cotangent
):
    bf16, f32 = jnp.bfloat16, jnp.float32
    groups, parts = lax.axis_size("fsdp"), lax.axis_size("seq")
    local_len, seq_total, width = tokens.shape
    assert seq_total == groups and parts == 4
    heads = HEADS // parts
    part = width // parts
    ff = w_up.shape[1]
    own_rows = width // groups
    ff_each = ff // groups // parts
    me, group = lax.axis_index("seq"), lax.axis_index("fsdp")
    f_bits = bits_of("fsdp")
    last = len(f_bits) - 1
    top, low, between = f_bits[0], f_bits[-1], f_bits[1:-1]
    sizes = (2,) * len(f_bits)
    span = local_len * groups
    pick = lambda a, at: lax.dynamic_index_in_dim(a, me, at, keepdims=False)
    deal = lambda a: lax.all_to_all(a, "fsdp", split_axis=0, concat_axis=0, tiled=True)
    across = lambda a: lax.all_to_all(a, "seq", split_axis=0, concat_axis=0, tiled=True)

    chooser = (pass_index[..., None] == jnp.arange(table.shape[0], dtype=jnp.int32)).astype(bf16)
    embedded = jnp.einsum("pnc,cd->npd", chooser, table, preferred_element_type=f32)
    summed = (jnp.swapaxes(tokens, 0, 1).astype(f32) + embedded).astype(bf16)
    inputs = deal(summed).reshape(span, width)
    qkv_slice = pick(w_qkv.reshape(own_rows, 3, parts, heads, DH), 2)
    qkv_slice = jnp.swapaxes(qkv_slice, 1, 2).reshape(own_rows, 3 * part)
    out_slice = pick(w_out.reshape(own_rows, parts, part), 1)
    gains = jnp.stack((gain_attn, gain_mlp), axis=1)
    qkv_slice, out_slice = after(summed, qkv_slice, out_slice)
    packet = jnp.concatenate((qkv_slice, out_slice, gains, jnp.zeros((own_rows, 126), bf16)), axis=1)
    packet = gather(packet, "fsdp", f_bits).reshape(width, -1)
    wq = packet[:, : 3 * part]
    out_cols = packet[:, 3 * part : width]
    gain_one = packet[:, width].astype(f32)
    gain_two = packet[:, width + 1].astype(f32)
    up = pick(w_up.reshape(own_rows, groups, parts, ff_each), 2).reshape(own_rows, ff // parts)
    down = pick(w_down.reshape(parts, ff_each, width), 0)
    up_came = swap(up, "fsdp", top)
    down_came = swap(down, "seq", 2)

    rows_2, rows_1 = swap(inputs, "seq", 2), swap(inputs, "seq", 1)
    rows = (inputs, rows_2, rows_1, swap(rows_2, "seq", 1))
    up, up_came, down, down_came = after(inputs, up, up_came, down, down_came)
    up = join(up, up_came, "fsdp", top, 0)
    down = jnp.stack((down, down_came))
    up_came = swap(up, "fsdp", between[0])
    down_came = swap(down, "fsdp", top)

    normed = [(norm_stats(b.astype(f32))[0] * gain_one).astype(bf16) for b in rows]
    qkv = jnp.stack([dotg(wq, b, 0, 1).astype(bf16) for b in normed])
    length = lax.dynamic_index_in_dim(lengths, group, 0, keepdims=False)
    slot = (me & 1) * 2 + (me >> 1)
    info = [jnp.stack((slot, length, jnp.int32(h))).astype(jnp.int32) for h in range(heads)]
    up, up_came, down, down_came = after(rows[3], up, up_came, down, down_came)
    up = join(up, up_came, "fsdp", between[0], 1)
    up = gather(up, "fsdp", between[1:], 2)
    down = join(down, down_came, "fsdp", top, 1)

    marks = jnp.swapaxes(pass_index, 0, 1)[..., None].astype(bf16)
    cot_packet = jnp.concatenate(
        (jnp.swapaxes(cotangent, 0, 1), jnp.broadcast_to(marks, marks.shape[:2] + (128,))), axis=2
    )
    cot_packet, out_cols = after(rows[3], cot_packet, out_cols)
    (qkv,) = after((up, down, cot_packet), qkv)
    cot_packet = deal(cot_packet).reshape(span, -1)
    up_came = swap(up, "fsdp", low)
    down_came = swap(down, "fsdp", between[0])
    out_2 = swap(out_cols, "seq", 2)
    lse = [None] * heads
    att_heads = jnp.zeros((parts, part, span), bf16)
    att_heads, lse[0] = attend(info[0], qkv, att_heads)
    up, up_came, out_cols, out_2 = after(att_heads, up, up_came, out_cols, out_2)
    up = join(up, up_came, "fsdp", low, last).reshape(width, ff // parts)
    out_pair = jnp.stack((out_cols, out_2))
    (qkv,) = after((up, out_pair), qkv)
    up_came = swap(up, "seq", 2)
    out_came = swap(out_pair, "seq", 1)
    att_heads, lse[1] = attend(info[1], qkv, att_heads)
    down, down_came = after(att_heads, down, down_came)
    down = join(down, down_came, "fsdp", between[0], 2)
    down = gather(down, "fsdp", between[1:], 3)
    (qkv,) = after(down, qkv)
    down_came = swap(down, "fsdp", low)
    att_heads, lse[2] = attend(info[2], qkv, att_heads)
    out_came, cot_packet = after(att_heads, out_came, cot_packet)
    cot = cot_packet[:, :width]
    passes = cot_packet[:, width]
    cot_far = swap(cot, "seq", 1)
    w_out_full = jnp.concatenate((out_pair, out_came))
    w_out_full = jnp.concatenate(
        [lax.dynamic_index_in_dim(w_out_full, r ^ slot, 0, keepdims=False) for r in (0, 2, 1, 3)], axis=1
    )
    att = across(att_heads).reshape(width, span)

    down, down_came, up, up_came = after(att, down, down_came, up, up_came)
    down = join(down, down_came, "fsdp", low, last + 1).reshape(2, ff // parts, width)
    residual = inputs.astype(f32) + dotg(att, w_out_full, 0, 0)
    z_two, inverse_two = norm_stats(residual)
    nm = (z_two * gain_two).astype(bf16)
    nm_far = swap(nm, "seq", 1)
    *far, up_2, down_2 = mlp_part(nm_far, cot_far, up_came, down[1])
    *near, up_2, down_2 = mlp_part(nm, cot, up_came, down[1], (), (up_2, down_2))
    *far, up_0, down_0 = mlp_part(nm_far, cot_far, up, down[0], far)
    up_came = swap(up_2, "seq", 2)
    far = [swap(a.astype(bf16), "seq", 1).astype(f32) for a in far]
    *near, up_0, down_0 = mlp_part(nm, cot, up, down[0], near, (up_0, down_0))
    result = (residual + near[0] + far[0]).astype(bf16)
    d_res_norm, d_gain_mlp = norm_back(z_two, inverse_two, gain_two, near[1] + far[1])
    d_residual = cot.astype(f32) + d_res_norm
    d_branch = d_residual.astype(bf16)
    d_att = dotg(w_out_full, d_branch, 1, 1).astype(bf16)
    d_heads = across(d_att.reshape(parts, part, span))

    down_0, down_2, result = after(d_att, down_0, down_2, result)
    down = jnp.stack((down_0, down_2)).reshape(2, *sizes, ff_each, width)
    down = halve(down, "fsdp", low, last + 1)
    up_0, up_came, result = after(d_heads, up_0, up_came, result)
    out_back = deal(result.reshape(groups, local_len, width))
    split = lambda a: a.reshape(*sizes, own_rows, ff // parts)
    up = halve(split(up_0), "fsdp", low, last, split(up_came))
    d_cols = d_branch.reshape(span, parts, part)
    d_out = jnp.stack([dotg(att, pick_at(d_cols, me ^ r), 1, 0).astype(bf16) for r in (0, 2, 1, 3)])
    (d_heads,) = after((up[0], d_out), d_heads)
    d_out_far = swap(d_out[2:], "seq", 1)
    d_qkv = jnp.zeros_like(qkv)
    d_qkv = attend_back(info[0], qkv, att_heads, d_heads, lse[0], d_qkv)
    down, d_out, d_out_far = after(d_qkv, down, d_out, d_out_far)
    down = halve(down[0], "fsdp", f_bits[-2], last, down[1])
    d_out = add(d_out[:2], d_out_far)
    (d_heads,) = after((down[0], d_out), d_heads)
    d_out_far = swap(d_out[1], "seq", 2)
    d_qkv = attend_back(info[1], qkv, att_heads, d_heads, lse[1], d_qkv)
    up, d_out, d_out_far = after(d_qkv, up, d_out, d_out_far)
    up = halve(up[0], "fsdp", f_bits[-2], last - 1, up[1])
    columns = lambda start, stop: sum(dotg(normed[r], d_qkv[r, start:stop], 0, 1) for r in range(parts)).astype(bf16)
    early = (2 * heads // 3) * 3 * DH
    d_wq = jnp.concatenate((columns(0, early), add(d_out[0], d_out_far)), axis=1)
    d_wq = halve(d_wq.reshape(*sizes, own_rows, early + part), "fsdp", low, last)
    (d_heads,) = after((up[0], d_wq[0]), d_heads)
    d_qkv = attend_back(info[2], qkv, att_heads, d_heads, lse[2], d_qkv)

    project_back = lambda a: jnp.einsum("rcp,dc->rpd", a, wq, preferred_element_type=f32).astype(bf16)
    d_far = swap(project_back(d_qkv[2:]), "seq", 1)
    d_near = project_back(d_qkv[:2])
    (d_tail,) = after(d_near, d_qkv)
    d_qkv = d_tail
    d_late = halve(columns(early, 3 * part).reshape(*sizes, own_rows, 3 * part - early), "fsdp", low, last)
    d_near = add(d_near, d_far)
    d_came = swap(d_near[1], "seq", 2)
    up, down, d_wq, d_late = after(d_near, up, down, d_wq, d_late)
    for k in reversed(range(last - 1)):
        up = halve(up[0], "fsdp", f_bits[k], k, up[1])
        down = halve(down[0], "fsdp", f_bits[k], k + 1, down[1])
    d_wq = tuple(jnp.concatenate(pair, axis=-1) for pair in zip(d_wq, d_late))
    for k in reversed(range(last)):
        d_wq = halve(d_wq[0], "fsdp", f_bits[k], k, *d_wq[1:])
    d_normed = d_near[0].astype(f32) + d_came.astype(f32)
    z_one, inverse_one = norm_stats(inputs.astype(f32))
    d_in_norm, d_gain_attn = norm_back(z_one, inverse_one, gain_one, d_normed)
    d_inputs = (d_residual + d_in_norm).astype(bf16)
    d_back = deal(d_inputs.reshape(groups, local_len, width))
    up, down, d_wq = after(d_inputs, up, down, d_wq)
    up = add(*up)
    down = add(*down)
    down = add(down[0], swap(down[1], "seq", 2))
    grads = gather(jnp.stack((up, down)), "seq", (2, 1)).reshape(parts, 2, own_rows, width).astype(f32)
    g_up = grads[:, 0].reshape(parts, own_rows, groups, ff_each).transpose(1, 2, 0, 3).reshape(own_rows, ff)
    g_down = grads[:, 1].reshape(ff // groups, width)

    count = table.shape[0]
    picks = (passes[None, :] == jnp.arange(count, dtype=jnp.int32)[:, None].astype(bf16)).astype(bf16)
    d_table = jnp.dot(picks, d_inputs, preferred_element_type=f32)
    small = jnp.concatenate((d_table, d_gain_attn, d_gain_mlp, jnp.zeros_like(d_gain_mlp)), axis=0)
    for bit in (1, 2):
        small = small + swap(small, "seq", bit)
    for bit in reversed(f_bits):
        small = small + swap(small, "fsdp", bit)
    owned_gain = lambda row: lax.dynamic_slice_in_dim(small[row], group * own_rows, own_rows)

    d_wq = gather(add(*d_wq), "seq", (2, 1)).reshape(parts, own_rows, width).astype(f32)
    g_out = jnp.swapaxes(d_wq[..., early : early + part], 0, 1)
    d_wq = jnp.concatenate((d_wq[..., :early], d_wq[..., early + part :]), axis=-1)
    g_qkv = d_wq.reshape(parts, own_rows, heads, 3, DH).transpose(1, 3, 0, 2, 4)
    return (
        jnp.swapaxes(out_back, 0, 1),
        jnp.swapaxes(d_back, 0, 1),
        small[:count],
        owned_gain(count),
        g_qkv.reshape(own_rows, 3 * width),
        g_out.reshape(own_rows, width),
        owned_gain(count + 1),
        g_up,
        g_down,
    )


def solution(mesh):
    return jax.shard_map(
        per_device,
        mesh=mesh,
        in_specs=(
            P(("seq", "fsdp"), None, None),
            P(("seq", "fsdp"), None),
            P(),
            P(),
            P("fsdp"),
            P("fsdp", None),
            P("fsdp", None),
            P("fsdp"),
            P("fsdp", None),
            P("fsdp", None),
            P(("seq", "fsdp"), None, None),
        ),
        out_specs=(
            P(("seq", "fsdp"), None, None),
            P(("seq", "fsdp"), None, None),
            P(),
            P("fsdp"),
            P("fsdp", None),
            P("fsdp", None),
            P("fsdp"),
            P("fsdp", None),
            P("fsdp", None),
        ),
        check_vma=False,
    )
```

```python
import functools

import jax
import jax.numpy as jnp
from jax import lax
from jax.experimental import pallas as pl
from jax.experimental.pallas import tpu as pltpu
from jax.sharding import PartitionSpec as P

HEADS = 12
EPSILON = 1e-05
LOG2E = 1.4426950408889634
LN2 = 0.6931471805599453
MASKED = -1e30
DH = 64


def dotg(a, b, ca, cb):
    return lax.dot_general(a, b, (((ca,), (cb,)), ((), ())), preferred_element_type=jnp.float32)


def slot_of(block, info):
    return (((block & 1) << 1) | (block >> 1)) ^ info[0]


def attend_body(info, qkv, before, out, lse, acc, *, blk):
    i = pl.program_id(0)
    length = info[1]
    qt = qkv[slot_of(i, info), 0:DH, :]
    scale = DH ** -0.5 * LOG2E

    def step(j, carry, masked):
        top, tot = carry
        kt = qkv[slot_of(j, info), DH : 2 * DH, :]
        vt = qkv[slot_of(j, info), 2 * DH : 3 * DH, :]
        st = dotg(kt, qt, 0, 0) * scale
        if masked:
            key_at = j * blk + lax.broadcasted_iota(jnp.int32, st.shape, 0)
            query_at = i * blk + lax.broadcasted_iota(jnp.int32, st.shape, 1)
            st = jnp.where((query_at >= key_at) & (key_at < length), st, MASKED)
        new_top = jnp.maximum(top, jnp.max(st, axis=0, keepdims=True))
        fade = jnp.exp2(top - new_top)
        pt = jnp.exp2(st - new_top)
        tot = tot * fade + jnp.sum(pt, axis=0, keepdims=True)
        acc[...] = acc[...] * fade + dotg(vt, pt.astype(jnp.bfloat16), 1, 0)
        return new_top, tot

    acc[...] = jnp.zeros_like(acc)
    carry = (jnp.full((1, blk), MASKED, jnp.float32), jnp.zeros((1, blk), jnp.float32))
    plain = jnp.minimum(i, length // blk)
    stop = jnp.minimum(i + 1, (length + blk - 1) // blk)
    carry = lax.fori_loop(0, plain, functools.partial(step, masked=False), carry)
    top, tot = lax.fori_loop(plain, stop, functools.partial(step, masked=True), carry)
    out[0] = (acc[...] / tot).astype(jnp.bfloat16)
    lse[0] = top + jnp.log2(tot)


def attend(info, qkv, before):
    blocks, rows, blk = qkv.shape
    heads = rows // (3 * DH)
    return pl.pallas_call(
        functools.partial(attend_body, blk=blk),
        grid_spec=pltpu.PrefetchScalarGridSpec(
            num_scalar_prefetch=1,
            grid=(blocks,),
            in_specs=[
                pl.BlockSpec((blocks, 3 * DH, blk), lambda i, info: (0, info[2], 0)),
                pl.BlockSpec(memory_space=pl.ANY),
            ],
            out_specs=[
                pl.BlockSpec((1, DH, blk), lambda i, info: (i, info[2], 0)),
                pl.BlockSpec((1, 1, blk), lambda i, info: (i, 0, 0)),
            ],
            scratch_shapes=[pltpu.VMEM((DH, blk), jnp.float32)],
        ),
        out_shape=[
            jax.ShapeDtypeStruct((blocks, heads * DH, blk), jnp.bfloat16),
            jax.ShapeDtypeStruct((blocks, 1, blk), jnp.float32),
        ],
        input_output_aliases={2: 0},
        compiler_params=pltpu.CompilerParams(vmem_limit_bytes=24 << 20),
        cost_estimate=SMALL,
        name="attend",
    )(info, qkv, before)


def attend_back_body(info, qkv, att, datt, lse, before, dqkv, dq, q_rows, do_rows, delta, *, blocks, blk):
    j = pl.program_id(0)
    length = info[1]
    scale = DH ** -0.5
    at_q, at_k, at_v = slice(0, DH), slice(DH, 2 * DH), slice(2 * DH, 3 * DH)

    @pl.when(j == 0)
    def _():
        dq[...] = jnp.zeros_like(dq)
        for b in range(blocks):
            dt = datt[b]
            q_rows[b] = qkv[slot_of(b, info), at_q, :].T
            do_rows[b] = dt.T
            delta[b] = jnp.sum(dt.astype(jnp.float32) * att[b].astype(jnp.float32), axis=0, keepdims=True)

    kt = qkv[slot_of(j, info), at_k, :]
    vt = qkv[slot_of(j, info), at_v, :]
    k_rows = kt.T
    v_rows = vt.T

    def step(i, carry, masked):
        dk, dv = carry
        qt = qkv[slot_of(i, info), at_q, :]
        st = jnp.dot(k_rows, qt, preferred_element_type=jnp.float32)
        pt = jnp.exp2(st * (scale * LOG2E) - lse[i])
        if masked:
            key_at = j * blk + lax.broadcasted_iota(jnp.int32, st.shape, 0)
            query_at = i * blk + lax.broadcasted_iota(jnp.int32, st.shape, 1)
            pt = jnp.where((query_at >= key_at) & (key_at < length), pt, 0.0)
        dpt = jnp.dot(v_rows, datt[i], preferred_element_type=jnp.float32)
        dst = (pt * (dpt - delta[i])).astype(jnp.bfloat16)
        dv = dv + jnp.dot(pt.astype(jnp.bfloat16), do_rows[i], preferred_element_type=jnp.float32)
        dk = dk + jnp.dot(dst, q_rows[i], preferred_element_type=jnp.float32)
        dq[i] = dq[i] + jnp.dot(kt, dst, preferred_element_type=jnp.float32)
        return dk, dv

    zero = jnp.zeros((blk, DH), jnp.float32)
    whole = (j + 1) * blk <= length
    some = j * blk < length
    masked_end = jnp.where(some, jnp.where(whole, j + 1, blocks), j)
    carry = lax.fori_loop(j, masked_end, functools.partial(step, masked=True), (zero, zero))
    dk, dv = lax.fori_loop(
        jnp.where(whole, j + 1, blocks), blocks, functools.partial(step, masked=False), carry
    )
    dqkv[slot_of(j, info), at_k, :] = (dk * scale).astype(jnp.bfloat16).T
    dqkv[slot_of(j, info), at_v, :] = dv.astype(jnp.bfloat16).T
    dqkv[slot_of(j, info), at_q, :] = (dq[j] * scale).astype(jnp.bfloat16)


def attend_back(info, qkv, att, datt, lse, before):
    blocks, rows, blk = qkv.shape
    third = pl.BlockSpec((blocks, 3 * DH, blk), lambda j, info: (0, info[2], 0))
    head = pl.BlockSpec((blocks, DH, blk), lambda j, info: (0, info[2], 0))
    return pl.pallas_call(
        functools.partial(attend_back_body, blocks=blocks, blk=blk),
        grid_spec=pltpu.PrefetchScalarGridSpec(
            num_scalar_prefetch=1,
            grid=(blocks,),
            in_specs=[
                third,
                head,
                head,
                pl.BlockSpec((blocks, 1, blk), lambda j, info: (0, 0, 0)),
                pl.BlockSpec(memory_space=pl.ANY),
            ],
            out_specs=third,
            scratch_shapes=[
                pltpu.VMEM((blocks, DH, blk), jnp.float32),
                pltpu.VMEM((blocks, blk, DH), jnp.bfloat16),
                pltpu.VMEM((blocks, blk, DH), jnp.bfloat16),
                pltpu.VMEM((blocks, 1, blk), jnp.float32),
            ],
        ),
        out_shape=jax.ShapeDtypeStruct(qkv.shape, jnp.bfloat16),
        input_output_aliases={5: 0},
        compiler_params=pltpu.CompilerParams(vmem_limit_bytes=24 << 20),
        cost_estimate=SMALL,
        name="attend_back",
    )(info, qkv, att, datt, lse, before)


SMALL = pl.CostEstimate(flops=1 << 20, bytes_accessed=1 << 20, transcendentals=0)
GELU_A = 0.7978845608028654
GELU_B = 0.044715


def mlp_body(nm, cot, wu, wd, *refs, begun, added):
    acc, dnm, dwu, dwd = refs[-4:]

    @pl.when(pl.program_id(0) == 0)
    def _():
        acc[...] = refs[0][...] if begun else jnp.zeros_like(acc)
        dnm[...] = refs[1][...] if begun else jnp.zeros_like(dnm)

    x = nm[...]
    g = cot[...]
    u = jnp.dot(x, wu[...], preferred_element_type=jnp.float32)
    da = dotg(g, wd[...], 1, 1)
    square = u * u
    th = jnp.tanh(GELU_A * u * (1.0 + GELU_B * square))
    half = 0.5 * (1.0 + th)
    a = (u * half).astype(jnp.bfloat16)
    slope = half + 0.5 * u * (1.0 - th * th) * (GELU_A * (1.0 + 3.0 * GELU_B * square))
    du = (da * slope).astype(jnp.bfloat16)
    acc[...] += jnp.dot(a, wd[...], preferred_element_type=jnp.float32)
    dnm[...] += dotg(du, wu[...], 1, 1)
    up = dotg(x, du, 0, 0)
    down = dotg(a, g, 0, 0)
    if added:
        up += refs[-6][...].astype(jnp.float32)
        down += refs[-5][...].astype(jnp.float32)
    dwu[...] = up.astype(jnp.bfloat16)
    dwd[...] = down.astype(jnp.bfloat16)


def mlp_part(nm, cot, wu, wd, sums=(), more=(), step=256):
    rows, width = nm.shape
    ff = wu.shape[1]
    whole = pl.BlockSpec((rows, width), lambda i: (0, 0))
    up = pl.BlockSpec((width, step), lambda i: (0, i))
    down = pl.BlockSpec((step, width), lambda i: (i, 0))
    return pl.pallas_call(
        functools.partial(mlp_body, begun=bool(sums), added=bool(more)),
        grid=(ff // step,),
        in_specs=[whole, whole, up, down] + [whole, whole][: len(sums)] + [up, down][: len(more)],
        out_specs=[whole, whole, up, down],
        out_shape=[
            jax.ShapeDtypeStruct((rows, width), jnp.float32),
            jax.ShapeDtypeStruct((rows, width), jnp.float32),
            jax.ShapeDtypeStruct(wu.shape, jnp.bfloat16),
            jax.ShapeDtypeStruct(wd.shape, jnp.bfloat16),
        ],
        input_output_aliases={4: 0, 5: 1} if sums else {},
        compiler_params=pltpu.CompilerParams(vmem_limit_bytes=36 << 20),
        cost_estimate=SMALL,
        name="mlp_part",
    )(nm, cot, wu, wd, *sums, *more)


def swap(value, axis, bit):
    count = lax.axis_size(axis)
    return lax.ppermute(value, axis, [(i, i ^ bit) for i in range(count)])


def bits_of(axis):
    count = lax.axis_size(axis)
    assert count & (count - 1) == 0, "axis size"
    return [1 << b for b in reversed(range(count.bit_length() - 1))]


def is_set(axis, bit):
    return (lax.axis_index(axis) & bit) != 0


def join(own, came, axis, bit, at):
    own, came = (jnp.expand_dims(a, at) for a in (own, came))
    shape = own.shape[:at] + (2,) + own.shape[at + 1 :]
    place = lax.broadcasted_iota(jnp.int32, shape, at)
    return jnp.where(place == is_set(axis, bit).astype(jnp.int32), own, came)


def gather(value, axis, bits, at=0):
    for k, bit in enumerate(bits):
        value = join(value, swap(value, axis, bit), axis, bit, at + k)
    return value


def spread(blocks, bit):
    return blocks | {r ^ bit: swap(b, "seq", bit) for r, b in blocks.items()}


def add(a, b):
    return (a.astype(jnp.float32) + b.astype(jnp.float32)).astype(a.dtype)


def fold(blocks, bit):
    return {r: add(b, swap(blocks[r ^ bit], "seq", bit)) for r, b in blocks.items() if not r & bit}


def halve(value, axis, bit, at, *more):
    mine = is_set(axis, bit).astype(jnp.int32)
    part = lambda which: functools.reduce(
        add, [lax.dynamic_index_in_dim(v, which, at, keepdims=False) for v in (value, *more)]
    )
    return part(mine), swap(part(1 - mine), axis, bit)


def norm_stats(values):
    centre = jnp.mean(values, axis=-1, keepdims=True)
    shifted = values - centre
    spread_of = jnp.mean(shifted * shifted, axis=-1, keepdims=True)
    inverse = lax.rsqrt(spread_of + EPSILON)
    return shifted * inverse, inverse


def norm_back(z, inverse, gain, grad):
    e = grad * gain
    back = (e - jnp.mean(e, axis=-1, keepdims=True) - z * jnp.mean(e * z, axis=-1, keepdims=True)) * inverse
    return back, jnp.sum(grad * z, axis=0, keepdims=True)


def pick_at(value, at):
    return lax.dynamic_index_in_dim(value, at, 1, keepdims=False)


def after(first, *values):
    return lax.optimization_barrier((first, values))[1]


def per_device(
    tokens, pass_index, lengths, table, gain_attn, w_qkv, w_out, gain_mlp, w_up, w_down, cotangent
):
    bf16, f32 = jnp.bfloat16, jnp.float32
    groups, parts = lax.axis_size("fsdp"), lax.axis_size("seq")
    local_len, seq_total, width = tokens.shape
    assert seq_total == groups and parts == 4
    heads = HEADS // parts
    part = width // parts
    ff = w_up.shape[1]
    own_rows = width // groups
    ff_each = ff // groups // parts
    me, group = lax.axis_index("seq"), lax.axis_index("fsdp")
    f_bits = bits_of("fsdp")
    last = len(f_bits) - 1
    top, low, between = f_bits[0], f_bits[-1], f_bits[1:-1]
    sizes = (2,) * len(f_bits)
    span = local_len * groups
    pick = lambda a, at: lax.dynamic_index_in_dim(a, me, at, keepdims=False)
    deal = lambda a: lax.all_to_all(a, "fsdp", split_axis=0, concat_axis=0, tiled=True)
    across = lambda a: lax.all_to_all(a, "seq", split_axis=0, concat_axis=0, tiled=True)

    chooser = (pass_index[..., None] == jnp.arange(table.shape[0], dtype=jnp.int32)).astype(bf16)
    embedded = jnp.einsum("pnc,cd->npd", chooser, table, preferred_element_type=f32)
    summed = (jnp.swapaxes(tokens, 0, 1).astype(f32) + embedded).astype(bf16)
    inputs = deal(summed).reshape(span, width)
    qkv_slice = pick(w_qkv.reshape(own_rows, 3, parts, heads, DH), 2)
    qkv_slice = jnp.swapaxes(qkv_slice, 1, 2).reshape(own_rows, 3 * part)
    out_slice = pick(w_out.reshape(own_rows, parts, part), 1)
    gains = jnp.stack((gain_attn, gain_mlp), axis=1)
    qkv_slice, out_slice = after(summed, qkv_slice, out_slice)
    packet = jnp.concatenate((qkv_slice, out_slice, gains, jnp.zeros((own_rows, 126), bf16)), axis=1)
    packet_came = swap(packet, "fsdp", top)
    up = pick(w_up.reshape(own_rows, groups, parts, ff_each), 2).reshape(own_rows, ff // parts)
    down = pick(w_down.reshape(parts, ff_each, width), 0)
    pair = jnp.stack((up, down))

    rows_2, rows_1 = swap(inputs, "seq", 2), swap(inputs, "seq", 1)
    rows = (inputs, rows_2, rows_1, swap(rows_2, "seq", 1))
    packet, packet_came, pair = after(inputs, packet, packet_came, pair)
    packet = gather(join(packet, packet_came, "fsdp", top, 0), "fsdp", f_bits[1:], 1).reshape(width, -1)
    wq = packet[:, : 3 * part]
    out_cols = packet[:, 3 * part : width]
    gain_one = packet[:, width].astype(f32)
    gain_two = packet[:, width + 1].astype(f32)
    pair_came = swap(pair, "fsdp", top)
    marks = jnp.swapaxes(pass_index, 0, 1)[..., None].astype(bf16)
    cot_packet = jnp.concatenate(
        (jnp.swapaxes(cotangent, 0, 1), jnp.broadcast_to(marks, marks.shape[:2] + (128,))), axis=2
    )

    normed = [(norm_stats(b.astype(f32))[0] * gain_one).astype(bf16) for b in rows]
    pair, pair_came, cot_packet, out_cols = after(rows[3], pair, pair_came, cot_packet, out_cols)
    pair = join(pair, pair_came, "fsdp", top, 1)
    pair = gather(pair, "fsdp", between, 2)
    cot_packet = deal(cot_packet).reshape(span, -1)
    out_2 = swap(out_cols, "seq", 2)
    qkv = jnp.stack([dotg(wq, b, 0, 1).astype(bf16) for b in normed])
    length = lax.dynamic_index_in_dim(lengths, group, 0, keepdims=False)
    slot = (me & 1) * 2 + (me >> 1)
    info = [jnp.stack((slot, length, jnp.int32(h))).astype(jnp.int32) for h in range(heads)]

    lse = [None] * heads
    att_heads = jnp.zeros((parts, part, span), bf16)
    att_heads, lse[0] = attend(info[0], qkv, att_heads)
    pair, out_cols, out_2 = after(att_heads, pair, out_cols, out_2)
    up, down = pair[0], pair[1]
    out_pair = jnp.stack((out_cols, out_2))
    (qkv,) = after((up, down, out_pair), qkv)
    up_came = swap(up, "fsdp", low)
    down_came = swap(down, "fsdp", low)
    down_2 = swap(down, "seq", 2)
    out_came = swap(out_pair, "seq", 1)
    att_heads, lse[1] = attend(info[1], qkv, att_heads)
    att_heads, lse[2] = attend(info[2], qkv, att_heads)
    up, up_came, out_came = after(att_heads, up, up_came, out_came)
    up = join(up, up_came, "fsdp", low, last).reshape(width, ff // parts)
    (att_heads,) = after(up, att_heads)
    up_2 = swap(up, "seq", 2)
    w_out_full = jnp.concatenate((out_pair, out_came))
    w_out_full = jnp.concatenate(
        [lax.dynamic_index_in_dim(w_out_full, r ^ slot, 0, keepdims=False) for r in (0, 2, 1, 3)], axis=1
    )
    att = across(att_heads).reshape(width, span)

    down, down_came, down_2, cot_packet = after(att, down, down_came, down_2, cot_packet)
    cot = cot_packet[:, :width]
    passes = cot_packet[:, width]
    cot_far = swap(cot, "seq", 1)
    down_2_came = swap(down_2, "fsdp", low)
    down = join(down, down_came, "fsdp", low, last).reshape(ff // parts, width)
    residual = inputs.astype(f32) + dotg(att, w_out_full, 0, 0)
    z_two, inverse_two = norm_stats(residual)
    nm = (z_two * gain_two).astype(bf16)
    nm_far = swap(nm, "seq", 1)
    *near, up_0, down_0 = mlp_part(nm, cot, up, down)
    *far, up_0, down_0 = mlp_part(nm_far, cot_far, up, down, (), (up_0, down_0))
    down_2, down_2_came, up_2 = after(far[0], down_2, down_2_came, up_2)
    down_2 = join(down_2, down_2_came, "fsdp", low, last).reshape(ff // parts, width)
    *far, d_up_2, d_down_2 = mlp_part(nm_far, cot_far, up_2, down_2, far)
    far = [swap(a.astype(bf16), "seq", 1).astype(f32) for a in far]
    *near, up_2, down_2 = mlp_part(nm, cot, up_2, down_2, near, (d_up_2, d_down_2))
    result = (residual + near[0] + far[0]).astype(bf16)
    d_res_norm, d_gain_mlp = norm_back(z_two, inverse_two, gain_two, near[1] + far[1])
    d_residual = cot.astype(f32) + d_res_norm
    d_branch = d_residual.astype(bf16)
    down = jnp.stack((down_0, down_2)).reshape(2, *sizes, ff_each, width)
    down = halve(down, "fsdp", low, last + 1)
    d_att = dotg(w_out_full, d_branch, 1, 1).astype(bf16)
    d_heads = across(d_att.reshape(parts, part, span))

    up_0, up_2, result = after(d_heads, up_0, up_2, result)
    up_came = swap(up_2, "seq", 2)
    out_back = deal(result.reshape(groups, local_len, width))
    d_cols = d_branch.reshape(span, parts, part)
    d_out = jnp.stack([dotg(att, pick_at(d_cols, me ^ r), 1, 0).astype(bf16) for r in (0, 2, 1, 3)])
    (d_heads,) = after(d_out, d_heads)
    d_out_far = swap(d_out[2:], "seq", 1)
    d_qkv = jnp.zeros_like(qkv)
    d_qkv = attend_back(info[0], qkv, att_heads, d_heads, lse[0], d_qkv)
    down, d_out, d_out_far = after(d_qkv, down, d_out, d_out_far)
    down = add(*down)
    d_out = add(d_out[:2], d_out_far)
    (d_heads,) = after((down, d_out), d_heads)
    d_out_far = swap(d_out[1], "seq", 2)
    d_qkv = attend_back(info[1], qkv, att_heads, d_heads, lse[1], d_qkv)
    up_0, up_came, down, d_out, d_out_far = after(d_qkv, up_0, up_came, down, d_out, d_out_far)
    split = lambda a: a.reshape(*sizes, own_rows, ff // parts)
    up = halve(split(up_0), "fsdp", low, last, split(up_came))
    down_came = swap(down[1], "seq", 2)
    d_out = add(d_out[0], d_out_far)
    (d_heads,) = after((up[0], d_out), d_heads)
    d_qkv = attend_back(info[2], qkv, att_heads, d_heads, lse[2], d_qkv)

    project_back = lambda a: jnp.einsum("rcp,dc->rpd", a, wq, preferred_element_type=f32).astype(bf16)
    d_far = swap(project_back(d_qkv[2:]), "seq", 1)
    d_near = project_back(d_qkv[:2])
    d_near = add(d_near, d_far)
    d_came = swap(d_near[1], "seq", 2)
    up, down, down_came, d_qkv = after(d_near, up, down, down_came, d_qkv)
    pair = jnp.stack((add(*up), add(down[0], down_came)))
    pair = halve(pair, "fsdp", f_bits[-2], last)
    d_wq = sum(dotg(normed[r], d_qkv[r], 0, 1) for r in range(parts)).astype(bf16)
    d_wq = jnp.concatenate((d_wq, d_out), axis=1).reshape(*sizes, own_rows, width)
    d_wq = halve(d_wq, "fsdp", low, last)
    pair, d_wq = after(d_came, pair, d_wq)
    for k in reversed(range(last - 1)):
        pair = halve(pair[0], "fsdp", f_bits[k], k + 1, pair[1])
    d_wq = halve(d_wq[0], "fsdp", f_bits[-2], last - 1, d_wq[1])
    d_normed = d_near[0].astype(f32) + d_came.astype(f32)
    z_one, inverse_one = norm_stats(inputs.astype(f32))
    d_in_norm, d_gain_attn = norm_back(z_one, inverse_one, gain_one, d_normed)
    d_inputs = (d_residual + d_in_norm).astype(bf16)
    d_back = deal(d_inputs.reshape(groups, local_len, width))
    pair, d_wq = after(d_inputs, pair, d_wq)
    for k in reversed(range(last - 1)):
        d_wq = halve(d_wq[0], "fsdp", f_bits[k], k, d_wq[1])
    grads = gather(add(*pair), "seq", (2, 1)).reshape(parts, 2, own_rows, width).astype(f32)
    g_up = grads[:, 0].reshape(parts, own_rows, groups, ff_each).transpose(1, 2, 0, 3).reshape(own_rows, ff)
    g_down = grads[:, 1].reshape(ff // groups, width)

    count = table.shape[0]
    picks = (passes[None, :] == jnp.arange(count, dtype=jnp.int32)[:, None].astype(bf16)).astype(bf16)
    d_table = jnp.dot(picks, d_inputs, preferred_element_type=f32)
    small = jnp.concatenate((d_table, d_gain_attn, d_gain_mlp, jnp.zeros_like(d_gain_mlp)), axis=0)
    for bit in (1, 2):
        small = small + swap(small, "seq", bit)
    for bit in reversed(f_bits):
        small = small + swap(small, "fsdp", bit)
    owned_gain = lambda row: lax.dynamic_slice_in_dim(small[row], group * own_rows, own_rows)

    d_wq = gather(add(*d_wq), "seq", (2, 1)).reshape(parts, own_rows, width).astype(f32)
    g_out = jnp.swapaxes(d_wq[..., 3 * part :], 0, 1)
    g_qkv = d_wq[..., : 3 * part].reshape(parts, own_rows, heads, 3, DH).transpose(1, 3, 0, 2, 4)
    return (
        jnp.swapaxes(out_back, 0, 1),
        jnp.swapaxes(d_back, 0, 1),
        small[:count],
        owned_gain(count),
        g_qkv.reshape(own_rows, 3 * width),
        g_out.reshape(own_rows, width),
        owned_gain(count + 1),
        g_up,
        g_down,
    )


def solution(mesh):
    return jax.shard_map(
        per_device,
        mesh=mesh,
        in_specs=(
            P(("seq", "fsdp"), None, None),
            P(("seq", "fsdp"), None),
            P(),
            P(),
            P("fsdp"),
            P("fsdp", None),
            P("fsdp", None),
            P("fsdp"),
            P("fsdp", None),
            P("fsdp", None),
            P(("seq", "fsdp"), None, None),
        ),
        out_specs=(
            P(("seq", "fsdp"), None, None),
            P(("seq", "fsdp"), None, None),
            P(),
            P("fsdp"),
            P("fsdp", None),
            P("fsdp", None),
            P("fsdp"),
            P("fsdp", None),
            P("fsdp", None),
        ),
        check_vma=False,
    )
```

```python
import functools

import jax
import jax.numpy as jnp
from jax import lax
from jax.experimental import pallas as pl
from jax.experimental.pallas import tpu as pltpu
from jax.sharding import PartitionSpec as P

HEADS = 12
EPSILON = 1e-05
LOG2E = 1.4426950408889634
LN2 = 0.6931471805599453
MASKED = -1e30
DH = 64


def dotg(a, b, ca, cb):
    return lax.dot_general(a, b, (((ca,), (cb,)), ((), ())), preferred_element_type=jnp.float32)


def slot_of(block, info):
    return (((block & 1) << 1) | (block >> 1)) ^ info[0]


def attend_body(info, qkv, *refs, blk):
    out, lse, acc = refs[-3:]
    i = pl.program_id(0)
    length = info[1]
    qt = qkv[slot_of(i, info), 0:DH, :]
    scale = DH ** -0.5 * LOG2E

    def step(j, carry, masked):
        top, tot = carry
        kt = qkv[slot_of(j, info), DH : 2 * DH, :]
        vt = qkv[slot_of(j, info), 2 * DH : 3 * DH, :]
        st = dotg(kt, qt, 0, 0) * scale
        if masked:
            key_at = j * blk + lax.broadcasted_iota(jnp.int32, st.shape, 0)
            query_at = i * blk + lax.broadcasted_iota(jnp.int32, st.shape, 1)
            st = jnp.where((query_at >= key_at) & (key_at < length), st, MASKED)
        new_top = jnp.maximum(top, jnp.max(st, axis=0, keepdims=True))
        fade = jnp.exp2(top - new_top)
        pt = jnp.exp2(st - new_top)
        tot = tot * fade + jnp.sum(pt, axis=0, keepdims=True)
        acc[...] = acc[...] * fade + dotg(vt, pt.astype(jnp.bfloat16), 1, 0)
        return new_top, tot

    acc[...] = jnp.zeros_like(acc)
    carry = (jnp.full((1, blk), MASKED, jnp.float32), jnp.zeros((1, blk), jnp.float32))
    plain = jnp.minimum(i, length // blk)
    stop = jnp.minimum(i + 1, (length + blk - 1) // blk)
    carry = lax.fori_loop(0, plain, functools.partial(step, masked=False), carry)
    top, tot = lax.fori_loop(plain, stop, functools.partial(step, masked=True), carry)
    out[0] = (acc[...] / tot).astype(jnp.bfloat16)
    lse[0] = top + jnp.log2(tot)


def attend(info, qkv, heads, h, before=None):
    blocks, _, blk = qkv.shape
    given = () if before is None else (before,)
    return pl.pallas_call(
        functools.partial(attend_body, blk=blk),
        grid_spec=pltpu.PrefetchScalarGridSpec(
            num_scalar_prefetch=1,
            grid=(blocks,),
            in_specs=[pl.BlockSpec((blocks, 3 * DH, blk), lambda i, info: (0, info[2], 0))]
            + [pl.BlockSpec(memory_space=pl.ANY)] * len(given),
            out_specs=[
                pl.BlockSpec((1, DH, blk), lambda i, info: (slot_of(i, info), h, 0)),
                pl.BlockSpec((1, 1, blk), lambda i, info: (i, 0, 0)),
            ],
            scratch_shapes=[pltpu.VMEM((DH, blk), jnp.float32)],
        ),
        out_shape=[
            jax.ShapeDtypeStruct((blocks, heads * DH, blk), jnp.bfloat16),
            jax.ShapeDtypeStruct((blocks, 1, blk), jnp.float32),
        ],
        input_output_aliases={2: 0} if given else {},
        compiler_params=pltpu.CompilerParams(vmem_limit_bytes=16 << 20),
        cost_estimate=SMALL,
        name="attend",
    )(info, qkv, *given)


def attend_back_body(info, qkv, att, datt, lse, dqkv, dq, q_rows, do_rows, delta, *, blocks, blk):
    j = pl.program_id(0)
    length = info[1]
    scale = DH ** -0.5
    at_q, at_k, at_v = slice(0, DH), slice(DH, 2 * DH), slice(2 * DH, 3 * DH)

    @pl.when(j == 0)
    def _():
        dq[...] = jnp.zeros_like(dq)
        for b in range(blocks):
            at = slot_of(b, info)
            dt = datt[at]
            q_rows[b] = qkv[at, at_q, :].T
            do_rows[b] = dt.T
            delta[b] = jnp.sum(dt.astype(jnp.float32) * att[at].astype(jnp.float32), axis=0, keepdims=True)

    kt = qkv[slot_of(j, info), at_k, :]
    vt = qkv[slot_of(j, info), at_v, :]
    k_rows = kt.T
    v_rows = vt.T

    def step(i, carry, masked):
        dk, dv = carry
        qt = qkv[slot_of(i, info), at_q, :]
        st = jnp.dot(k_rows, qt, preferred_element_type=jnp.float32)
        pt = jnp.exp2(st * (scale * LOG2E) - lse[i])
        if masked:
            key_at = j * blk + lax.broadcasted_iota(jnp.int32, st.shape, 0)
            query_at = i * blk + lax.broadcasted_iota(jnp.int32, st.shape, 1)
            pt = jnp.where((query_at >= key_at) & (key_at < length), pt, 0.0)
        dpt = jnp.dot(v_rows, datt[slot_of(i, info)], preferred_element_type=jnp.float32)
        dst = (pt * (dpt - delta[i])).astype(jnp.bfloat16)
        dv = dv + jnp.dot(pt.astype(jnp.bfloat16), do_rows[i], preferred_element_type=jnp.float32)
        dk = dk + jnp.dot(dst, q_rows[i], preferred_element_type=jnp.float32)
        dq[i] = dq[i] + jnp.dot(kt, dst, preferred_element_type=jnp.float32)
        return dk, dv

    zero = jnp.zeros((blk, DH), jnp.float32)
    whole = (j + 1) * blk <= length
    some = j * blk < length
    masked_end = jnp.where(some, jnp.where(whole, j + 1, blocks), j)
    carry = lax.fori_loop(j, masked_end, functools.partial(step, masked=True), (zero, zero))
    dk, dv = lax.fori_loop(
        jnp.where(whole, j + 1, blocks), blocks, functools.partial(step, masked=False), carry
    )
    dqkv[slot_of(j, info), at_k, :] = (dk * scale).astype(jnp.bfloat16).T
    dqkv[slot_of(j, info), at_v, :] = dv.astype(jnp.bfloat16).T
    dqkv[slot_of(j, info), at_q, :] = (dq[j] * scale).astype(jnp.bfloat16)


def attend_back(info, qkv, att, datt, lse, at, h):
    blocks, rows, blk = qkv.shape
    third = pl.BlockSpec((blocks, 3 * DH, blk), lambda j, info: (0, info[2], 0))
    head = lambda h: pl.BlockSpec((blocks, DH, blk), lambda j, info: (0, h, 0))
    return pl.pallas_call(
        functools.partial(attend_back_body, blocks=blocks, blk=blk),
        grid_spec=pltpu.PrefetchScalarGridSpec(
            num_scalar_prefetch=1,
            grid=(blocks,),
            in_specs=[
                third,
                head(at),
                head(h),
                pl.BlockSpec((blocks, 1, blk), lambda j, info: (0, 0, 0)),
            ],
            out_specs=pl.BlockSpec((blocks, 3 * DH, blk), lambda j, info: (0, 0, 0)),
            scratch_shapes=[
                pltpu.VMEM((blocks, DH, blk), jnp.float32),
                pltpu.VMEM((blocks, blk, DH), jnp.bfloat16),
                pltpu.VMEM((blocks, blk, DH), jnp.bfloat16),
                pltpu.VMEM((blocks, 1, blk), jnp.float32),
            ],
        ),
        out_shape=jax.ShapeDtypeStruct((blocks, 3 * DH, blk), jnp.bfloat16),
        compiler_params=pltpu.CompilerParams(vmem_limit_bytes=18 << 20),
        cost_estimate=SMALL,
        name="attend_back",
    )(info, qkv, att, datt, lse)


SMALL = pl.CostEstimate(flops=1 << 20, bytes_accessed=1 << 20, transcendentals=0)
GELU_A = 0.7978845608028654
GELU_B = 0.044715


def mlp_body(nm, cot, wu, wd, *refs, begun, added):
    acc, dnm, dwu, dwd = refs[-4:]

    @pl.when(pl.program_id(0) == 0)
    def _():
        acc[...] = refs[0][...] if begun else jnp.zeros_like(acc)
        dnm[...] = refs[1][...] if begun else jnp.zeros_like(dnm)

    x = nm[...]
    g = cot[...]
    u = jnp.dot(x, wu[...], preferred_element_type=jnp.float32)
    da = dotg(g, wd[...], 1, 1)
    square = u * u
    th = jnp.tanh(GELU_A * u * (1.0 + GELU_B * square))
    half = 0.5 * (1.0 + th)
    a = (u * half).astype(jnp.bfloat16)
    slope = half + 0.5 * u * (1.0 - th * th) * (GELU_A * (1.0 + 3.0 * GELU_B * square))
    du = (da * slope).astype(jnp.bfloat16)
    acc[...] += jnp.dot(a, wd[...], preferred_element_type=jnp.float32)
    dnm[...] += dotg(du, wu[...], 1, 1)
    up = dotg(x, du, 0, 0)
    down = dotg(a, g, 0, 0)
    if added:
        up += refs[-6][...].astype(jnp.float32)
        down += refs[-5][...].astype(jnp.float32)
    dwu[...] = up.astype(jnp.bfloat16)
    dwd[...] = down.astype(jnp.bfloat16)


def mlp_part(nm, cot, wu, wd, sums=(), more=(), step=256):
    rows, width = nm.shape
    ff = wu.shape[1]
    whole = pl.BlockSpec((rows, width), lambda i: (0, 0))
    up = pl.BlockSpec((width, step), lambda i: (0, i))
    down = pl.BlockSpec((step, width), lambda i: (i, 0))
    return pl.pallas_call(
        functools.partial(mlp_body, begun=bool(sums), added=bool(more)),
        grid=(ff // step,),
        in_specs=[whole, whole, up, down] + [whole, whole][: len(sums)] + [up, down][: len(more)],
        out_specs=[whole, whole, up, down],
        out_shape=[
            jax.ShapeDtypeStruct((rows, width), jnp.float32),
            jax.ShapeDtypeStruct((rows, width), jnp.float32),
            jax.ShapeDtypeStruct(wu.shape, jnp.bfloat16),
            jax.ShapeDtypeStruct(wd.shape, jnp.bfloat16),
        ],
        input_output_aliases={4: 0, 5: 1} if sums else {},
        compiler_params=pltpu.CompilerParams(vmem_limit_bytes=26 << 20),
        cost_estimate=SMALL,
        name="mlp_part",
    )(nm, cot, wu, wd, *sums, *more)


ORDER = (0, 2, 1, 3)


def cut(array, axis, steps):
    shape = tuple(n // steps if k == axis else n for k, n in enumerate(array.shape))
    return pl.BlockSpec(shape, lambda i: tuple(i if k == axis else 0 for k in range(len(shape))))


def row_call(body, name, out_shape, place, operands, in_axes, out_axes, steps=1, scratch=()):
    return pl.pallas_call(
        body,
        grid=(steps,),
        in_specs=[pl.BlockSpec(memory_space=pltpu.SMEM)] + [cut(a, k, steps) for a, k in zip(operands, in_axes)],
        out_specs=[cut(a, k, steps) for a, k in zip(out_shape, out_axes)],
        out_shape=out_shape,
        scratch_shapes=scratch,
        compiler_params=pltpu.CompilerParams(vmem_limit_bytes=20 << 20),
        cost_estimate=SMALL,
        name=name,
    )(place, *operands)


def rows_at(place, slot, part):
    return pl.ds(pl.multiple_of((place[0] ^ ORDER[slot]) * part, DH), part)


def project_out_body(place, *refs):
    early, late, (w, inputs, gain, residual, nm) = refs[:4], refs[4:8], refs[8:]
    part = early[0].shape[0] + late[0].shape[0]
    residual[...] = inputs[...].astype(jnp.float32)
    for s in range(4):
        heads = jnp.concatenate((late[s][...], early[s][...]), axis=0)
        residual[...] += dotg(heads, w[rows_at(place, s, part), :], 0, 0)
    z, _ = norm_stats(residual[...])
    nm[...] = (z * gain[...]).astype(jnp.bfloat16)


def turn_body(place, residual, sum_near, sum_far, grad_near, grad_far, cot, gain, w, *refs):
    result, d_residual, d_branch, d_gain, d_heads = refs
    part = d_heads.shape[1]
    result[...] = (residual[...] + sum_near[...] + sum_far[...].astype(jnp.float32)).astype(jnp.bfloat16)
    z, inverse = norm_stats(residual[...])
    back, gain_part = norm_back(z, inverse, gain[...], grad_near[...] + grad_far[...].astype(jnp.float32))

    @pl.when(pl.program_id(0) == 0)
    def _():
        d_gain[...] = jnp.zeros_like(d_gain)

    d_gain[...] += gain_part
    d_residual[...] = cot[...].astype(jnp.float32) + back
    d_branch[...] = d_residual[...].astype(jnp.bfloat16)
    for s in range(4):
        d_heads[s] = dotg(w[rows_at(place, s, part), :], d_branch[...], 1, 1).astype(jnp.bfloat16)


def join_columns_body(place, *refs):
    pieces, out = refs[:4], refs[4]
    part = pieces[0].shape[1]

    def fill(me):
        for s in range(4):
            d = me ^ ORDER[s]
            out[:, d * part : (d + 1) * part] = pieces[s][...]

    for me in range(4):
        pl.when(place[0] == me)(functools.partial(fill, me))


def out_grad_body(place, *refs):
    early, late, (d_branch, near, far, out) = refs[:4], refs[4:8], refs[8:]
    part = early[0].shape[0] + late[0].shape[0]
    for s in range(4):
        heads = jnp.concatenate((late[s][...], early[s][...]), axis=0)
        out[rows_at(place, s, part), :] = jnp.dot(
            heads, d_branch[...], preferred_element_type=jnp.float32
        ).astype(jnp.bfloat16)

    def fill(me):
        for s in range(4):
            d = me ^ ORDER[s]
            (near, far)[s // 2][s % 2] = out[:, d * part : (d + 1) * part]

    for me in range(4):
        pl.when(place[0] == me)(functools.partial(fill, me))


def rows_grad_body(place, *refs):
    *heads, w, out = refs
    for s in range(out.shape[0]):
        grad = jnp.concatenate([h[s] for h in heads], axis=0)
        out[s] = dotg(grad, w[...], 0, 1).astype(jnp.bfloat16)


def weight_grad_body(place, *refs):
    normed, heads, (own, came, out) = refs[:4], refs[4:-3], refs[-3:]
    total = 0.0
    for s in range(4):
        total += dotg(normed[s][...], jnp.concatenate([h[s] for h in heads], axis=0), 0, 1)
    rest = (own[...].astype(jnp.float32) + came[...].astype(jnp.float32)).astype(jnp.bfloat16)
    out[...] = jnp.concatenate((total.astype(jnp.bfloat16), rest), axis=1)


def swap(value, axis, bit):
    count = lax.axis_size(axis)
    return lax.ppermute(value, axis, [(i, i ^ bit) for i in range(count)])


def bits_of(axis):
    count = lax.axis_size(axis)
    assert count & (count - 1) == 0, "axis size"
    return [1 << b for b in reversed(range(count.bit_length() - 1))]


def is_set(axis, bit):
    return (lax.axis_index(axis) & bit) != 0


def join(own, came, axis, bit, at):
    own, came = (jnp.expand_dims(a, at) for a in (own, came))
    shape = own.shape[:at] + (2,) + own.shape[at + 1 :]
    place = lax.broadcasted_iota(jnp.int32, shape, at)
    return jnp.where(place == is_set(axis, bit).astype(jnp.int32), own, came)


def gather(value, axis, bits, at=0):
    for k, bit in enumerate(bits):
        value = join(value, swap(value, axis, bit), axis, bit, at + k)
    return value


def spread(blocks, bit):
    return blocks | {r ^ bit: swap(b, "seq", bit) for r, b in blocks.items()}


def add(a, b):
    return (a.astype(jnp.float32) + b.astype(jnp.float32)).astype(a.dtype)


def fold(blocks, bit):
    return {r: add(b, swap(blocks[r ^ bit], "seq", bit)) for r, b in blocks.items() if not r & bit}


def halve(value, axis, bit, at, *more):
    mine = is_set(axis, bit).astype(jnp.int32)
    part = lambda which: functools.reduce(
        add, [lax.dynamic_index_in_dim(v, which, at, keepdims=False) for v in (value, *more)]
    )
    return part(mine), swap(part(1 - mine), axis, bit)


def norm_stats(values):
    centre = jnp.mean(values, axis=-1, keepdims=True)
    shifted = values - centre
    spread_of = jnp.mean(shifted * shifted, axis=-1, keepdims=True)
    inverse = lax.rsqrt(spread_of + EPSILON)
    return shifted * inverse, inverse


def norm_back(z, inverse, gain, grad):
    e = grad * gain
    back = (e - jnp.mean(e, axis=-1, keepdims=True) - z * jnp.mean(e * z, axis=-1, keepdims=True)) * inverse
    return back, jnp.sum(grad * z, axis=0, keepdims=True)


def pick_at(value, at):
    return lax.dynamic_index_in_dim(value, at, 1, keepdims=False)


def after(first, *values):
    return lax.optimization_barrier((first, values))[1]


def per_device(
    tokens, pass_index, lengths, table, gain_attn, w_qkv, w_out, gain_mlp, w_up, w_down, cotangent
):
    bf16, f32 = jnp.bfloat16, jnp.float32
    groups, parts = lax.axis_size("fsdp"), lax.axis_size("seq")
    local_len, seq_total, width = tokens.shape
    assert seq_total == groups and parts == 4
    heads = HEADS // parts
    part = width // parts
    ff = w_up.shape[1]
    own_rows = width // groups
    ff_each = ff // groups // parts
    me, group = lax.axis_index("seq"), lax.axis_index("fsdp")
    f_bits = bits_of("fsdp")
    last = len(f_bits) - 1
    top, low, between = f_bits[0], f_bits[-1], f_bits[1:-1]
    sizes = (2,) * len(f_bits)
    span = local_len * groups
    pick = lambda a, at: lax.dynamic_index_in_dim(a, me, at, keepdims=False)
    deal = lambda a: lax.all_to_all(a, "fsdp", split_axis=0, concat_axis=0, tiled=True)
    across = lambda a: [a[0]] + [swap(a[s], "seq", r) for s, r in enumerate(ORDER) if r]

    chooser = (pass_index[..., None] == jnp.arange(table.shape[0], dtype=jnp.int32)).astype(bf16)
    embedded = jnp.einsum("pnc,cd->npd", chooser, table, preferred_element_type=f32)
    summed = (jnp.swapaxes(tokens, 0, 1).astype(f32) + embedded).astype(bf16)
    inputs = deal(summed).reshape(span, width)
    qkv_slice = pick(w_qkv.reshape(own_rows, 3, parts, heads, DH), 2)
    qkv_slice = jnp.swapaxes(qkv_slice, 1, 2).reshape(own_rows, 3 * part)
    out_slice = pick(w_out.reshape(own_rows, parts, part), 1)
    gains = jnp.stack((gain_attn, gain_mlp), axis=1)
    qkv_slice, out_slice = after(summed, qkv_slice, out_slice)
    packet = jnp.concatenate((qkv_slice, out_slice, gains, jnp.zeros((own_rows, 126), bf16)), axis=1)
    packet_came = swap(packet, "fsdp", top)
    up = pick(w_up.reshape(own_rows, groups, parts, ff_each), 2).reshape(own_rows, ff // parts)
    down = pick(w_down.reshape(parts, ff_each, width), 0)
    pair = jnp.stack((up, down))

    rows_2, rows_1 = swap(inputs, "seq", 2), swap(inputs, "seq", 1)
    rows = (inputs, rows_2, rows_1, swap(rows_2, "seq", 1))
    packet, packet_came, pair = after(inputs, packet, packet_came, pair)
    packet = gather(join(packet, packet_came, "fsdp", top, 0), "fsdp", between, 1)
    packet, pair = lax.optimization_barrier((packet, pair))
    packet = gather(packet, "fsdp", (low,), last).reshape(width, -1)
    wq = packet[:, : 3 * part]
    out_cols = packet[:, 3 * part : width]
    gain_one = packet[:, width].astype(f32)
    gain_two = packet[:, width + 1].astype(f32)
    pair_came = swap(pair, "fsdp", top)
    marks = jnp.swapaxes(pass_index, 0, 1)[..., None].astype(bf16)
    cot_packet = jnp.concatenate(
        (jnp.swapaxes(cotangent, 0, 1), jnp.broadcast_to(marks, marks.shape[:2] + (128,))), axis=2
    )

    normed = [(norm_stats(b.astype(f32))[0] * gain_one).astype(bf16) for b in rows]
    pair, pair_came, out_cols = after(rows[3], pair, pair_came, out_cols)
    pair = join(pair, pair_came, "fsdp", top, 1)
    pair = gather(pair, "fsdp", between, 2)
    out_2 = swap(out_cols, "seq", 2)
    qkv = jnp.stack([dotg(wq, b, 0, 1).astype(bf16) for b in normed])
    length = lax.dynamic_index_in_dim(lengths, group, 0, keepdims=False)
    slot = (me & 1) * 2 + (me >> 1)
    info = [jnp.stack((slot, length, jnp.int32(h))).astype(jnp.int32) for h in range(heads)]

    lse, many = [None] * heads, heads - 1
    att, lse[1] = attend(info[1], qkv, many, 0)
    pair, out_cols, out_2, cot_packet = after(att, pair, out_cols, out_2, cot_packet)
    up, down = pair[0], pair[1]
    (qkv,) = after((up, down), qkv)
    cot_packet = deal(cot_packet).reshape(span, -1)
    up_came = swap(up, "fsdp", low)
    down_2 = swap(down, "seq", 2)
    out_1, out_3 = swap(out_cols, "seq", 1), swap(out_2, "seq", 1)
    for h in range(2, heads):
        att, lse[h] = attend(info[h], qkv, many, h - 1, att)
    att, out_1, out_3, down = lax.optimization_barrier((att, out_1, out_3, down))
    place = me.astype(jnp.int32)[None]
    square = jax.ShapeDtypeStruct((width, width), bf16)
    (w_out_full,) = row_call(
        join_columns_body, "join_columns", [square], place, [out_cols, out_2, out_1, out_3], [None] * 4, [None]
    )
    (qkv,) = after((att, w_out_full), qkv)
    att_early = across(att)
    down_came = swap(down, "fsdp", low)
    att_lone, lse[0] = attend(info[0], qkv, 1, 0)
    up, up_came, down_2, att_lone, att_early = lax.optimization_barrier((up, up_came, down_2, att_lone, att_early))
    att_late = across(att_lone)
    up = join(up, up_came, "fsdp", low, last).reshape(width, ff // parts)

    att_late, up, down, down_came, down_2, cot_packet = lax.optimization_barrier(
        (att_late, up, down, down_came, down_2, cot_packet)
    )
    up_2 = swap(up, "seq", 2)
    cot = cot_packet[:, :width]
    passes = cot_packet[:, width]
    cot_far = swap(cot, "seq", 1)
    down_2_came = swap(down_2, "fsdp", low)
    down = join(down, down_came, "fsdp", low, last).reshape(ff // parts, width)
    rows_f32 = jax.ShapeDtypeStruct((span, width), f32)
    rows_bf16 = jax.ShapeDtypeStruct((span, width), bf16)
    residual, nm = row_call(
        project_out_body, "project_out", [rows_f32, rows_bf16], place,
        [*att_early, *att_late, w_out_full, inputs, gain_two[None]], [1] * 8 + [None, 0, None], [0, 0], parts,
    )
    nm_far = swap(nm, "seq", 1)
    *near, up_0, down_0 = mlp_part(nm, cot, up, down)
    *far, up_0, down_0 = mlp_part(nm_far, cot_far, up, down, (), (up_0, down_0))
    down_2, down_2_came, up_2 = after(far[0], down_2, down_2_came, up_2)
    down_2 = join(down_2, down_2_came, "fsdp", low, last).reshape(ff // parts, width)
    *far, d_up_2, d_down_2 = mlp_part(nm_far, cot_far, up_2, down_2, far)
    far = [swap(a.astype(bf16), "seq", 1) for a in far]
    *near, up_2, down_2 = mlp_part(nm, cot, up_2, down_2, near, (d_up_2, d_down_2))
    down = jnp.stack((down_0, down_2)).reshape(2, *sizes, ff_each, width)
    down = halve(down, "fsdp", low, last + 1)
    head_rows = jax.ShapeDtypeStruct((parts, part, span), bf16)
    result, d_residual, d_branch, d_gain_mlp, d_heads = row_call(
        turn_body,
        "turn",
        [rows_bf16, rows_f32, rows_bf16, jax.ShapeDtypeStruct((1, width), f32), head_rows],
        place,
        [residual, near[0], far[0], near[1], far[1], cot, gain_two[None], w_out_full],
        [0] * 6 + [None] * 2,
        [0, 0, 0, None, 2],
        parts,
    )
    d_heads = jnp.stack(across(d_heads))
    halves = jax.ShapeDtypeStruct((2, width, part), bf16)
    d_out, d_out_far = row_call(
        out_grad_body, "out_grad", [halves, halves], place, [*att_early, *att_late, d_branch], [None] * 9, [None] * 2,
        scratch=[pltpu.VMEM((width, width), bf16)],
    )
    d_heads, d_out, d_out_far, up_0, up_2, result = lax.optimization_barrier(
        (d_heads, d_out, d_out_far, up_0, up_2, result)
    )

    up_came = swap(up_2, "seq", 2)
    out_back = deal(result.reshape(groups, local_len, width))
    d_out_far = swap(d_out_far, "seq", 1)
    d_qkv = [attend_back(info[0], qkv, att_lone, d_heads, lse[0], 0, 0)]
    down, d_out, d_out_far = after(d_qkv, down, d_out, d_out_far)
    down = halve(down[0], "fsdp", f_bits[-2], last, down[1])
    d_out = add(d_out, d_out_far)
    (d_heads,) = after((down[0], d_out), d_heads)
    d_out_far = swap(d_out[1], "seq", 2)
    for h in range(1, many):
        d_qkv.append(attend_back(info[h], qkv, att, d_heads, lse[h], h - 1, h))
    up_0, up_came, down, d_out, d_out_far, out_back = after(d_qkv, up_0, up_came, down, d_out, d_out_far, out_back)
    split = lambda a: a.reshape(*sizes, own_rows, ff // parts)
    up = halve(split(up_0), "fsdp", low, last, split(up_came))
    for k in reversed(range(last - 1)):
        down = halve(down[0], "fsdp", f_bits[k], k + 1, down[1])
    d_out = d_out[0]
    (d_heads,) = after((up[0], down[0], out_back), d_heads)
    d_qkv.append(attend_back(info[many], qkv, att, d_heads, lse[many], many - 1, many))
    d_qkv, down, up = lax.optimization_barrier((d_qkv, down, up))

    half = jax.ShapeDtypeStruct((2, span, width), bf16)
    project_back = lambda a: row_call(rows_grad_body, "rows_grad", [half], place, [*a, wq], [None] * (heads + 1), [None])[0]
    d_far = swap(project_back([d[2:] for d in d_qkv]), "seq", 1)
    d_near = project_back([d[:2] for d in d_qkv])
    (d_tail,) = after(d_near, d_qkv)
    down = add(*down)
    down_came = swap(down[1], "seq", 2)
    up = halve(up[0], "fsdp", f_bits[-2], last - 1, up[1])
    (d_wq,) = row_call(
        weight_grad_body, "weight_grad", [square], place, [*normed, *d_tail, d_out, d_out_far],
        [None] * (6 + heads), [None],
    )
    d_near, d_wq = lax.optimization_barrier((d_near, d_wq))
    d_wq = halve(d_wq.reshape(*sizes, own_rows, width), "fsdp", low, last)
    d_near = add(d_near, d_far)
    d_came = swap(d_near[1], "seq", 2)
    up, down_came = after(d_near, up, down_came)
    for k in reversed(range(last - 1)):
        up = halve(up[0], "fsdp", f_bits[k], k, up[1])
    d_wq = halve(d_wq[0], "fsdp", f_bits[-2], last - 1, d_wq[1])
    up, d_wq = after(d_came, up, d_wq)
    for k in reversed(range(last - 1)):
        d_wq = halve(d_wq[0], "fsdp", f_bits[k], k, d_wq[1])
    d_normed = d_near[0].astype(f32) + d_came.astype(f32)
    z_one, inverse_one = norm_stats(inputs.astype(f32))
    d_in_norm, d_gain_attn = norm_back(z_one, inverse_one, gain_one, d_normed)
    d_inputs = (d_residual + d_in_norm).astype(bf16)
    d_back = deal(d_inputs.reshape(groups, local_len, width))
    up, down, down_came = after(d_inputs, up, down, down_came)
    (d_wq,) = after(d_back, d_wq)
    pair = jnp.stack((add(*up), add(down[0], down_came)))
    grads = gather(pair, "seq", (2, 1)).reshape(parts, 2, own_rows, width).astype(f32)
    g_up = grads[:, 0].reshape(parts, own_rows, groups, ff_each).transpose(1, 2, 0, 3).reshape(own_rows, ff)
    g_down = grads[:, 1].reshape(ff // groups, width)

    count = table.shape[0]
    picks = (passes[None, :] == jnp.arange(count, dtype=jnp.int32)[:, None].astype(bf16)).astype(bf16)
    d_table = jnp.dot(picks, d_inputs, preferred_element_type=f32)
    small = jnp.concatenate((d_table, d_gain_attn, d_gain_mlp, jnp.zeros_like(d_gain_mlp)), axis=0)
    for bit in (1, 2):
        small = small + swap(small, "seq", bit)
    small = small + swap(small, "fsdp", low)
    (small,) = after(d_back, small)
    for bit in reversed(f_bits[:-1]):
        small = small + swap(small, "fsdp", bit)
    owned_gain = lambda row: lax.dynamic_slice_in_dim(small[row], group * own_rows, own_rows)

    d_wq = gather(add(*d_wq), "seq", (2, 1)).reshape(parts, own_rows, width).astype(f32)
    g_out = jnp.swapaxes(d_wq[..., 3 * part :], 0, 1)
    g_qkv = d_wq[..., : 3 * part].reshape(parts, own_rows, heads, 3, DH).transpose(1, 3, 0, 2, 4)
    return (
        jnp.swapaxes(out_back, 0, 1),
        jnp.swapaxes(d_back, 0, 1),
        small[:count],
        owned_gain(count),
        g_qkv.reshape(own_rows, 3 * width),
        g_out.reshape(own_rows, width),
        owned_gain(count + 1),
        g_up,
        g_down,
    )


def solution(mesh):
    return jax.shard_map(
        per_device,
        mesh=mesh,
        in_specs=(
            P(("seq", "fsdp"), None, None),
            P(("seq", "fsdp"), None),
            P(),
            P(),
            P("fsdp"),
            P("fsdp", None),
            P("fsdp", None),
            P("fsdp"),
            P("fsdp", None),
            P("fsdp", None),
            P(("seq", "fsdp"), None, None),
        ),
        out_specs=(
            P(("seq", "fsdp"), None, None),
            P(("seq", "fsdp"), None, None),
            P(),
            P("fsdp"),
            P("fsdp", None),
            P("fsdp", None),
            P("fsdp"),
            P("fsdp", None),
            P("fsdp", None),
        ),
        check_vma=False,
    )
```

```python
import functools

import jax
import jax.numpy as jnp
from jax import lax
from jax.experimental import pallas as pl
from jax.experimental.pallas import tpu as pltpu
from jax.sharding import PartitionSpec as P

HEADS = 12
EPSILON = 1e-05
LOG2E = 1.4426950408889634
LN2 = 0.6931471805599453
MASKED = -1e30
DH = 64


def dotg(a, b, ca, cb):
    return lax.dot_general(a, b, (((ca,), (cb,)), ((), ())), preferred_element_type=jnp.float32)


def slot_of(block, info):
    return (((block & 1) << 1) | (block >> 1)) ^ info[0]


def attend_body(info, qkv, *refs, blk):
    out, lse, acc = refs[-3:]
    i = pl.program_id(0)
    length = info[1]
    qt = qkv[slot_of(i, info), 0:DH, :]
    scale = DH ** -0.5 * LOG2E

    def step(j, carry, masked):
        top, tot = carry
        kt = qkv[slot_of(j, info), DH : 2 * DH, :]
        vt = qkv[slot_of(j, info), 2 * DH : 3 * DH, :]
        st = dotg(kt, qt, 0, 0) * scale
        if masked:
            key_at = j * blk + lax.broadcasted_iota(jnp.int32, st.shape, 0)
            query_at = i * blk + lax.broadcasted_iota(jnp.int32, st.shape, 1)
            st = jnp.where((query_at >= key_at) & (key_at < length), st, MASKED)
        new_top = jnp.maximum(top, jnp.max(st, axis=0, keepdims=True))
        fade = jnp.exp2(top - new_top)
        pt = jnp.exp2(st - new_top)
        tot = tot * fade + jnp.sum(pt, axis=0, keepdims=True)
        acc[...] = acc[...] * fade + dotg(vt, pt.astype(jnp.bfloat16), 1, 0)
        return new_top, tot

    acc[...] = jnp.zeros_like(acc)
    carry = (jnp.full((1, blk), MASKED, jnp.float32), jnp.zeros((1, blk), jnp.float32))
    plain = jnp.minimum(i, length // blk)
    stop = jnp.minimum(i + 1, (length + blk - 1) // blk)
    carry = lax.fori_loop(0, plain, functools.partial(step, masked=False), carry)
    top, tot = lax.fori_loop(plain, stop, functools.partial(step, masked=True), carry)
    out[0] = (acc[...] / tot).astype(jnp.bfloat16)
    lse[0] = top + jnp.log2(tot)


def attend(info, qkv, heads, h, before=None):
    blocks, _, blk = qkv.shape
    given = () if before is None else (before,)
    return pl.pallas_call(
        functools.partial(attend_body, blk=blk),
        grid_spec=pltpu.PrefetchScalarGridSpec(
            num_scalar_prefetch=1,
            grid=(blocks,),
            in_specs=[pl.BlockSpec((blocks, 3 * DH, blk), lambda i, info: (0, info[2], 0))]
            + [pl.BlockSpec(memory_space=pl.ANY)] * len(given),
            out_specs=[
                pl.BlockSpec((1, DH, blk), lambda i, info: (slot_of(i, info), h, 0)),
                pl.BlockSpec((1, 1, blk), lambda i, info: (i, 0, 0)),
            ],
            scratch_shapes=[pltpu.VMEM((DH, blk), jnp.float32)],
        ),
        out_shape=[
            jax.ShapeDtypeStruct((blocks, heads * DH, blk), jnp.bfloat16),
            jax.ShapeDtypeStruct((blocks, 1, blk), jnp.float32),
        ],
        input_output_aliases={2: 0} if given else {},
        compiler_params=pltpu.CompilerParams(vmem_limit_bytes=16 << 20),
        cost_estimate=SMALL,
        name="attend",
    )(info, qkv, *given)


def attend_back_body(info, qkv, att, *refs, blocks, blk):
    came, (lse, dqkv, dq, q_rows, do_rows, delta, datt) = refs[:blocks], refs[blocks:]
    j = pl.program_id(0)
    length = info[1]
    scale = DH ** -0.5
    at_q, at_k, at_v = slice(0, DH), slice(DH, 2 * DH), slice(2 * DH, 3 * DH)

    @pl.when(j == 0)
    def _():
        dq[...] = jnp.zeros_like(dq)
        for b in range(blocks):
            datt[b] = came[b][...]
        for b in range(blocks):
            at = slot_of(b, info)
            dt = datt[at]
            q_rows[b] = qkv[at, at_q, :].T
            do_rows[b] = dt.T
            delta[b] = jnp.sum(dt.astype(jnp.float32) * att[at].astype(jnp.float32), axis=0, keepdims=True)

    kt = qkv[slot_of(j, info), at_k, :]
    vt = qkv[slot_of(j, info), at_v, :]
    k_rows = kt.T
    v_rows = vt.T

    def step(i, carry, masked):
        dk, dv = carry
        qt = qkv[slot_of(i, info), at_q, :]
        st = jnp.dot(k_rows, qt, preferred_element_type=jnp.float32)
        pt = jnp.exp2(st * (scale * LOG2E) - lse[i])
        if masked:
            key_at = j * blk + lax.broadcasted_iota(jnp.int32, st.shape, 0)
            query_at = i * blk + lax.broadcasted_iota(jnp.int32, st.shape, 1)
            pt = jnp.where((query_at >= key_at) & (key_at < length), pt, 0.0)
        dpt = jnp.dot(v_rows, datt[slot_of(i, info)], preferred_element_type=jnp.float32)
        dst = (pt * (dpt - delta[i])).astype(jnp.bfloat16)
        dv = dv + jnp.dot(pt.astype(jnp.bfloat16), do_rows[i], preferred_element_type=jnp.float32)
        dk = dk + jnp.dot(dst, q_rows[i], preferred_element_type=jnp.float32)
        dq[i] = dq[i] + jnp.dot(kt, dst, preferred_element_type=jnp.float32)
        return dk, dv

    zero = jnp.zeros((blk, DH), jnp.float32)
    whole = (j + 1) * blk <= length
    some = j * blk < length
    masked_end = jnp.where(some, jnp.where(whole, j + 1, blocks), j)
    carry = lax.fori_loop(j, masked_end, functools.partial(step, masked=True), (zero, zero))
    dk, dv = lax.fori_loop(
        jnp.where(whole, j + 1, blocks), blocks, functools.partial(step, masked=False), carry
    )
    dqkv[slot_of(j, info), at_k, :] = (dk * scale).astype(jnp.bfloat16).T
    dqkv[slot_of(j, info), at_v, :] = dv.astype(jnp.bfloat16).T
    dqkv[slot_of(j, info), at_q, :] = (dq[j] * scale).astype(jnp.bfloat16)


def attend_back(info, qkv, att, datt, lse, at, h):
    blocks, rows, blk = qkv.shape
    third = pl.BlockSpec((blocks, 3 * DH, blk), lambda j, info: (0, info[2], 0))
    head = lambda h: pl.BlockSpec((blocks, DH, blk), lambda j, info: (0, h, 0))
    return pl.pallas_call(
        functools.partial(attend_back_body, blocks=blocks, blk=blk),
        grid_spec=pltpu.PrefetchScalarGridSpec(
            num_scalar_prefetch=1,
            grid=(blocks,),
            in_specs=[
                third,
                head(at),
                *[pl.BlockSpec((DH, blk), lambda j, info: (h, 0))] * blocks,
                pl.BlockSpec((blocks, 1, blk), lambda j, info: (0, 0, 0)),
            ],
            out_specs=pl.BlockSpec((blocks, 3 * DH, blk), lambda j, info: (0, 0, 0)),
            scratch_shapes=[
                pltpu.VMEM((blocks, DH, blk), jnp.float32),
                pltpu.VMEM((blocks, blk, DH), jnp.bfloat16),
                pltpu.VMEM((blocks, blk, DH), jnp.bfloat16),
                pltpu.VMEM((blocks, 1, blk), jnp.float32),
                pltpu.VMEM((blocks, DH, blk), jnp.bfloat16),
            ],
        ),
        out_shape=jax.ShapeDtypeStruct((blocks, 3 * DH, blk), jnp.bfloat16),
        compiler_params=pltpu.CompilerParams(vmem_limit_bytes=18 << 20),
        cost_estimate=SMALL,
        name="attend_back",
    )(info, qkv, att, *datt, lse)


SMALL = pl.CostEstimate(flops=1 << 20, bytes_accessed=1 << 20, transcendentals=0)
GELU_A = 0.7978845608028654
GELU_B = 0.044715


def mlp_body(nm, cot, wu, wd, *refs, begun, added):
    acc, dnm, dwu, dwd = refs[-4:]

    @pl.when(pl.program_id(0) == 0)
    def _():
        acc[...] = refs[0][...] if begun else jnp.zeros_like(acc)
        dnm[...] = refs[1][...] if begun else jnp.zeros_like(dnm)

    x = nm[...]
    g = cot[...]
    u = jnp.dot(x, wu[...], preferred_element_type=jnp.float32)
    da = dotg(g, wd[...], 1, 1)
    square = u * u
    th = jnp.tanh(GELU_A * u * (1.0 + GELU_B * square))
    half = 0.5 * (1.0 + th)
    a = (u * half).astype(jnp.bfloat16)
    slope = half + 0.5 * u * (1.0 - th * th) * (GELU_A * (1.0 + 3.0 * GELU_B * square))
    du = (da * slope).astype(jnp.bfloat16)
    acc[...] += jnp.dot(a, wd[...], preferred_element_type=jnp.float32)
    dnm[...] += dotg(du, wu[...], 1, 1)
    up = dotg(x, du, 0, 0)
    down = dotg(a, g, 0, 0)
    if added:
        up += refs[-6][...].astype(jnp.float32)
        down += refs[-5][...].astype(jnp.float32)
    dwu[...] = up.astype(jnp.bfloat16)
    dwd[...] = down.astype(jnp.bfloat16)


def mlp_part(nm, cot, wu, wd, sums=(), more=(), step=256):
    rows, width = nm.shape
    ff = wu.shape[1]
    whole = pl.BlockSpec((rows, width), lambda i: (0, 0))
    up = pl.BlockSpec((width, step), lambda i: (0, i))
    down = pl.BlockSpec((step, width), lambda i: (i, 0))
    return pl.pallas_call(
        functools.partial(mlp_body, begun=bool(sums), added=bool(more)),
        grid=(ff // step,),
        in_specs=[whole, whole, up, down] + [whole, whole][: len(sums)] + [up, down][: len(more)],
        out_specs=[whole, whole, up, down],
        out_shape=[
            jax.ShapeDtypeStruct((rows, width), jnp.float32),
            jax.ShapeDtypeStruct((rows, width), jnp.float32),
            jax.ShapeDtypeStruct(wu.shape, jnp.bfloat16),
            jax.ShapeDtypeStruct(wd.shape, jnp.bfloat16),
        ],
        input_output_aliases={4: 0, 5: 1} if sums else {},
        compiler_params=pltpu.CompilerParams(vmem_limit_bytes=26 << 20),
        cost_estimate=SMALL,
        name="mlp_part",
    )(nm, cot, wu, wd, *sums, *more)


ORDER = (0, 2, 1, 3)


def cut(array, axis, steps):
    shape = tuple(n // steps if k == axis else n for k, n in enumerate(array.shape))
    return pl.BlockSpec(shape, lambda i: tuple(i if k == axis else 0 for k in range(len(shape))))


def row_call(body, name, out_shape, place, operands, in_axes, out_axes, steps=1, scratch=()):
    return pl.pallas_call(
        body,
        grid=(steps,),
        in_specs=[pl.BlockSpec(memory_space=pltpu.SMEM)] + [cut(a, k, steps) for a, k in zip(operands, in_axes)],
        out_specs=[cut(a, k, steps) for a, k in zip(out_shape, out_axes)],
        out_shape=out_shape,
        scratch_shapes=scratch,
        compiler_params=pltpu.CompilerParams(vmem_limit_bytes=20 << 20),
        cost_estimate=SMALL,
        name=name,
    )(place, *operands)


def rows_at(place, slot, part):
    return pl.ds(pl.multiple_of((place[0] ^ ORDER[slot]) * part, DH), part)


def project_out_body(place, *refs):
    early, late, (w, inputs, gain, residual, nm) = refs[:4], refs[4:8], refs[8:]
    part = early[0].shape[0] + late[0].shape[0]
    residual[...] = inputs[...].astype(jnp.float32)
    for s in range(4):
        heads = jnp.concatenate((late[s][...], early[s][...]), axis=0)
        residual[...] += dotg(heads, w[rows_at(place, s, part), :], 0, 0)
    z, _ = norm_stats(residual[...])
    nm[...] = (z * gain[...]).astype(jnp.bfloat16)


def turn_body(place, residual, sum_near, sum_far, grad_near, grad_far, cot, gain, w, *refs):
    result, d_residual, d_branch, d_gain, d_heads = refs
    part = d_heads.shape[1]
    result[...] = (residual[...] + sum_near[...] + sum_far[...].astype(jnp.float32)).astype(jnp.bfloat16)
    z, inverse = norm_stats(residual[...])
    back, gain_part = norm_back(z, inverse, gain[...], grad_near[...] + grad_far[...].astype(jnp.float32))

    @pl.when(pl.program_id(0) == 0)
    def _():
        d_gain[...] = jnp.zeros_like(d_gain)

    d_gain[...] += gain_part
    d_residual[...] = cot[...].astype(jnp.float32) + back
    d_branch[...] = d_residual[...].astype(jnp.bfloat16)
    for s in range(4):
        d_heads[s] = dotg(w[rows_at(place, s, part), :], d_branch[...], 1, 1).astype(jnp.bfloat16)


def join_columns_body(place, *refs):
    pieces, out = refs[:4], refs[4]
    part = pieces[0].shape[1]

    def fill(me):
        for s in range(4):
            d = me ^ ORDER[s]
            out[:, d * part : (d + 1) * part] = pieces[s][...]

    for me in range(4):
        pl.when(place[0] == me)(functools.partial(fill, me))


def out_grad_body(place, *refs):
    early, late, (d_branch, *pieces, out) = refs[:4], refs[4:8], refs[8:]
    part = early[0].shape[0] + late[0].shape[0]
    for s in range(4):
        heads = jnp.concatenate((late[s][...], early[s][...]), axis=0)
        out[rows_at(place, s, part), :] = jnp.dot(
            heads, d_branch[...], preferred_element_type=jnp.float32
        ).astype(jnp.bfloat16)

    def fill(me):
        for s in range(4):
            d = me ^ ORDER[s]
            pieces[s][...] = out[:, d * part : (d + 1) * part]

    for me in range(4):
        pl.when(place[0] == me)(functools.partial(fill, me))


def rows_grad_body(place, *refs):
    *heads, w, out = refs
    for s in range(out.shape[0]):
        grad = jnp.concatenate([h[s] for h in heads], axis=0)
        out[s] = dotg(grad, w[...], 0, 1).astype(jnp.bfloat16)


def weight_grad_body(place, *refs):
    normed, heads, (*parts, out) = refs[:4], refs[4:-4], refs[-4:]
    total = 0.0
    for s in range(4):
        total += dotg(normed[s][...], jnp.concatenate([h[s] for h in heads], axis=0), 0, 1)
    rest = sum(p[...].astype(jnp.float32) for p in parts).astype(jnp.bfloat16)
    out[...] = jnp.concatenate((total.astype(jnp.bfloat16), rest), axis=1)


def swap(value, axis, bit):
    count = lax.axis_size(axis)
    return lax.ppermute(value, axis, [(i, i ^ bit) for i in range(count)])


def bits_of(axis):
    count = lax.axis_size(axis)
    assert count & (count - 1) == 0, "axis size"
    return [1 << b for b in reversed(range(count.bit_length() - 1))]


def is_set(axis, bit):
    return (lax.axis_index(axis) & bit) != 0


def join(own, came, axis, bit, at):
    own, came = (jnp.expand_dims(a, at) for a in (own, came))
    shape = own.shape[:at] + (2,) + own.shape[at + 1 :]
    place = lax.broadcasted_iota(jnp.int32, shape, at)
    return jnp.where(place == is_set(axis, bit).astype(jnp.int32), own, came)


def gather(value, axis, bits, at=0):
    for k, bit in enumerate(bits):
        value = join(value, swap(value, axis, bit), axis, bit, at + k)
    return value


def spread(blocks, bit):
    return blocks | {r ^ bit: swap(b, "seq", bit) for r, b in blocks.items()}


def add(a, b):
    return (a.astype(jnp.float32) + b.astype(jnp.float32)).astype(a.dtype)


def fold(blocks, bit):
    return {r: add(b, swap(blocks[r ^ bit], "seq", bit)) for r, b in blocks.items() if not r & bit}


def halve(value, axis, bit, at, *more):
    mine = is_set(axis, bit).astype(jnp.int32)
    part = lambda which: functools.reduce(
        add, [lax.dynamic_index_in_dim(v, which, at, keepdims=False) for v in (value, *more)]
    )
    return part(mine), swap(part(1 - mine), axis, bit)


def norm_stats(values):
    centre = jnp.mean(values, axis=-1, keepdims=True)
    shifted = values - centre
    spread_of = jnp.mean(shifted * shifted, axis=-1, keepdims=True)
    inverse = lax.rsqrt(spread_of + EPSILON)
    return shifted * inverse, inverse


def norm_back(z, inverse, gain, grad):
    e = grad * gain
    back = (e - jnp.mean(e, axis=-1, keepdims=True) - z * jnp.mean(e * z, axis=-1, keepdims=True)) * inverse
    return back, jnp.sum(grad * z, axis=0, keepdims=True)


def pick_at(value, at):
    return lax.dynamic_index_in_dim(value, at, 1, keepdims=False)


def after(first, *values):
    return lax.optimization_barrier((first, values))[1]


def per_device(
    tokens, pass_index, lengths, table, gain_attn, w_qkv, w_out, gain_mlp, w_up, w_down, cotangent
):
    bf16, f32 = jnp.bfloat16, jnp.float32
    groups, parts = lax.axis_size("fsdp"), lax.axis_size("seq")
    local_len, seq_total, width = tokens.shape
    assert seq_total == groups and parts == 4
    heads = HEADS // parts
    part = width // parts
    ff = w_up.shape[1]
    own_rows = width // groups
    ff_each = ff // groups // parts
    me, group = lax.axis_index("seq"), lax.axis_index("fsdp")
    f_bits = bits_of("fsdp")
    last = len(f_bits) - 1
    top, low, between = f_bits[0], f_bits[-1], f_bits[1:-1]
    sizes = (2,) * len(f_bits)
    span = local_len * groups
    pick = lambda a, at: lax.dynamic_index_in_dim(a, me, at, keepdims=False)
    deal = lambda a: lax.all_to_all(a, "fsdp", split_axis=0, concat_axis=0, tiled=True)
    across = lambda a: [a[0]] + [swap(a[s], "seq", r) for s, r in enumerate(ORDER) if r]

    chooser = (pass_index[..., None] == jnp.arange(table.shape[0], dtype=jnp.int32)).astype(bf16)
    embedded = jnp.einsum("pnc,cd->npd", chooser, table, preferred_element_type=f32)
    summed = (jnp.swapaxes(tokens, 0, 1).astype(f32) + embedded).astype(bf16)
    inputs = deal(summed).reshape(span, width)
    qkv_slice = pick(w_qkv.reshape(own_rows, 3, parts, heads, DH), 2)
    qkv_slice = jnp.swapaxes(qkv_slice, 1, 2).reshape(own_rows, 3 * part)
    out_slice = pick(w_out.reshape(own_rows, parts, part), 1)
    gains = jnp.stack((gain_attn, gain_mlp), axis=1)
    qkv_slice, out_slice = after(summed, qkv_slice, out_slice)
    packet = jnp.concatenate((qkv_slice, out_slice, gains, jnp.zeros((own_rows, 126), bf16)), axis=1)
    packet_came = swap(packet, "fsdp", top)
    up = pick(w_up.reshape(own_rows, groups, parts, ff_each), 2).reshape(own_rows, ff // parts)
    down = pick(w_down.reshape(parts, ff_each, width), 0)
    pair = jnp.stack((up, down))

    rows_2, rows_1 = swap(inputs, "seq", 2), swap(inputs, "seq", 1)
    rows = (inputs, rows_2, rows_1, swap(rows_2, "seq", 1))
    packet, packet_came, pair = after(inputs, packet, packet_came, pair)
    packet = gather(join(packet, packet_came, "fsdp", top, 0), "fsdp", between, 1)
    packet, pair = lax.optimization_barrier((packet, pair))
    packet = gather(packet, "fsdp", (low,), last).reshape(width, -1)
    wq = packet[:, : 3 * part]
    out_cols = packet[:, 3 * part : width]
    gain_one = packet[:, width].astype(f32)
    gain_two = packet[:, width + 1].astype(f32)
    pair_came = swap(pair, "fsdp", top)
    marks = jnp.swapaxes(pass_index, 0, 1)[..., None].astype(bf16)
    cot_packet = jnp.concatenate(
        (jnp.swapaxes(cotangent, 0, 1), jnp.broadcast_to(marks, marks.shape[:2] + (128,))), axis=2
    )

    normed = [(norm_stats(b.astype(f32))[0] * gain_one).astype(bf16) for b in rows]
    pair, pair_came, out_cols = after(rows[3], pair, pair_came, out_cols)
    pair = join(pair, pair_came, "fsdp", top, 1)
    pair = gather(pair, "fsdp", between, 2)
    out_2 = swap(out_cols, "seq", 2)
    qkv = jnp.stack([dotg(wq, b, 0, 1).astype(bf16) for b in normed])
    length = lax.dynamic_index_in_dim(lengths, group, 0, keepdims=False)
    slot = (me & 1) * 2 + (me >> 1)
    info = [jnp.stack((slot, length, jnp.int32(h))).astype(jnp.int32) for h in range(heads)]

    lse, many = [None] * heads, heads - 1
    att, lse[1] = attend(info[1], qkv, many, 0)
    pair, out_cols, out_2, cot_packet = after(att, pair, out_cols, out_2, cot_packet)
    up, down = pair[0], pair[1]
    (qkv,) = after((up, down), qkv)
    cot_packet = deal(cot_packet).reshape(span, -1)
    up_came = swap(up, "fsdp", low)
    down_2 = swap(down, "seq", 2)
    out_1, out_3 = swap(out_cols, "seq", 1), swap(out_2, "seq", 1)
    for h in range(2, heads):
        att, lse[h] = attend(info[h], qkv, many, h - 1, att)
    att, out_1, out_3, down = lax.optimization_barrier((att, out_1, out_3, down))
    place = me.astype(jnp.int32)[None]
    square = jax.ShapeDtypeStruct((width, width), bf16)
    (w_out_full,) = row_call(
        join_columns_body, "join_columns", [square], place, [out_cols, out_2, out_1, out_3], [None] * 4, [None]
    )
    (qkv,) = after((att, w_out_full), qkv)
    att_early = across(att)
    down_came = swap(down, "fsdp", low)
    att_lone, lse[0] = attend(info[0], qkv, 1, 0)
    up, up_came, down_2, att_lone, att_early = lax.optimization_barrier((up, up_came, down_2, att_lone, att_early))
    att_late = across(att_lone)
    up = join(up, up_came, "fsdp", low, last).reshape(width, ff // parts)

    att_late, up, down, down_came, down_2, cot_packet = lax.optimization_barrier(
        (att_late, up, down, down_came, down_2, cot_packet)
    )
    up_2 = swap(up, "seq", 2)
    cot = cot_packet[:, :width]
    passes = cot_packet[:, width]
    cot_far = swap(cot, "seq", 1)
    down_2_came = swap(down_2, "fsdp", low)
    down = join(down, down_came, "fsdp", low, last).reshape(ff // parts, width)
    rows_f32 = jax.ShapeDtypeStruct((span, width), f32)
    rows_bf16 = jax.ShapeDtypeStruct((span, width), bf16)
    residual, nm = row_call(
        project_out_body, "project_out", [rows_f32, rows_bf16], place,
        [*att_early, *att_late, w_out_full, inputs, gain_two[None]], [1] * 8 + [None, 0, None], [0, 0], parts,
    )
    nm_far = swap(nm, "seq", 1)
    *near, up_0, down_0 = mlp_part(nm, cot, up, down)
    *far, up_0, down_0 = mlp_part(nm_far, cot_far, up, down, (), (up_0, down_0))
    down_2, down_2_came, up_2 = after(far[0], down_2, down_2_came, up_2)
    down_2 = join(down_2, down_2_came, "fsdp", low, last).reshape(ff // parts, width)
    *far, d_up_2, d_down_2 = mlp_part(nm_far, cot_far, up_2, down_2, far)
    far = [swap(a.astype(bf16), "seq", 1) for a in far]
    *near, up_2, down_2 = mlp_part(nm, cot, up_2, down_2, near, (d_up_2, d_down_2))
    down = jnp.stack((down_0, down_2)).reshape(2, *sizes, ff_each, width)
    down = halve(down, "fsdp", low, last + 1)
    head_rows = jax.ShapeDtypeStruct((parts, part, span), bf16)
    result, d_residual, d_branch, d_gain_mlp, d_heads = row_call(
        turn_body,
        "turn",
        [rows_bf16, rows_f32, rows_bf16, jax.ShapeDtypeStruct((1, width), f32), head_rows],
        place,
        [residual, near[0], far[0], near[1], far[1], cot, gain_two[None], w_out_full],
        [0] * 6 + [None] * 2,
        [0, 0, 0, None, 2],
        parts,
    )
    d_heads = across(d_heads)
    piece = jax.ShapeDtypeStruct((width, part), bf16)
    d_out, d_out_x, *d_out_far = row_call(
        out_grad_body, "out_grad", [piece] * 4, place, [*att_early, *att_late, d_branch], [None] * 9, [None] * 4,
        scratch=[pltpu.VMEM((width, width), bf16)],
    )
    d_heads, d_out, d_out_x, d_out_far, up_0, up_2, result = lax.optimization_barrier(
        (d_heads, d_out, d_out_x, d_out_far, up_0, up_2, result)
    )

    up_came = swap(up_2, "seq", 2)
    out_back = deal(result.reshape(groups, local_len, width))
    d_out_1, d_out_3 = [swap(a, "seq", 1) for a in d_out_far]
    d_qkv = [attend_back(info[0], qkv, att_lone, d_heads, lse[0], 0, 0)]
    down, d_out_x, d_out_3 = after(d_qkv, down, d_out_x, d_out_3)
    down = halve(down[0], "fsdp", f_bits[-2], last, down[1])
    d_out_x = add(d_out_x, d_out_3)
    d_heads = after((down[0], d_out_x), d_heads)[0]
    d_out_x = swap(d_out_x, "seq", 2)
    for h in range(1, many):
        d_qkv.append(attend_back(info[h], qkv, att, d_heads, lse[h], h - 1, h))
    up_0, up_came, down, d_out_x, out_back = after(d_qkv, up_0, up_came, down, d_out_x, out_back)
    split = lambda a: a.reshape(*sizes, own_rows, ff // parts)
    up = halve(split(up_0), "fsdp", low, last, split(up_came))
    for k in reversed(range(last - 1)):
        down = halve(down[0], "fsdp", f_bits[k], k + 1, down[1])
    (d_heads,) = after((up[0], down[0], out_back), d_heads)
    d_qkv.append(attend_back(info[many], qkv, att, d_heads, lse[many], many - 1, many))
    d_qkv, down, up = lax.optimization_barrier((d_qkv, down, up))

    half = jax.ShapeDtypeStruct((2, span, width), bf16)
    project_back = lambda a: row_call(rows_grad_body, "rows_grad", [half], place, [*a, wq], [None] * (heads + 1), [None])[0]
    d_far = swap(project_back([d[2:] for d in d_qkv]), "seq", 1)
    d_near = project_back([d[:2] for d in d_qkv])
    (d_tail,) = after(d_near, d_qkv)
    down = add(*down)
    up = halve(up[0], "fsdp", f_bits[-2], last - 1, up[1])
    (d_wq,) = row_call(
        weight_grad_body, "weight_grad", [square], place, [*normed, *d_tail, d_out, d_out_1, d_out_x],
        [None] * (7 + heads), [None],
    )
    d_near, d_wq, up = lax.optimization_barrier((d_near, d_wq, up))
    d_wq = halve(d_wq.reshape(*sizes, own_rows, width), "fsdp", low, last)
    for k in reversed(range(last - 1)):
        up = halve(up[0], "fsdp", f_bits[k], k, up[1])
    (d_near,) = after(up[0], d_near)
    d_near = add(d_near, d_far)
    d_came = swap(d_near[1], "seq", 2)
    d_wq = halve(d_wq[0], "fsdp", f_bits[-2], last - 1, d_wq[1])
    d_wq, down = after(d_came, d_wq, down)
    down_came = swap(down[1], "seq", 2)
    for k in reversed(range(last - 1)):
        d_wq = halve(d_wq[0], "fsdp", f_bits[k], k, d_wq[1])
    d_normed = d_near[0].astype(f32) + d_came.astype(f32)
    z_one, inverse_one = norm_stats(inputs.astype(f32))
    d_in_norm, d_gain_attn = norm_back(z_one, inverse_one, gain_one, d_normed)
    d_inputs = (d_residual + d_in_norm).astype(bf16)
    d_back = deal(d_inputs.reshape(groups, local_len, width))
    up, d_wq = after(d_inputs, up, d_wq)
    (d_wq,) = after(d_back, d_wq)
    pair = jnp.stack((add(*up), add(down[0], down_came)))
    grads = gather(pair, "seq", (2, 1)).reshape(parts, 2, own_rows, width).astype(f32)
    g_up = grads[:, 0].reshape(parts, own_rows, groups, ff_each).transpose(1, 2, 0, 3).reshape(own_rows, ff)
    g_down = grads[:, 1].reshape(ff // groups, width)

    count = table.shape[0]
    picks = (passes[None, :] == jnp.arange(count, dtype=jnp.int32)[:, None].astype(bf16)).astype(bf16)
    d_table = jnp.dot(picks, d_inputs, preferred_element_type=f32)
    small = jnp.concatenate((d_table, d_gain_attn, d_gain_mlp, jnp.zeros_like(d_gain_mlp)), axis=0)
    for bit in (1, 2):
        small = small + swap(small, "seq", bit)
    for bit in reversed(f_bits[1:]):
        small = small + swap(small, "fsdp", bit)
    (small,) = after(d_back, small)
    small = small + swap(small, "fsdp", top)
    owned_gain = lambda row: lax.dynamic_slice_in_dim(small[row], group * own_rows, own_rows)

    d_wq = gather(add(*d_wq), "seq", (2, 1)).reshape(parts, own_rows, width).astype(f32)
    g_out = jnp.swapaxes(d_wq[..., 3 * part :], 0, 1)
    g_qkv = d_wq[..., : 3 * part].reshape(parts, own_rows, heads, 3, DH).transpose(1, 3, 0, 2, 4)
    return (
        jnp.swapaxes(out_back, 0, 1),
        jnp.swapaxes(d_back, 0, 1),
        small[:count],
        owned_gain(count),
        g_qkv.reshape(own_rows, 3 * width),
        g_out.reshape(own_rows, width),
        owned_gain(count + 1),
        g_up,
        g_down,
    )


def solution(mesh):
    return jax.shard_map(
        per_device,
        mesh=mesh,
        in_specs=(
            P(("seq", "fsdp"), None, None),
            P(("seq", "fsdp"), None),
            P(),
            P(),
            P("fsdp"),
            P("fsdp", None),
            P("fsdp", None),
            P("fsdp"),
            P("fsdp", None),
            P("fsdp", None),
            P(("seq", "fsdp"), None, None),
        ),
        out_specs=(
            P(("seq", "fsdp"), None, None),
            P(("seq", "fsdp"), None, None),
            P(),
            P("fsdp"),
            P("fsdp", None),
            P("fsdp", None),
            P("fsdp"),
            P("fsdp", None),
            P("fsdp", None),
        ),
        check_vma=False,
    )
```

```python
import functools

import jax
import jax.numpy as jnp
from jax import lax
from jax.experimental import pallas as pl
from jax.experimental.pallas import tpu as pltpu
from jax.sharding import PartitionSpec as P

HEADS = 12
EPSILON = 1e-05
LOG2E = 1.4426950408889634
LN2 = 0.6931471805599453
MASKED = -1e30
DH = 64


def dotg(a, b, ca, cb):
    return lax.dot_general(a, b, (((ca,), (cb,)), ((), ())), preferred_element_type=jnp.float32)


def slot_of(block, info):
    return (((block & 1) << 1) | (block >> 1)) ^ info[0]


def attend_body(info, qkv, *refs, blk):
    out, lse, acc = refs[-3:]
    i = pl.program_id(0)
    length = info[1]
    qt = qkv[slot_of(i, info), 0:DH, :]
    scale = DH ** -0.5 * LOG2E

    def step(j, carry, masked):
        top, tot = carry
        kt = qkv[slot_of(j, info), DH : 2 * DH, :]
        vt = qkv[slot_of(j, info), 2 * DH : 3 * DH, :]
        st = dotg(kt, qt, 0, 0) * scale
        if masked:
            key_at = j * blk + lax.broadcasted_iota(jnp.int32, st.shape, 0)
            query_at = i * blk + lax.broadcasted_iota(jnp.int32, st.shape, 1)
            st = jnp.where((query_at >= key_at) & (key_at < length), st, MASKED)
        new_top = jnp.maximum(top, jnp.max(st, axis=0, keepdims=True))
        fade = jnp.exp2(top - new_top)
        pt = jnp.exp2(st - new_top)
        tot = tot * fade + jnp.sum(pt, axis=0, keepdims=True)
        acc[...] = acc[...] * fade + dotg(vt, pt.astype(jnp.bfloat16), 1, 0)
        return new_top, tot

    acc[...] = jnp.zeros_like(acc)
    carry = (jnp.full((1, blk), MASKED, jnp.float32), jnp.zeros((1, blk), jnp.float32))
    plain = jnp.minimum(i, length // blk)
    stop = jnp.minimum(i + 1, (length + blk - 1) // blk)
    carry = lax.fori_loop(0, plain, functools.partial(step, masked=False), carry)
    top, tot = lax.fori_loop(plain, stop, functools.partial(step, masked=True), carry)
    out[0] = (acc[...] / tot).astype(jnp.bfloat16)
    lse[0] = top + jnp.log2(tot)


def attend(info, qkv):
    blocks, _, blk = qkv.shape
    return pl.pallas_call(
        functools.partial(attend_body, blk=blk),
        grid_spec=pltpu.PrefetchScalarGridSpec(
            num_scalar_prefetch=1,
            grid=(blocks,),
            in_specs=[pl.BlockSpec((blocks, 3 * DH, blk), lambda i, info: (0, info[2], 0))],
            out_specs=[
                pl.BlockSpec((1, DH, blk), lambda i, info: (slot_of(i, info), 0, 0)),
                pl.BlockSpec((1, 1, blk), lambda i, info: (i, 0, 0)),
            ],
            scratch_shapes=[pltpu.VMEM((DH, blk), jnp.float32)],
        ),
        out_shape=[
            jax.ShapeDtypeStruct((blocks, DH, blk), jnp.bfloat16),
            jax.ShapeDtypeStruct((blocks, 1, blk), jnp.float32),
        ],
        compiler_params=pltpu.CompilerParams(vmem_limit_bytes=16 << 20),
        cost_estimate=SMALL,
        name="attend",
    )(info, qkv)


def attend_back_body(info, qkv, att, *refs, blocks, blk):
    came, (lse, dqkv, dq, q_rows, do_rows, delta, datt) = refs[:blocks], refs[blocks:]
    j = pl.program_id(0)
    length = info[1]
    scale = DH ** -0.5
    at_q, at_k, at_v = slice(0, DH), slice(DH, 2 * DH), slice(2 * DH, 3 * DH)

    @pl.when(j == 0)
    def _():
        dq[...] = jnp.zeros_like(dq)
        for b in range(blocks):
            datt[b] = came[b][...]
        for b in range(blocks):
            at = slot_of(b, info)
            dt = datt[at]
            q_rows[b] = qkv[at, at_q, :].T
            do_rows[b] = dt.T
            delta[b] = jnp.sum(dt.astype(jnp.float32) * att[at].astype(jnp.float32), axis=0, keepdims=True)

    kt = qkv[slot_of(j, info), at_k, :]
    vt = qkv[slot_of(j, info), at_v, :]
    k_rows = kt.T
    v_rows = vt.T

    def step(i, carry, masked):
        dk, dv = carry
        qt = qkv[slot_of(i, info), at_q, :]
        st = jnp.dot(k_rows, qt, preferred_element_type=jnp.float32)
        pt = jnp.exp2(st * (scale * LOG2E) - lse[i])
        if masked:
            key_at = j * blk + lax.broadcasted_iota(jnp.int32, st.shape, 0)
            query_at = i * blk + lax.broadcasted_iota(jnp.int32, st.shape, 1)
            pt = jnp.where((query_at >= key_at) & (key_at < length), pt, 0.0)
        dpt = jnp.dot(v_rows, datt[slot_of(i, info)], preferred_element_type=jnp.float32)
        dst = (pt * (dpt - delta[i])).astype(jnp.bfloat16)
        dv = dv + jnp.dot(pt.astype(jnp.bfloat16), do_rows[i], preferred_element_type=jnp.float32)
        dk = dk + jnp.dot(dst, q_rows[i], preferred_element_type=jnp.float32)
        dq[i] = dq[i] + jnp.dot(kt, dst, preferred_element_type=jnp.float32)
        return dk, dv

    zero = jnp.zeros((blk, DH), jnp.float32)
    whole = (j + 1) * blk <= length
    some = j * blk < length
    masked_end = jnp.where(some, jnp.where(whole, j + 1, blocks), j)
    carry = lax.fori_loop(j, masked_end, functools.partial(step, masked=True), (zero, zero))
    dk, dv = lax.fori_loop(
        jnp.where(whole, j + 1, blocks), blocks, functools.partial(step, masked=False), carry
    )
    dqkv[slot_of(j, info), at_k, :] = (dk * scale).astype(jnp.bfloat16).T
    dqkv[slot_of(j, info), at_v, :] = dv.astype(jnp.bfloat16).T
    dqkv[slot_of(j, info), at_q, :] = (dq[j] * scale).astype(jnp.bfloat16)


def attend_back(info, qkv, att, datt, lse):
    blocks, rows, blk = qkv.shape
    third = pl.BlockSpec((blocks, 3 * DH, blk), lambda j, info: (0, info[2], 0))
    return pl.pallas_call(
        functools.partial(attend_back_body, blocks=blocks, blk=blk),
        grid_spec=pltpu.PrefetchScalarGridSpec(
            num_scalar_prefetch=1,
            grid=(blocks,),
            in_specs=[
                third,
                pl.BlockSpec((blocks, DH, blk), lambda j, info: (0, 0, 0)),
                *[pl.BlockSpec((DH, blk), lambda j, info: (info[2], 0))] * blocks,
                pl.BlockSpec((blocks, 1, blk), lambda j, info: (0, 0, 0)),
            ],
            out_specs=pl.BlockSpec((blocks, 3 * DH, blk), lambda j, info: (0, 0, 0)),
            scratch_shapes=[
                pltpu.VMEM((blocks, DH, blk), jnp.float32),
                pltpu.VMEM((blocks, blk, DH), jnp.bfloat16),
                pltpu.VMEM((blocks, blk, DH), jnp.bfloat16),
                pltpu.VMEM((blocks, 1, blk), jnp.float32),
                pltpu.VMEM((blocks, DH, blk), jnp.bfloat16),
            ],
        ),
        out_shape=jax.ShapeDtypeStruct((blocks, 3 * DH, blk), jnp.bfloat16),
        compiler_params=pltpu.CompilerParams(vmem_limit_bytes=18 << 20),
        cost_estimate=SMALL,
        name="attend_back",
    )(info, qkv, att, *datt, lse)


SMALL = pl.CostEstimate(flops=1 << 20, bytes_accessed=1 << 20, transcendentals=0)
GELU_A = 0.7978845608028654
GELU_B = 0.044715


def mlp_body(nm, cot, wu, wd, *refs, begun):
    acc, dnm, dwu, dwd = refs[-4:]

    @pl.when(pl.program_id(0) == 0)
    def _():
        acc[...] = refs[0][...] if begun else jnp.zeros_like(acc)
        dnm[...] = refs[1][...] if begun else jnp.zeros_like(dnm)

    x = nm[...]
    g = cot[...]
    u = jnp.dot(x, wu[...], preferred_element_type=jnp.float32)
    da = dotg(g, wd[...], 1, 1)
    square = u * u
    th = jnp.tanh(GELU_A * u * (1.0 + GELU_B * square))
    half = 0.5 * (1.0 + th)
    a = (u * half).astype(jnp.bfloat16)
    slope = half + 0.5 * u * (1.0 - th * th) * (GELU_A * (1.0 + 3.0 * GELU_B * square))
    du = (da * slope).astype(jnp.bfloat16)
    acc[...] += jnp.dot(a, wd[...], preferred_element_type=jnp.float32)
    dnm[...] += dotg(du, wu[...], 1, 1)
    dwu[...] = dotg(x, du, 0, 0).astype(jnp.bfloat16)
    dwd[...] = dotg(a, g, 0, 0).astype(jnp.bfloat16)


def mlp_part(nm, cot, wu, wd, sums=(), step=256):
    rows, width = nm.shape
    ff = wu.shape[1]
    whole = pl.BlockSpec((rows, width), lambda i: (0, 0))
    up = pl.BlockSpec((width, step), lambda i: (0, i))
    down = pl.BlockSpec((step, width), lambda i: (i, 0))
    return pl.pallas_call(
        functools.partial(mlp_body, begun=bool(sums)),
        grid=(ff // step,),
        in_specs=[whole, whole, up, down] + [whole, whole][: len(sums)],
        out_specs=[whole, whole, up, down],
        out_shape=[
            jax.ShapeDtypeStruct((rows, width), jnp.float32),
            jax.ShapeDtypeStruct((rows, width), jnp.float32),
            jax.ShapeDtypeStruct(wu.shape, jnp.bfloat16),
            jax.ShapeDtypeStruct(wd.shape, jnp.bfloat16),
        ],
        input_output_aliases={4: 0, 5: 1} if sums else {},
        compiler_params=pltpu.CompilerParams(vmem_limit_bytes=26 << 20),
        cost_estimate=SMALL,
        name="mlp_part",
    )(nm, cot, wu, wd, *sums)


ORDER = (0, 2, 1, 3)


def cut(array, axis, steps):
    shape = tuple(n // steps if k == axis else n for k, n in enumerate(array.shape))
    return pl.BlockSpec(shape, lambda i: tuple(i if k == axis else 0 for k in range(len(shape))))


def row_call(body, name, out_shape, place, operands, in_axes, out_axes, steps=1, scratch=()):
    return pl.pallas_call(
        body,
        grid=(steps,),
        in_specs=[pl.BlockSpec(memory_space=pltpu.SMEM)] + [cut(a, k, steps) for a, k in zip(operands, in_axes)],
        out_specs=[cut(a, k, steps) for a, k in zip(out_shape, out_axes)],
        out_shape=out_shape,
        scratch_shapes=scratch,
        compiler_params=pltpu.CompilerParams(vmem_limit_bytes=20 << 20),
        cost_estimate=SMALL,
        name=name,
    )(place, *operands)


def rows_at(place, slot, part):
    return pl.ds(pl.multiple_of((place[0] ^ ORDER[slot]) * part, DH), part)


def project_out_body(place, *refs):
    pieces, (w, inputs, gain, residual, nm) = refs[:-5], refs[-5:]
    part = len(pieces) // 4 * DH
    residual[...] = inputs[...].astype(jnp.float32)
    for s in range(4):
        heads = jnp.concatenate([p[...] for p in pieces[s::4]], axis=0)
        residual[...] += dotg(heads, w[rows_at(place, s, part), :], 0, 0)
    z, _ = norm_stats(residual[...])
    nm[...] = (z * gain[...]).astype(jnp.bfloat16)


def turn_body(place, residual, sum_near, sum_far, grad_near, grad_far, cot, gain, w, *refs):
    result, d_residual, d_branch, d_gain, d_heads = refs
    part = d_heads.shape[1]
    result[...] = (residual[...] + sum_near[...] + sum_far[...].astype(jnp.float32)).astype(jnp.bfloat16)
    z, inverse = norm_stats(residual[...])
    back, gain_part = norm_back(z, inverse, gain[...], grad_near[...] + grad_far[...].astype(jnp.float32))

    @pl.when(pl.program_id(0) == 0)
    def _():
        d_gain[...] = jnp.zeros_like(d_gain)

    d_gain[...] += gain_part
    d_residual[...] = cot[...].astype(jnp.float32) + back
    d_branch[...] = d_residual[...].astype(jnp.bfloat16)
    for s in range(4):
        d_heads[s] = dotg(w[rows_at(place, s, part), :], d_branch[...], 1, 1).astype(jnp.bfloat16)


def join_columns_body(place, *refs):
    pieces, out = refs[:4], refs[4]
    part = pieces[0].shape[1]

    def fill(me):
        for s in range(4):
            d = me ^ ORDER[s]
            out[:, d * part : (d + 1) * part] = pieces[s][...]

    for me in range(4):
        pl.when(place[0] == me)(functools.partial(fill, me))


def out_grad_body(place, *refs):
    came, (d_branch, *pieces, out) = refs[:-6], refs[-6:]
    part = len(came) // 4 * DH
    for s in range(4):
        heads = jnp.concatenate([p[...] for p in came[s::4]], axis=0)
        out[rows_at(place, s, part), :] = jnp.dot(
            heads, d_branch[...], preferred_element_type=jnp.float32
        ).astype(jnp.bfloat16)

    def fill(me):
        for s in range(4):
            d = me ^ ORDER[s]
            pieces[s][...] = out[:, d * part : (d + 1) * part]

    for me in range(4):
        pl.when(place[0] == me)(functools.partial(fill, me))


def rows_grad_body(place, *refs):
    *heads, w, out = refs
    for s in range(out.shape[0]):
        grad = jnp.concatenate([h[s] for h in heads], axis=0)
        out[s] = dotg(grad, w[...], 0, 1).astype(jnp.bfloat16)


def weight_grad_body(place, *refs):
    normed, heads, (*parts, out) = refs[:4], refs[4:-4], refs[-4:]
    total = 0.0
    for s in range(4):
        total += dotg(normed[s][...], jnp.concatenate([h[s] for h in heads], axis=0), 0, 1)
    rest = sum(p[...].astype(jnp.float32) for p in parts).astype(jnp.bfloat16)
    out[...] = jnp.concatenate((total.astype(jnp.bfloat16), rest), axis=1)


def pick_up_body(place, w, out, *, each):
    def fill(me):
        for g in range(out.shape[1] // each):
            out[:, g * each : (g + 1) * each] = w[:, (g * 4 + me) * each : (g * 4 + me + 1) * each]

    for me in range(4):
        pl.when(place[0] == me)(functools.partial(fill, me))


def place_up_body(place, grads, out, *, each):
    for p in range(4):
        for g in range(grads.shape[-1] // each):
            at = (g * 4 + p) * each
            out[:, at : at + each] = grads[p, :, g * each : (g + 1) * each].astype(jnp.float32)


def place_qkv_body(place, grads, qkv, out):
    width = out.shape[1]
    part = width // 4
    heads = part // DH
    for p in range(4):
        out[:, p * part : (p + 1) * part] = grads[p, :, 3 * part :].astype(jnp.float32)
        for h in range(heads):
            for which in range(3):
                at = which * width + (p * heads + h) * DH
                start = (h * 3 + which) * DH
                qkv[:, at : at + DH] = grads[p, :, start : start + DH].astype(jnp.float32)


def swap(value, axis, bit):
    count = lax.axis_size(axis)
    return lax.ppermute(value, axis, [(i, i ^ bit) for i in range(count)])


def bits_of(axis):
    count = lax.axis_size(axis)
    assert count & (count - 1) == 0, "axis size"
    return [1 << b for b in reversed(range(count.bit_length() - 1))]


def is_set(axis, bit):
    return (lax.axis_index(axis) & bit) != 0


def join(own, came, axis, bit, at):
    own, came = (jnp.expand_dims(a, at) for a in (own, came))
    shape = own.shape[:at] + (2,) + own.shape[at + 1 :]
    place = lax.broadcasted_iota(jnp.int32, shape, at)
    return jnp.where(place == is_set(axis, bit).astype(jnp.int32), own, came)


def gather(value, axis, bits, at=0):
    for k, bit in enumerate(bits):
        value = join(value, swap(value, axis, bit), axis, bit, at + k)
    return value


def spread(blocks, bit):
    return blocks | {r ^ bit: swap(b, "seq", bit) for r, b in blocks.items()}


def add(a, b):
    return (a.astype(jnp.float32) + b.astype(jnp.float32)).astype(a.dtype)


def fold(blocks, bit):
    return {r: add(b, swap(blocks[r ^ bit], "seq", bit)) for r, b in blocks.items() if not r & bit}


def halve(value, axis, bit, at, *more):
    mine = is_set(axis, bit).astype(jnp.int32)
    part = lambda which: functools.reduce(
        add, [lax.dynamic_index_in_dim(v, which, at, keepdims=False) for v in (value, *more)]
    )
    return part(mine), swap(part(1 - mine), axis, bit)


def norm_stats(values):
    centre = jnp.mean(values, axis=-1, keepdims=True)
    shifted = values - centre
    spread_of = jnp.mean(shifted * shifted, axis=-1, keepdims=True)
    inverse = lax.rsqrt(spread_of + EPSILON)
    return shifted * inverse, inverse


def norm_back(z, inverse, gain, grad):
    e = grad * gain
    back = (e - jnp.mean(e, axis=-1, keepdims=True) - z * jnp.mean(e * z, axis=-1, keepdims=True)) * inverse
    return back, jnp.sum(grad * z, axis=0, keepdims=True)


def pick_at(value, at):
    return lax.dynamic_index_in_dim(value, at, 1, keepdims=False)


def after(first, *values):
    return lax.optimization_barrier((first, values))[1]


def per_device(
    tokens, pass_index, lengths, table, gain_attn, w_qkv, w_out, gain_mlp, w_up, w_down, cotangent
):
    bf16, f32 = jnp.bfloat16, jnp.float32
    groups, parts = lax.axis_size("fsdp"), lax.axis_size("seq")
    local_len, seq_total, width = tokens.shape
    assert seq_total == groups and parts == 4
    heads = HEADS // parts
    part = width // parts
    ff = w_up.shape[1]
    own_rows = width // groups
    ff_each = ff // groups // parts
    me, group = lax.axis_index("seq"), lax.axis_index("fsdp")
    f_bits = bits_of("fsdp")
    last = len(f_bits) - 1
    top, low, between = f_bits[0], f_bits[-1], f_bits[1:-1]
    sizes = (2,) * len(f_bits)
    span = local_len * groups
    pick = lambda a, at: lax.dynamic_index_in_dim(a, me, at, keepdims=False)
    deal = lambda a: lax.all_to_all(a, "fsdp", split_axis=0, concat_axis=0, tiled=True)
    across = lambda a: [a[0]] + [swap(a[s], "seq", r) for s, r in enumerate(ORDER) if r]

    chooser = (pass_index[..., None] == jnp.arange(table.shape[0], dtype=jnp.int32)).astype(bf16)
    embedded = jnp.einsum("pnc,cd->npd", chooser, table, preferred_element_type=f32)
    summed = (jnp.swapaxes(tokens, 0, 1).astype(f32) + embedded).astype(bf16)
    inputs = deal(summed).reshape(span, width)
    qkv_slice = pick(w_qkv.reshape(own_rows, 3, parts, heads, DH), 2)
    qkv_slice = jnp.swapaxes(qkv_slice, 1, 2).reshape(own_rows, 3 * part)
    out_slice = pick(w_out.reshape(own_rows, parts, part), 1)
    gains = jnp.stack((gain_attn, gain_mlp), axis=1)
    qkv_slice, out_slice = after(summed, qkv_slice, out_slice)
    packet = jnp.concatenate((qkv_slice, out_slice, gains, jnp.zeros((own_rows, 126), bf16)), axis=1)
    packet_came = swap(packet, "fsdp", top)
    place = me.astype(jnp.int32)[None]
    (up,) = row_call(
        functools.partial(pick_up_body, each=ff_each), "pick_up",
        [jax.ShapeDtypeStruct((own_rows, ff // parts), bf16)], place, [w_up], [None], [None],
    )
    down = pick(w_down.reshape(parts, ff_each, width), 0)
    pair = jnp.stack((up, down))

    rows_2, rows_1 = swap(inputs, "seq", 2), swap(inputs, "seq", 1)
    rows = (inputs, rows_2, rows_1, swap(rows_2, "seq", 1))
    packet, packet_came, pair = after(inputs, packet, packet_came, pair)
    packet = gather(join(packet, packet_came, "fsdp", top, 0), "fsdp", between, 1)
    packet, pair = lax.optimization_barrier((packet, pair))
    packet = gather(packet, "fsdp", (low,), last).reshape(width, -1)
    wq = packet[:, : 3 * part]
    out_cols = packet[:, 3 * part : width]
    gain_one = packet[:, width].astype(f32)
    gain_two = packet[:, width + 1].astype(f32)
    pair_came = swap(pair, "fsdp", top)
    marks = jnp.swapaxes(pass_index, 0, 1)[..., None].astype(bf16)
    cot_packet = jnp.concatenate(
        (jnp.swapaxes(cotangent, 0, 1), jnp.broadcast_to(marks, marks.shape[:2] + (128,))), axis=2
    )

    normed = [(norm_stats(b.astype(f32))[0] * gain_one).astype(bf16) for b in rows]
    pair, pair_came, out_cols = after(rows[3], pair, pair_came, out_cols)
    pair = join(pair, pair_came, "fsdp", top, 1)
    pair = gather(pair, "fsdp", between, 2)
    out_2 = swap(out_cols, "seq", 2)
    qkv = jnp.stack([dotg(wq, b, 0, 1).astype(bf16) for b in normed])
    length = lax.dynamic_index_in_dim(lengths, group, 0, keepdims=False)
    slot = (me & 1) * 2 + (me >> 1)
    info = [jnp.stack((slot, length, jnp.int32(h))).astype(jnp.int32) for h in range(heads)]

    att, lse, crossed, many = [None] * heads, [None] * heads, [None] * heads, heads - 1
    att[1], lse[1] = attend(info[1], qkv)
    pair, out_cols, out_2, cot_packet = after(att[1], pair, out_cols, out_2, cot_packet)
    up, down = pair[0], pair[1]
    (qkv,) = after((up, down), qkv)
    cot_packet = deal(cot_packet).reshape(span, -1)
    up_came = swap(up, "fsdp", low)
    down_2 = swap(down, "seq", 2)
    out_1, out_3 = swap(out_cols, "seq", 1), swap(out_2, "seq", 1)
    for h in range(2, heads):
        att[h], lse[h] = attend(info[h], qkv)
    att[1:], out_1, out_3, down = lax.optimization_barrier((att[1:], out_1, out_3, down))
    square = jax.ShapeDtypeStruct((width, width), bf16)
    (w_out_full,) = row_call(
        join_columns_body, "join_columns", [square], place, [out_cols, out_2, out_1, out_3], [None] * 4, [None]
    )
    (qkv,) = after((att[1:], w_out_full), qkv)
    crossed[1:] = [across(a) for a in att[1:]]
    down_came = swap(down, "fsdp", low)
    att[0], lse[0] = attend(info[0], qkv)
    up, up_came, down_2, att[0], crossed[1:] = lax.optimization_barrier((up, up_came, down_2, att[0], crossed[1:]))
    crossed[0] = across(att[0])
    up = join(up, up_came, "fsdp", low, last).reshape(width, ff // parts)

    crossed[0], up, down, down_came, down_2, cot_packet = lax.optimization_barrier(
        (crossed[0], up, down, down_came, down_2, cot_packet)
    )
    crossed = [piece for pieces in crossed for piece in pieces]
    up_2 = swap(up, "seq", 2)
    cot = cot_packet[:, :width]
    passes = cot_packet[:, width]
    cot_far = swap(cot, "seq", 1)
    down_2_came = swap(down_2, "fsdp", low)
    down = join(down, down_came, "fsdp", low, last).reshape(ff // parts, width)
    rows_f32 = jax.ShapeDtypeStruct((span, width), f32)
    rows_bf16 = jax.ShapeDtypeStruct((span, width), bf16)
    residual, nm = row_call(
        project_out_body, "project_out", [rows_f32, rows_bf16], place,
        [*crossed, w_out_full, inputs, gain_two[None]], [1] * len(crossed) + [None, 0, None], [0, 0], parts,
    )
    nm_far = swap(nm, "seq", 1)
    *near, up_0, down_0 = mlp_part(nm, cot, up, down)
    *far, up_1, down_1 = mlp_part(nm_far, cot_far, up, down)
    down_2, down_2_came, up_2 = after(far[0], down_2, down_2_came, up_2)
    down_2 = join(down_2, down_2_came, "fsdp", low, last).reshape(ff // parts, width)
    *far, d_up_2, d_down_2 = mlp_part(nm_far, cot_far, up_2, down_2, far)
    far = [swap(a.astype(bf16), "seq", 1) for a in far]
    *near, up_2, down_2 = mlp_part(nm, cot, up_2, down_2, near)
    up_2 = add(up_2, d_up_2)
    down = jnp.stack((add(down_0, down_1), add(down_2, d_down_2))).reshape(2, *sizes, ff_each, width)
    down = halve(down, "fsdp", low, last + 1)
    head_rows = jax.ShapeDtypeStruct((parts, part, span), bf16)
    result, d_residual, d_branch, d_gain_mlp, d_heads = row_call(
        turn_body,
        "turn",
        [rows_bf16, rows_f32, rows_bf16, jax.ShapeDtypeStruct((1, width), f32), head_rows],
        place,
        [residual, near[0], far[0], near[1], far[1], cot, gain_two[None], w_out_full],
        [0] * 6 + [None] * 2,
        [0, 0, 0, None, 2],
        parts,
    )
    d_heads = across(d_heads)
    piece = jax.ShapeDtypeStruct((width, part), bf16)
    d_out, d_out_x, *d_out_far = row_call(
        out_grad_body, "out_grad", [piece] * 4, place, [*crossed, d_branch], [None] * (len(crossed) + 1), [None] * 4,
        scratch=[pltpu.VMEM((width, width), bf16)],
    )
    d_heads, d_out, d_out_x, d_out_far, up_0, up_1, up_2, result = lax.optimization_barrier(
        (d_heads, d_out, d_out_x, d_out_far, up_0, up_1, up_2, result)
    )

    up_came = swap(up_2, "seq", 2)
    out_back = deal(result.reshape(groups, local_len, width))
    d_out_1, d_out_3 = [swap(a, "seq", 1) for a in d_out_far]
    d_qkv = [attend_back(info[0], qkv, att[0], d_heads, lse[0])]
    down, d_out_x, d_out_3 = after(d_qkv, down, d_out_x, d_out_3)
    down = halve(down[0], "fsdp", f_bits[-2], last, down[1])
    d_out_x = add(d_out_x, d_out_3)
    d_heads = after((down[0], d_out_x), d_heads)[0]
    d_out_x = swap(d_out_x, "seq", 2)
    for h in range(1, many):
        d_qkv.append(attend_back(info[h], qkv, att[h], d_heads, lse[h]))
    up_0, up_1, up_came, down, d_out_x, out_back = after(d_qkv, up_0, up_1, up_came, down, d_out_x, out_back)
    split = lambda a: a.reshape(*sizes, own_rows, ff // parts)
    up = halve(split(up_0), "fsdp", low, last, split(up_1), split(up_came))
    for k in reversed(range(last - 1)):
        down = halve(down[0], "fsdp", f_bits[k], k + 1, down[1])
    (d_heads,) = after((up[0], down[0], out_back), d_heads)
    d_qkv.append(attend_back(info[many], qkv, att[many], d_heads, lse[many]))
    d_qkv, down, up = lax.optimization_barrier((d_qkv, down, up))

    half = jax.ShapeDtypeStruct((2, span, width), bf16)
    project_back = lambda a: row_call(rows_grad_body, "rows_grad", [half], place, [*a, wq], [None] * (heads + 1), [None])[0]
    d_far = swap(project_back([d[2:] for d in d_qkv]), "seq", 1)
    d_near = project_back([d[:2] for d in d_qkv])
    (d_tail,) = after(d_near, d_qkv)
    down = add(*down)
    up = halve(up[0], "fsdp", f_bits[-2], last - 1, up[1])
    (d_wq,) = row_call(
        weight_grad_body, "weight_grad", [square], place, [*normed, *d_tail, d_out, d_out_1, d_out_x],
        [None] * (7 + heads), [None],
    )
    d_near, d_wq, up = lax.optimization_barrier((d_near, d_wq, up))
    d_wq = halve(d_wq.reshape(*sizes, own_rows, width), "fsdp", low, last)
    for k in reversed(range(last - 1)):
        up = halve(up[0], "fsdp", f_bits[k], k, up[1])
    (d_near,) = after(up[0], d_near)
    d_near = add(d_near, d_far)
    d_came = swap(d_near[1], "seq", 2)
    d_wq = halve(d_wq[0], "fsdp", f_bits[-2], last - 1, d_wq[1])
    d_wq, down = after(d_came, d_wq, down)
    down_came = swap(down[1], "seq", 2)
    for k in reversed(range(last - 1)):
        d_wq = halve(d_wq[0], "fsdp", f_bits[k], k, d_wq[1])
    d_normed = d_near[0].astype(f32) + d_came.astype(f32)
    z_one, inverse_one = norm_stats(inputs.astype(f32))
    d_in_norm, d_gain_attn = norm_back(z_one, inverse_one, gain_one, d_normed)
    d_inputs = (d_residual + d_in_norm).astype(bf16)
    d_back = deal(d_inputs.reshape(groups, local_len, width))
    up, d_wq = after(d_inputs, up, d_wq)
    (d_wq,) = after(d_back, d_wq)
    pair = jnp.stack((add(*up), add(down[0], down_came)))
    grads = gather(pair, "seq", (2, 1)).reshape(parts, 2, own_rows, width)
    (g_up,) = row_call(
        functools.partial(place_up_body, each=ff_each), "place_up",
        [jax.ShapeDtypeStruct((own_rows, ff), f32)], place, [grads[:, 0]], [None], [None],
    )
    g_down = grads[:, 1].reshape(ff // groups, width).astype(f32)

    count = table.shape[0]
    picks = (passes[None, :] == jnp.arange(count, dtype=jnp.int32)[:, None].astype(bf16)).astype(bf16)
    d_table = jnp.dot(picks, d_inputs, preferred_element_type=f32)
    small = jnp.concatenate((d_table, d_gain_attn, d_gain_mlp, jnp.zeros_like(d_gain_mlp)), axis=0)
    for bit in (1, 2):
        small = small + swap(small, "seq", bit)
    for bit in reversed(f_bits[1:]):
        small = small + swap(small, "fsdp", bit)
    (small,) = after(d_back, small)
    small = small + swap(small, "fsdp", top)
    owned_gain = lambda row: lax.dynamic_slice_in_dim(small[row], group * own_rows, own_rows)

    d_wq = gather(add(*d_wq), "seq", (2, 1)).reshape(parts, own_rows, width)
    g_qkv, g_out = row_call(
        place_qkv_body, "place_qkv",
        [jax.ShapeDtypeStruct((own_rows, 3 * width), f32), jax.ShapeDtypeStruct((own_rows, width), f32)],
        place, [d_wq], [None], [None] * 2,
    )
    return (
        jnp.swapaxes(out_back, 0, 1),
        jnp.swapaxes(d_back, 0, 1),
        small[:count],
        owned_gain(count),
        g_qkv,
        g_out,
        owned_gain(count + 1),
        g_up,
        g_down,
    )


def solution(mesh):
    return jax.shard_map(
        per_device,
        mesh=mesh,
        in_specs=(
            P(("seq", "fsdp"), None, None),
            P(("seq", "fsdp"), None),
            P(),
            P(),
            P("fsdp"),
            P("fsdp", None),
            P("fsdp", None),
            P("fsdp"),
            P("fsdp", None),
            P("fsdp", None),
            P(("seq", "fsdp"), None, None),
        ),
        out_specs=(
            P(("seq", "fsdp"), None, None),
            P(("seq", "fsdp"), None, None),
            P(),
            P("fsdp"),
            P("fsdp", None),
            P("fsdp", None),
            P("fsdp"),
            P("fsdp", None),
            P("fsdp", None),
        ),
        check_vma=False,
    )
```

```python
import functools

import jax
import jax.numpy as jnp
from jax import lax
from jax.experimental import pallas as pl
from jax.experimental.pallas import tpu as pltpu
from jax.sharding import PartitionSpec as P

HEADS = 12
EPSILON = 1e-05
LOG2E = 1.4426950408889634
LN2 = 0.6931471805599453
MASKED = -1e30
DH = 64


def dotg(a, b, ca, cb):
    return lax.dot_general(a, b, (((ca,), (cb,)), ((), ())), preferred_element_type=jnp.float32)


def slot_of(block, info):
    return (((block & 1) << 1) | (block >> 1)) ^ info[0]


def attend_body(info, qkv, *refs, blk):
    out, lse, acc = refs[-3:]
    i = pl.program_id(0)
    length = info[1]
    qt = qkv[slot_of(i, info), 0:DH, :]
    scale = DH ** -0.5 * LOG2E

    def step(j, carry, masked):
        top, tot = carry
        kt = qkv[slot_of(j, info), DH : 2 * DH, :]
        vt = qkv[slot_of(j, info), 2 * DH : 3 * DH, :]
        st = dotg(kt, qt, 0, 0) * scale
        if masked:
            key_at = j * blk + lax.broadcasted_iota(jnp.int32, st.shape, 0)
            query_at = i * blk + lax.broadcasted_iota(jnp.int32, st.shape, 1)
            st = jnp.where((query_at >= key_at) & (key_at < length), st, MASKED)
        new_top = jnp.maximum(top, jnp.max(st, axis=0, keepdims=True))
        fade = jnp.exp2(top - new_top)
        pt = jnp.exp2(st - new_top)
        tot = tot * fade + jnp.sum(pt, axis=0, keepdims=True)
        acc[...] = acc[...] * fade + dotg(vt, pt.astype(jnp.bfloat16), 1, 0)
        return new_top, tot

    acc[...] = jnp.zeros_like(acc)
    carry = (jnp.full((1, blk), MASKED, jnp.float32), jnp.zeros((1, blk), jnp.float32))
    plain = jnp.minimum(i, length // blk)
    stop = jnp.minimum(i + 1, (length + blk - 1) // blk)
    carry = lax.fori_loop(0, plain, functools.partial(step, masked=False), carry)
    top, tot = lax.fori_loop(plain, stop, functools.partial(step, masked=True), carry)
    out[0] = (acc[...] / tot).astype(jnp.bfloat16)
    lse[0] = top + jnp.log2(tot)


def attend(info, qkv):
    blocks, _, blk = qkv.shape
    return pl.pallas_call(
        functools.partial(attend_body, blk=blk),
        grid_spec=pltpu.PrefetchScalarGridSpec(
            num_scalar_prefetch=1,
            grid=(blocks,),
            in_specs=[pl.BlockSpec((blocks, 3 * DH, blk), lambda i, info: (0, info[2], 0))],
            out_specs=[
                pl.BlockSpec((1, DH, blk), lambda i, info: (slot_of(i, info), 0, 0)),
                pl.BlockSpec((1, 1, blk), lambda i, info: (i, 0, 0)),
            ],
            scratch_shapes=[pltpu.VMEM((DH, blk), jnp.float32)],
        ),
        out_shape=[
            jax.ShapeDtypeStruct((blocks, DH, blk), jnp.bfloat16),
            jax.ShapeDtypeStruct((blocks, 1, blk), jnp.float32),
        ],
        compiler_params=pltpu.CompilerParams(vmem_limit_bytes=16 << 20),
        cost_estimate=SMALL,
        name="attend",
    )(info, qkv)


def attend_back_body(info, qkv, att, *refs, blocks, blk):
    came, (lse, dqkv, dq, q_rows, do_rows, delta, datt) = refs[:blocks], refs[blocks:]
    j = pl.program_id(0)
    length = info[1]
    scale = DH ** -0.5
    at_q, at_k, at_v = slice(0, DH), slice(DH, 2 * DH), slice(2 * DH, 3 * DH)

    @pl.when(j == 0)
    def _():
        dq[...] = jnp.zeros_like(dq)
        for b in range(blocks):
            datt[b] = came[b][...]
        for b in range(blocks):
            at = slot_of(b, info)
            dt = datt[at]
            q_rows[b] = qkv[at, at_q, :].T
            do_rows[b] = dt.T
            delta[b] = jnp.sum(dt.astype(jnp.float32) * att[at].astype(jnp.float32), axis=0, keepdims=True)

    kt = qkv[slot_of(j, info), at_k, :]
    vt = qkv[slot_of(j, info), at_v, :]
    k_rows = kt.T
    v_rows = vt.T

    def step(i, carry, masked):
        dk, dv = carry
        qt = qkv[slot_of(i, info), at_q, :]
        st = jnp.dot(k_rows, qt, preferred_element_type=jnp.float32)
        pt = jnp.exp2(st * (scale * LOG2E) - lse[i])
        if masked:
            key_at = j * blk + lax.broadcasted_iota(jnp.int32, st.shape, 0)
            query_at = i * blk + lax.broadcasted_iota(jnp.int32, st.shape, 1)
            pt = jnp.where((query_at >= key_at) & (key_at < length), pt, 0.0)
        dpt = jnp.dot(v_rows, datt[slot_of(i, info)], preferred_element_type=jnp.float32)
        dst = (pt * (dpt - delta[i])).astype(jnp.bfloat16)
        dv = dv + jnp.dot(pt.astype(jnp.bfloat16), do_rows[i], preferred_element_type=jnp.float32)
        dk = dk + jnp.dot(dst, q_rows[i], preferred_element_type=jnp.float32)
        dq[i] = dq[i] + jnp.dot(kt, dst, preferred_element_type=jnp.float32)
        return dk, dv

    zero = jnp.zeros((blk, DH), jnp.float32)
    whole = (j + 1) * blk <= length
    some = j * blk < length
    masked_end = jnp.where(some, jnp.where(whole, j + 1, blocks), j)
    carry = lax.fori_loop(j, masked_end, functools.partial(step, masked=True), (zero, zero))
    dk, dv = lax.fori_loop(
        jnp.where(whole, j + 1, blocks), blocks, functools.partial(step, masked=False), carry
    )
    dqkv[slot_of(j, info), at_k, :] = (dk * scale).astype(jnp.bfloat16).T
    dqkv[slot_of(j, info), at_v, :] = dv.astype(jnp.bfloat16).T
    dqkv[slot_of(j, info), at_q, :] = (dq[j] * scale).astype(jnp.bfloat16)


def attend_back(info, qkv, att, datt, lse):
    blocks, rows, blk = qkv.shape
    third = pl.BlockSpec((blocks, 3 * DH, blk), lambda j, info: (0, info[2], 0))
    return pl.pallas_call(
        functools.partial(attend_back_body, blocks=blocks, blk=blk),
        grid_spec=pltpu.PrefetchScalarGridSpec(
            num_scalar_prefetch=1,
            grid=(blocks,),
            in_specs=[
                third,
                pl.BlockSpec((blocks, DH, blk), lambda j, info: (0, 0, 0)),
                *[pl.BlockSpec((DH, blk), lambda j, info: (info[2], 0))] * blocks,
                pl.BlockSpec((blocks, 1, blk), lambda j, info: (0, 0, 0)),
            ],
            out_specs=pl.BlockSpec((blocks, 3 * DH, blk), lambda j, info: (0, 0, 0)),
            scratch_shapes=[
                pltpu.VMEM((blocks, DH, blk), jnp.float32),
                pltpu.VMEM((blocks, blk, DH), jnp.bfloat16),
                pltpu.VMEM((blocks, blk, DH), jnp.bfloat16),
                pltpu.VMEM((blocks, 1, blk), jnp.float32),
                pltpu.VMEM((blocks, DH, blk), jnp.bfloat16),
            ],
        ),
        out_shape=jax.ShapeDtypeStruct((blocks, 3 * DH, blk), jnp.bfloat16),
        compiler_params=pltpu.CompilerParams(vmem_limit_bytes=18 << 20),
        cost_estimate=SMALL,
        name="attend_back",
    )(info, qkv, att, *datt, lse)


SMALL = pl.CostEstimate(flops=1 << 20, bytes_accessed=1 << 20, transcendentals=0)
GELU_A = 0.7978845608028654
GELU_B = 0.044715


def mlp_body(nm, cot, wu, wd, *refs, begun):
    acc, dnm, dwu, dwd = refs[-4:]

    @pl.when(pl.program_id(0) == 0)
    def _():
        acc[...] = refs[0][...] if begun else jnp.zeros_like(acc)
        dnm[...] = refs[1][...] if begun else jnp.zeros_like(dnm)

    x = nm[...]
    g = cot[...]
    u = jnp.dot(x, wu[...], preferred_element_type=jnp.float32)
    da = dotg(g, wd[...], 1, 1)
    square = u * u
    th = jnp.tanh(GELU_A * u * (1.0 + GELU_B * square))
    half = 0.5 * (1.0 + th)
    a = (u * half).astype(jnp.bfloat16)
    slope = half + 0.5 * u * (1.0 - th * th) * (GELU_A * (1.0 + 3.0 * GELU_B * square))
    du = (da * slope).astype(jnp.bfloat16)
    acc[...] += jnp.dot(a, wd[...], preferred_element_type=jnp.float32)
    dnm[...] += dotg(du, wu[...], 1, 1)
    dwu[...] = dotg(x, du, 0, 0).astype(jnp.bfloat16)
    dwd[...] = dotg(a, g, 0, 0).astype(jnp.bfloat16)


def mlp_part(nm, cot, wu, wd, sums=(), step=256):
    rows, width = nm.shape
    ff = wu.shape[1]
    whole = pl.BlockSpec((rows, width), lambda i: (0, 0))
    up = pl.BlockSpec((width, step), lambda i: (0, i))
    down = pl.BlockSpec((step, width), lambda i: (i, 0))
    return pl.pallas_call(
        functools.partial(mlp_body, begun=bool(sums)),
        grid=(ff // step,),
        in_specs=[whole, whole, up, down] + [whole, whole][: len(sums)],
        out_specs=[whole, whole, up, down],
        out_shape=[
            jax.ShapeDtypeStruct((rows, width), jnp.float32),
            jax.ShapeDtypeStruct((rows, width), jnp.float32),
            jax.ShapeDtypeStruct(wu.shape, jnp.bfloat16),
            jax.ShapeDtypeStruct(wd.shape, jnp.bfloat16),
        ],
        input_output_aliases={4: 0, 5: 1} if sums else {},
        compiler_params=pltpu.CompilerParams(vmem_limit_bytes=26 << 20),
        cost_estimate=SMALL,
        name="mlp_part",
    )(nm, cot, wu, wd, *sums)


ORDER = (0, 2, 1, 3)


def cut(array, axis, steps):
    shape = tuple(n // steps if k == axis else n for k, n in enumerate(array.shape))
    return pl.BlockSpec(shape, lambda i: tuple(i if k == axis else 0 for k in range(len(shape))))


def row_call(body, name, out_shape, place, operands, in_axes, out_axes, steps=1, scratch=()):
    return pl.pallas_call(
        body,
        grid=(steps,),
        in_specs=[pl.BlockSpec(memory_space=pltpu.SMEM)] + [cut(a, k, steps) for a, k in zip(operands, in_axes)],
        out_specs=[cut(a, k, steps) for a, k in zip(out_shape, out_axes)],
        out_shape=out_shape,
        scratch_shapes=scratch,
        compiler_params=pltpu.CompilerParams(vmem_limit_bytes=20 << 20),
        cost_estimate=SMALL,
        name=name,
    )(place, *operands)


def rows_at(place, slot, part):
    return pl.ds(pl.multiple_of((place[0] ^ ORDER[slot]) * part, DH), part)


def project_out_body(place, *refs):
    pieces, (w, inputs, gain, residual, nm) = refs[:-5], refs[-5:]
    part = len(pieces) // 4 * DH
    residual[...] = inputs[...].astype(jnp.float32)
    for s in range(4):
        heads = jnp.concatenate([p[...] for p in pieces[s::4]], axis=0)
        residual[...] += dotg(heads, w[rows_at(place, s, part), :], 0, 0)
    z, _ = norm_stats(residual[...])
    nm[...] = (z * gain[...]).astype(jnp.bfloat16)


def turn_body(place, residual, sum_near, sum_far, grad_near, grad_far, cot, gain, w, *refs):
    result, d_residual, d_branch, d_gain, *d_heads = refs
    part = d_heads[0].shape[0]
    result[...] = (residual[...] + sum_near[...] + sum_far[...].astype(jnp.float32)).astype(jnp.bfloat16)
    z, inverse = norm_stats(residual[...])
    back, gain_part = norm_back(z, inverse, gain[...], grad_near[...] + grad_far[...].astype(jnp.float32))

    @pl.when(pl.program_id(0) == 0)
    def _():
        d_gain[...] = jnp.zeros_like(d_gain)

    d_gain[...] += gain_part
    d_residual[...] = cot[...].astype(jnp.float32) + back
    d_branch[...] = d_residual[...].astype(jnp.bfloat16)
    for s in range(4):
        d_heads[s][...] = dotg(w[rows_at(place, s, part), :], d_branch[...], 1, 1).astype(jnp.bfloat16)


def join_columns_body(place, *refs):
    pieces, out = refs[:4], refs[4]
    part = pieces[0].shape[1]

    def fill(me):
        for s in range(4):
            d = me ^ ORDER[s]
            out[:, d * part : (d + 1) * part] = pieces[s][...]

    for me in range(4):
        pl.when(place[0] == me)(functools.partial(fill, me))


def out_grad_body(place, *refs):
    came, (d_branch, *pieces, out) = refs[:-6], refs[-6:]
    part = len(came) // 4 * DH
    for s in range(4):
        heads = jnp.concatenate([p[...] for p in came[s::4]], axis=0)
        out[rows_at(place, s, part), :] = jnp.dot(
            heads, d_branch[...], preferred_element_type=jnp.float32
        ).astype(jnp.bfloat16)

    def fill(me):
        for s in range(4):
            d = me ^ ORDER[s]
            pieces[s][...] = out[:, d * part : (d + 1) * part]

    for me in range(4):
        pl.when(place[0] == me)(functools.partial(fill, me))


def rows_grad_body(place, *refs):
    *heads, w, out = refs
    for s in range(out.shape[0]):
        grad = jnp.concatenate([h[s] for h in heads], axis=0)
        out[s] = dotg(grad, w[:, : grad.shape[0]], 0, 1).astype(jnp.bfloat16)


def weight_grad_body(place, *refs):
    normed, heads, (*parts, out) = refs[:4], refs[4:-4], refs[-4:]
    total = 0.0
    for s in range(4):
        total += dotg(normed[s][...], jnp.concatenate([h[s] for h in heads], axis=0), 0, 1)
    rest = sum(p[...].astype(jnp.float32) for p in parts).astype(jnp.bfloat16)
    out[...] = jnp.concatenate((total.astype(jnp.bfloat16), rest), axis=1)


def pick_up_body(place, w, out, *, each):
    def fill(me):
        for g in range(out.shape[1] // each):
            out[:, g * each : (g + 1) * each] = w[:, (g * 4 + me) * each : (g * 4 + me + 1) * each]

    for me in range(4):
        pl.when(place[0] == me)(functools.partial(fill, me))


def place_up_body(place, grads, out, *, each):
    for p in range(4):
        for g in range(grads.shape[-1] // each):
            at = (g * 4 + p) * each
            out[:, at : at + each] = grads[p, :, g * each : (g + 1) * each].astype(jnp.float32)


def place_qkv_body(place, grads, qkv, out):
    width = out.shape[1]
    part = width // 4
    heads = part // DH
    for p in range(4):
        out[:, p * part : (p + 1) * part] = grads[p, :, 3 * part :].astype(jnp.float32)
        for h in range(heads):
            for which in range(3):
                at = which * width + (p * heads + h) * DH
                start = (h * 3 + which) * DH
                qkv[:, at : at + DH] = grads[p, :, start : start + DH].astype(jnp.float32)


def swap(value, axis, bit):
    count = lax.axis_size(axis)
    return lax.ppermute(value, axis, [(i, i ^ bit) for i in range(count)])


def bits_of(axis):
    count = lax.axis_size(axis)
    assert count & (count - 1) == 0, "axis size"
    return [1 << b for b in reversed(range(count.bit_length() - 1))]


def is_set(axis, bit):
    return (lax.axis_index(axis) & bit) != 0


def join(own, came, axis, bit, at):
    own, came = (jnp.expand_dims(a, at) for a in (own, came))
    shape = own.shape[:at] + (2,) + own.shape[at + 1 :]
    place = lax.broadcasted_iota(jnp.int32, shape, at)
    return jnp.where(place == is_set(axis, bit).astype(jnp.int32), own, came)


def gather(value, axis, bits, at=0):
    for k, bit in enumerate(bits):
        value = join(value, swap(value, axis, bit), axis, bit, at + k)
    return value


def spread(blocks, bit):
    return blocks | {r ^ bit: swap(b, "seq", bit) for r, b in blocks.items()}


def add(a, b):
    return (a.astype(jnp.float32) + b.astype(jnp.float32)).astype(a.dtype)


def fold(blocks, bit):
    return {r: add(b, swap(blocks[r ^ bit], "seq", bit)) for r, b in blocks.items() if not r & bit}


def halve(value, axis, bit, at, *more):
    mine = is_set(axis, bit).astype(jnp.int32)
    part = lambda which: functools.reduce(
        add, [lax.dynamic_index_in_dim(v, which, at, keepdims=False) for v in (value, *more)]
    )
    return part(mine), swap(part(1 - mine), axis, bit)


def norm_stats(values):
    centre = jnp.mean(values, axis=-1, keepdims=True)
    shifted = values - centre
    spread_of = jnp.mean(shifted * shifted, axis=-1, keepdims=True)
    inverse = lax.rsqrt(spread_of + EPSILON)
    return shifted * inverse, inverse


def norm_back(z, inverse, gain, grad):
    e = grad * gain
    back = (e - jnp.mean(e, axis=-1, keepdims=True) - z * jnp.mean(e * z, axis=-1, keepdims=True)) * inverse
    return back, jnp.sum(grad * z, axis=0, keepdims=True)


def pick_at(value, at):
    return lax.dynamic_index_in_dim(value, at, 1, keepdims=False)


def after(first, *values):
    return lax.optimization_barrier((first, values))[1]


def per_device(
    tokens, pass_index, lengths, table, gain_attn, w_qkv, w_out, gain_mlp, w_up, w_down, cotangent
):
    bf16, f32 = jnp.bfloat16, jnp.float32
    groups, parts = lax.axis_size("fsdp"), lax.axis_size("seq")
    local_len, seq_total, width = tokens.shape
    assert seq_total == groups and parts == 4
    heads = HEADS // parts
    part = width // parts
    ff = w_up.shape[1]
    own_rows = width // groups
    ff_each = ff // groups // parts
    me, group = lax.axis_index("seq"), lax.axis_index("fsdp")
    f_bits = bits_of("fsdp")
    last = len(f_bits) - 1
    top, low, between = f_bits[0], f_bits[-1], f_bits[1:-1]
    sizes = (2,) * len(f_bits)
    span = local_len * groups
    pick = lambda a, at: lax.dynamic_index_in_dim(a, me, at, keepdims=False)
    deal = lambda a: lax.all_to_all(a, "fsdp", split_axis=0, concat_axis=0, tiled=True)
    across = lambda a: [a[0]] + [swap(a[s], "seq", r) for s, r in enumerate(ORDER) if r]

    chooser = (pass_index[..., None] == jnp.arange(table.shape[0], dtype=jnp.int32)).astype(bf16)
    embedded = jnp.einsum("pnc,cd->npd", chooser, table, preferred_element_type=f32)
    summed = (jnp.swapaxes(tokens, 0, 1).astype(f32) + embedded).astype(bf16)
    inputs = deal(summed).reshape(span, width)
    qkv_slice = pick(w_qkv.reshape(own_rows, 3, parts, heads, DH), 2)
    qkv_slice = jnp.swapaxes(qkv_slice, 1, 2).reshape(own_rows, 3 * part)
    out_slice = pick(w_out.reshape(own_rows, parts, part), 1)
    gains = jnp.stack((gain_attn, gain_mlp), axis=1)
    qkv_slice, out_slice = after(summed, qkv_slice, out_slice)
    packet = jnp.concatenate((qkv_slice, out_slice, gains, jnp.zeros((own_rows, 126), bf16)), axis=1)
    packet_came = swap(packet, "fsdp", top)
    place = me.astype(jnp.int32)[None]
    (up,) = row_call(
        functools.partial(pick_up_body, each=ff_each), "pick_up",
        [jax.ShapeDtypeStruct((own_rows, ff // parts), bf16)], place, [w_up], [None], [None],
    )
    down = pick(w_down.reshape(parts, ff_each, width), 0)
    pair = jnp.stack((up, down))

    rows_2, rows_1 = swap(inputs, "seq", 2), swap(inputs, "seq", 1)
    rows = (inputs, rows_2, rows_1, swap(rows_2, "seq", 1))
    packet, packet_came, pair = after(inputs, packet, packet_came, pair)
    packet = gather(join(packet, packet_came, "fsdp", top, 0), "fsdp", between, 1)
    packet, pair = lax.optimization_barrier((packet, pair))
    packet = gather(packet, "fsdp", (low,), last).reshape(width, -1)
    wq = packet[:, : 3 * part]
    out_cols = packet[:, 3 * part : width]
    gain_one = packet[:, width].astype(f32)
    gain_two = packet[:, width + 1].astype(f32)
    pair_came = swap(pair, "fsdp", top)
    marks = jnp.swapaxes(pass_index, 0, 1)[..., None].astype(bf16)
    cot_packet = jnp.concatenate(
        (jnp.swapaxes(cotangent, 0, 1), jnp.broadcast_to(marks, marks.shape[:2] + (128,))), axis=2
    )

    normed = [(norm_stats(b.astype(f32))[0] * gain_one).astype(bf16) for b in rows]
    pair, pair_came, out_cols = after(rows[3], pair, pair_came, out_cols)
    pair = join(pair, pair_came, "fsdp", top, 1)
    pair = gather(pair, "fsdp", between, 2)
    out_2 = swap(out_cols, "seq", 2)
    qkv = jnp.stack([dotg(wq, b, 0, 1).astype(bf16) for b in normed])
    length = lax.dynamic_index_in_dim(lengths, group, 0, keepdims=False)
    slot = (me & 1) * 2 + (me >> 1)
    info = [jnp.stack((slot, length, jnp.int32(h))).astype(jnp.int32) for h in range(heads)]

    att, lse, crossed, many = [None] * heads, [None] * heads, [None] * heads, heads - 1
    att[1], lse[1] = attend(info[1], qkv)
    pair, out_cols, out_2, cot_packet = after(att[1], pair, out_cols, out_2, cot_packet)
    up, down = pair[0], pair[1]
    (qkv,) = after((up, down), qkv)
    cot_packet = deal(cot_packet).reshape(span, -1)
    up_came = swap(up, "fsdp", low)
    down_2 = swap(down, "seq", 2)
    out_1, out_3 = swap(out_cols, "seq", 1), swap(out_2, "seq", 1)
    for h in range(2, heads):
        att[h], lse[h] = attend(info[h], qkv)
    att[1:], out_1, out_3, down = lax.optimization_barrier((att[1:], out_1, out_3, down))
    square = jax.ShapeDtypeStruct((width, width), bf16)
    (w_out_full,) = row_call(
        join_columns_body, "join_columns", [square], place, [out_cols, out_2, out_1, out_3], [None] * 4, [None]
    )
    (qkv,) = after((att[1:], w_out_full), qkv)
    crossed[1:] = [across(a) for a in att[1:]]
    down_came = swap(down, "fsdp", low)
    att[0], lse[0] = attend(info[0], qkv)
    up, up_came, down_2, att[0], crossed[1:] = lax.optimization_barrier((up, up_came, down_2, att[0], crossed[1:]))
    crossed[0] = across(att[0])
    up = join(up, up_came, "fsdp", low, last).reshape(width, ff // parts)

    crossed[0], up, down, down_came, down_2, cot_packet = lax.optimization_barrier(
        (crossed[0], up, down, down_came, down_2, cot_packet)
    )
    crossed = [piece for pieces in crossed for piece in pieces]
    up_2 = swap(up, "seq", 2)
    cot = cot_packet[:, :width]
    passes = cot_packet[:, width]
    cot_far = swap(cot, "seq", 1)
    down_2_came = swap(down_2, "fsdp", low)
    down = join(down, down_came, "fsdp", low, last).reshape(ff // parts, width)
    rows_f32 = jax.ShapeDtypeStruct((span, width), f32)
    rows_bf16 = jax.ShapeDtypeStruct((span, width), bf16)
    residual, nm = row_call(
        project_out_body, "project_out", [rows_f32, rows_bf16], place,
        [*crossed, w_out_full, inputs, gain_two[None]], [1] * len(crossed) + [None, 0, None], [0, 0], parts,
    )
    nm_far = swap(nm, "seq", 1)
    *near, up_0, down_0 = mlp_part(nm, cot, up, down)
    *far, up_1, down_1 = mlp_part(nm_far, cot_far, up, down)
    down_2, down_2_came, up_2 = after(far[0], down_2, down_2_came, up_2)
    down_2 = join(down_2, down_2_came, "fsdp", low, last).reshape(ff // parts, width)
    *far, d_up_2, d_down_2 = mlp_part(nm_far, cot_far, up_2, down_2, far)
    far = [swap(a.astype(bf16), "seq", 1) for a in far]
    *near, up_2, down_2 = mlp_part(nm, cot, up_2, down_2, near)
    up_2 = add(up_2, d_up_2)
    down = jnp.stack((add(down_0, down_1), add(down_2, d_down_2))).reshape(2, *sizes, ff_each, width)
    down = halve(down, "fsdp", low, last + 1)
    head_rows = jax.ShapeDtypeStruct((part, span), bf16)
    result, d_residual, d_branch, d_gain_mlp, *d_heads = row_call(
        turn_body,
        "turn",
        [rows_bf16, rows_f32, rows_bf16, jax.ShapeDtypeStruct((1, width), f32)] + [head_rows] * parts,
        place,
        [residual, near[0], far[0], near[1], far[1], cot, gain_two[None], w_out_full],
        [0] * 6 + [None] * 2,
        [0, 0, 0, None] + [1] * parts,
        parts,
    )
    d_heads = across(d_heads)
    piece = jax.ShapeDtypeStruct((width, part), bf16)
    d_out, d_out_x, *d_out_far = row_call(
        out_grad_body, "out_grad", [piece] * 4, place, [*crossed, d_branch], [None] * (len(crossed) + 1), [None] * 4,
        scratch=[pltpu.VMEM((width, width), bf16)],
    )
    d_heads, d_out, d_out_x, d_out_far, up_0, up_1, up_2, result = lax.optimization_barrier(
        (d_heads, d_out, d_out_x, d_out_far, up_0, up_1, up_2, result)
    )

    up_came = swap(up_2, "seq", 2)
    out_back = deal(result.reshape(groups, local_len, width))
    d_out_1, d_out_3 = [swap(a, "seq", 1) for a in d_out_far]
    d_qkv = [attend_back(info[0], qkv, att[0], d_heads, lse[0])]
    down, d_out_x, d_out_3 = after(d_qkv, down, d_out_x, d_out_3)
    down = halve(down[0], "fsdp", f_bits[-2], last, down[1])
    d_out_x = add(d_out_x, d_out_3)
    d_heads = after((down[0], d_out_x), d_heads)[0]
    d_out_x = swap(d_out_x, "seq", 2)
    for h in range(1, many):
        d_qkv.append(attend_back(info[h], qkv, att[h], d_heads, lse[h]))
    up_0, up_1, up_came, down, d_out_x, out_back = after(d_qkv, up_0, up_1, up_came, down, d_out_x, out_back)
    split = lambda a: a.reshape(*sizes, own_rows, ff // parts)
    up = halve(split(up_0), "fsdp", low, last, split(up_1), split(up_came))
    for k in reversed(range(last - 1)):
        down = halve(down[0], "fsdp", f_bits[k], k + 1, down[1])
    (d_heads,) = after((up[0], down[0], out_back), d_heads)
    d_qkv.append(attend_back(info[many], qkv, att[many], d_heads, lse[many]))
    d_qkv, down, up = lax.optimization_barrier((d_qkv, down, up))

    half = jax.ShapeDtypeStruct((2, span, width), bf16)
    project_back = lambda a: row_call(rows_grad_body, "rows_grad", [half], place, [*a, packet], [None] * (heads + 1), [None])[0]
    d_far = swap(project_back([d[2:] for d in d_qkv]), "seq", 1)
    d_near = project_back([d[:2] for d in d_qkv])
    (d_tail,) = after(d_near, d_qkv)
    down = add(*down)
    up = halve(up[0], "fsdp", f_bits[-2], last - 1, up[1])
    (d_wq,) = row_call(
        weight_grad_body, "weight_grad", [square], place, [*normed, *d_tail, d_out, d_out_1, d_out_x],
        [None] * (7 + heads), [None],
    )
    d_near, d_wq, up = lax.optimization_barrier((d_near, d_wq, up))
    d_wq = halve(d_wq.reshape(*sizes, own_rows, width), "fsdp", low, last)
    for k in reversed(range(last - 1)):
        up = halve(up[0], "fsdp", f_bits[k], k, up[1])
    (d_near,) = after(up[0], d_near)
    d_near = add(d_near, d_far)
    d_came = swap(d_near[1], "seq", 2)
    d_wq = halve(d_wq[0], "fsdp", f_bits[-2], last - 1, d_wq[1])
    d_wq, down = after(d_came, d_wq, down)
    down_came = swap(down[1], "seq", 2)
    for k in reversed(range(last - 1)):
        d_wq = halve(d_wq[0], "fsdp", f_bits[k], k, d_wq[1])
    d_normed = d_near[0].astype(f32) + d_came.astype(f32)
    z_one, inverse_one = norm_stats(inputs.astype(f32))
    d_in_norm, d_gain_attn = norm_back(z_one, inverse_one, gain_one, d_normed)
    d_inputs = (d_residual + d_in_norm).astype(bf16)
    d_back = deal(d_inputs.reshape(groups, local_len, width))
    up, d_wq = after(d_inputs, up, d_wq)
    (d_wq,) = after(d_back, d_wq)
    pair = jnp.stack((add(*up), add(down[0], down_came)))
    grads = gather(pair, "seq", (2, 1)).reshape(parts, 2, own_rows, width)
    (g_up,) = row_call(
        functools.partial(place_up_body, each=ff_each), "place_up",
        [jax.ShapeDtypeStruct((own_rows, ff), f32)], place, [grads[:, 0]], [None], [None],
    )
    g_down = grads[:, 1].reshape(ff // groups, width).astype(f32)

    count = table.shape[0]
    picks = (passes[None, :] == jnp.arange(count, dtype=jnp.int32)[:, None].astype(bf16)).astype(bf16)
    d_table = jnp.dot(picks, d_inputs, preferred_element_type=f32)
    small = jnp.concatenate((d_table, d_gain_attn, d_gain_mlp, jnp.zeros_like(d_gain_mlp)), axis=0)
    for bit in (1, 2):
        small = small + swap(small, "seq", bit)
    for bit in reversed(f_bits[1:]):
        small = small + swap(small, "fsdp", bit)
    (small,) = after(d_back, small)
    small = small + swap(small, "fsdp", top)
    owned_gain = lambda row: lax.dynamic_slice_in_dim(small[row], group * own_rows, own_rows)

    d_wq = gather(add(*d_wq), "seq", (2, 1)).reshape(parts, own_rows, width)
    g_qkv, g_out = row_call(
        place_qkv_body, "place_qkv",
        [jax.ShapeDtypeStruct((own_rows, 3 * width), f32), jax.ShapeDtypeStruct((own_rows, width), f32)],
        place, [d_wq], [None], [None] * 2,
    )
    return (
        jnp.swapaxes(out_back, 0, 1),
        jnp.swapaxes(d_back, 0, 1),
        small[:count],
        owned_gain(count),
        g_qkv,
        g_out,
        owned_gain(count + 1),
        g_up,
        g_down,
    )


def solution(mesh):
    return jax.shard_map(
        per_device,
        mesh=mesh,
        in_specs=(
            P(("seq", "fsdp"), None, None),
            P(("seq", "fsdp"), None),
            P(),
            P(),
            P("fsdp"),
            P("fsdp", None),
            P("fsdp", None),
            P("fsdp"),
            P("fsdp", None),
            P("fsdp", None),
            P(("seq", "fsdp"), None, None),
        ),
        out_specs=(
            P(("seq", "fsdp"), None, None),
            P(("seq", "fsdp"), None, None),
            P(),
            P("fsdp"),
            P("fsdp", None),
            P("fsdp", None),
            P("fsdp"),
            P("fsdp", None),
            P("fsdp", None),
        ),
        check_vma=False,
    )
```

```python
import functools

import jax
import jax.numpy as jnp
from jax import lax
from jax.experimental import pallas as pl
from jax.experimental.pallas import tpu as pltpu
from jax.sharding import PartitionSpec as P

HEADS = 12
EPSILON = 1e-05
LOG2E = 1.4426950408889634
LN2 = 0.6931471805599453
MASKED = -1e30
DH = 64


def dotg(a, b, ca, cb):
    return lax.dot_general(a, b, (((ca,), (cb,)), ((), ())), preferred_element_type=jnp.float32)


def slot_of(block, info):
    return (((block & 1) << 1) | (block >> 1)) ^ info[0]


def attend_body(info, qkv, *refs, blk):
    out, lse, acc = refs[-3:]
    i = pl.program_id(0)
    length = info[1]
    qt = qkv[slot_of(i, info), 0:DH, :]
    scale = DH ** -0.5 * LOG2E

    def step(j, carry, masked):
        top, tot = carry
        kt = qkv[slot_of(j, info), DH : 2 * DH, :]
        vt = qkv[slot_of(j, info), 2 * DH : 3 * DH, :]
        st = dotg(kt, qt, 0, 0) * scale
        if masked:
            key_at = j * blk + lax.broadcasted_iota(jnp.int32, st.shape, 0)
            query_at = i * blk + lax.broadcasted_iota(jnp.int32, st.shape, 1)
            st = jnp.where((query_at >= key_at) & (key_at < length), st, MASKED)
        new_top = jnp.maximum(top, jnp.max(st, axis=0, keepdims=True))
        fade = jnp.exp2(top - new_top)
        pt = jnp.exp2(st - new_top)
        tot = tot * fade + jnp.sum(pt, axis=0, keepdims=True)
        acc[...] = acc[...] * fade + dotg(vt, pt.astype(jnp.bfloat16), 1, 0)
        return new_top, tot

    acc[...] = jnp.zeros_like(acc)
    carry = (jnp.full((1, blk), MASKED, jnp.float32), jnp.zeros((1, blk), jnp.float32))
    plain = jnp.minimum(i, length // blk)
    stop = jnp.minimum(i + 1, (length + blk - 1) // blk)
    carry = lax.fori_loop(0, plain, functools.partial(step, masked=False), carry)
    top, tot = lax.fori_loop(plain, stop, functools.partial(step, masked=True), carry)
    out[0] = (acc[...] / tot).astype(jnp.bfloat16)
    lse[0] = top + jnp.log2(tot)


def attend(info, qkv):
    blocks, _, blk = qkv.shape
    return pl.pallas_call(
        functools.partial(attend_body, blk=blk),
        grid_spec=pltpu.PrefetchScalarGridSpec(
            num_scalar_prefetch=1,
            grid=(blocks,),
            in_specs=[pl.BlockSpec((blocks, 3 * DH, blk), lambda i, info: (0, info[2], 0))],
            out_specs=[
                pl.BlockSpec((1, DH, blk), lambda i, info: (slot_of(i, info), 0, 0)),
                pl.BlockSpec((1, 1, blk), lambda i, info: (i, 0, 0)),
            ],
            scratch_shapes=[pltpu.VMEM((DH, blk), jnp.float32)],
        ),
        out_shape=[
            jax.ShapeDtypeStruct((blocks, DH, blk), jnp.bfloat16),
            jax.ShapeDtypeStruct((blocks, 1, blk), jnp.float32),
        ],
        compiler_params=pltpu.CompilerParams(vmem_limit_bytes=16 << 20),
        cost_estimate=SMALL,
        name="attend",
    )(info, qkv)


def attend_back_body(info, qkv, att, *refs, blocks, blk):
    came, (lse, dqkv, dq, q_rows, do_rows, delta, datt) = refs[:blocks], refs[blocks:]
    j = pl.program_id(0)
    length = info[1]
    scale = DH ** -0.5
    at_q, at_k, at_v = slice(0, DH), slice(DH, 2 * DH), slice(2 * DH, 3 * DH)

    @pl.when(j == 0)
    def _():
        dq[...] = jnp.zeros_like(dq)
        for b in range(blocks):
            datt[b] = came[b][...]
        for b in range(blocks):
            at = slot_of(b, info)
            dt = datt[at]
            q_rows[b] = qkv[at, at_q, :].T
            do_rows[b] = dt.T
            delta[b] = jnp.sum(dt.astype(jnp.float32) * att[at].astype(jnp.float32), axis=0, keepdims=True)

    kt = qkv[slot_of(j, info), at_k, :]
    vt = qkv[slot_of(j, info), at_v, :]
    k_rows = kt.T
    v_rows = vt.T

    def step(i, carry, masked):
        dk, dv = carry
        qt = qkv[slot_of(i, info), at_q, :]
        st = jnp.dot(k_rows, qt, preferred_element_type=jnp.float32)
        pt = jnp.exp2(st * (scale * LOG2E) - lse[i])
        if masked:
            key_at = j * blk + lax.broadcasted_iota(jnp.int32, st.shape, 0)
            query_at = i * blk + lax.broadcasted_iota(jnp.int32, st.shape, 1)
            pt = jnp.where((query_at >= key_at) & (key_at < length), pt, 0.0)
        dpt = jnp.dot(v_rows, datt[slot_of(i, info)], preferred_element_type=jnp.float32)
        dst = (pt * (dpt - delta[i])).astype(jnp.bfloat16)
        dv = dv + jnp.dot(pt.astype(jnp.bfloat16), do_rows[i], preferred_element_type=jnp.float32)
        dk = dk + jnp.dot(dst, q_rows[i], preferred_element_type=jnp.float32)
        dq[i] = dq[i] + jnp.dot(kt, dst, preferred_element_type=jnp.float32)
        return dk, dv

    zero = jnp.zeros((blk, DH), jnp.float32)
    whole = (j + 1) * blk <= length
    some = j * blk < length
    masked_end = jnp.where(some, jnp.where(whole, j + 1, blocks), j)
    carry = lax.fori_loop(j, masked_end, functools.partial(step, masked=True), (zero, zero))
    dk, dv = lax.fori_loop(
        jnp.where(whole, j + 1, blocks), blocks, functools.partial(step, masked=False), carry
    )
    dqkv[slot_of(j, info), at_k, :] = (dk * scale).astype(jnp.bfloat16).T
    dqkv[slot_of(j, info), at_v, :] = dv.astype(jnp.bfloat16).T
    dqkv[slot_of(j, info), at_q, :] = (dq[j] * scale).astype(jnp.bfloat16)


def attend_back(info, qkv, att, datt, lse):
    blocks, rows, blk = qkv.shape
    third = pl.BlockSpec((blocks, 3 * DH, blk), lambda j, info: (0, info[2], 0))
    return pl.pallas_call(
        functools.partial(attend_back_body, blocks=blocks, blk=blk),
        grid_spec=pltpu.PrefetchScalarGridSpec(
            num_scalar_prefetch=1,
            grid=(blocks,),
            in_specs=[
                third,
                pl.BlockSpec((blocks, DH, blk), lambda j, info: (0, 0, 0)),
                *[pl.BlockSpec((DH, blk), lambda j, info: (info[2], 0))] * blocks,
                pl.BlockSpec((blocks, 1, blk), lambda j, info: (0, 0, 0)),
            ],
            out_specs=pl.BlockSpec((blocks, 3 * DH, blk), lambda j, info: (0, 0, 0)),
            scratch_shapes=[
                pltpu.VMEM((blocks, DH, blk), jnp.float32),
                pltpu.VMEM((blocks, blk, DH), jnp.bfloat16),
                pltpu.VMEM((blocks, blk, DH), jnp.bfloat16),
                pltpu.VMEM((blocks, 1, blk), jnp.float32),
                pltpu.VMEM((blocks, DH, blk), jnp.bfloat16),
            ],
        ),
        out_shape=jax.ShapeDtypeStruct((blocks, 3 * DH, blk), jnp.bfloat16),
        compiler_params=pltpu.CompilerParams(vmem_limit_bytes=18 << 20),
        cost_estimate=SMALL,
        name="attend_back",
    )(info, qkv, att, *datt, lse)


SMALL = pl.CostEstimate(flops=1 << 20, bytes_accessed=1 << 20, transcendentals=0)
GELU_A = 0.7978845608028654
GELU_B = 0.044715


def mlp_body(nm, cot, wu, wd, *refs, begun):
    acc, dnm, dwu, dwd = refs[-4:]

    @pl.when(pl.program_id(0) == 0)
    def _():
        acc[...] = refs[0][...] if begun else jnp.zeros_like(acc)
        dnm[...] = refs[1][...] if begun else jnp.zeros_like(dnm)

    x = nm[...]
    g = cot[...]
    u = jnp.dot(x, wu[...], preferred_element_type=jnp.float32)
    da = dotg(g, wd[...], 1, 1)
    square = u * u
    th = jnp.tanh(GELU_A * u * (1.0 + GELU_B * square))
    half = 0.5 * (1.0 + th)
    a = (u * half).astype(jnp.bfloat16)
    slope = half + 0.5 * u * (1.0 - th * th) * (GELU_A * (1.0 + 3.0 * GELU_B * square))
    du = (da * slope).astype(jnp.bfloat16)
    acc[...] += jnp.dot(a, wd[...], preferred_element_type=jnp.float32)
    dnm[...] += dotg(du, wu[...], 1, 1)
    dwu[...] = dotg(x, du, 0, 0).astype(jnp.bfloat16)
    dwd[...] = dotg(a, g, 0, 0).astype(jnp.bfloat16)


def mlp_part(nm, cot, wu, wd, sums=(), step=256):
    rows, width = nm.shape
    ff = wu.shape[1]
    whole = pl.BlockSpec((rows, width), lambda i: (0, 0))
    up = pl.BlockSpec((width, step), lambda i: (0, i))
    down = pl.BlockSpec((step, width), lambda i: (i, 0))
    return pl.pallas_call(
        functools.partial(mlp_body, begun=bool(sums)),
        grid=(ff // step,),
        in_specs=[whole, whole, up, down] + [whole, whole][: len(sums)],
        out_specs=[whole, whole, up, down],
        out_shape=[
            jax.ShapeDtypeStruct((rows, width), jnp.float32),
            jax.ShapeDtypeStruct((rows, width), jnp.float32),
            jax.ShapeDtypeStruct(wu.shape, jnp.bfloat16),
            jax.ShapeDtypeStruct(wd.shape, jnp.bfloat16),
        ],
        input_output_aliases={4: 0, 5: 1} if sums else {},
        compiler_params=pltpu.CompilerParams(vmem_limit_bytes=26 << 20),
        cost_estimate=SMALL,
        name="mlp_part",
    )(nm, cot, wu, wd, *sums)


ORDER = (0, 2, 1, 3)


def cut(array, axis, steps):
    shape = tuple(n // steps if k == axis else n for k, n in enumerate(array.shape))
    return pl.BlockSpec(shape, lambda i: tuple(i if k == axis else 0 for k in range(len(shape))))


def row_call(body, name, out_shape, place, operands, in_axes, out_axes, steps=1, scratch=()):
    return pl.pallas_call(
        body,
        grid=(steps,),
        in_specs=[pl.BlockSpec(memory_space=pltpu.SMEM)] + [cut(a, k, steps) for a, k in zip(operands, in_axes)],
        out_specs=[cut(a, k, steps) for a, k in zip(out_shape, out_axes)],
        out_shape=out_shape,
        scratch_shapes=scratch,
        compiler_params=pltpu.CompilerParams(vmem_limit_bytes=20 << 20),
        cost_estimate=SMALL,
        name=name,
    )(place, *operands)


def rows_at(place, slot, part):
    return pl.ds(pl.multiple_of((place[0] ^ ORDER[slot]) * part, DH), part)


def project_out_body(place, *refs):
    pieces, (w, inputs, gain, residual, nm) = refs[:-5], refs[-5:]
    part = len(pieces) // 4 * DH
    residual[...] = inputs[...].astype(jnp.float32)
    for s in range(4):
        heads = jnp.concatenate([p[...] for p in pieces[s::4]], axis=0)
        residual[...] += dotg(heads, w[rows_at(place, s, part), :], 0, 0)
    z, _ = norm_stats(residual[...])
    nm[...] = (z * gain[...]).astype(jnp.bfloat16)


def turn_body(place, residual, sum_near, sum_far, grad_near, grad_far, cot, gain, w, *refs):
    result, d_residual, d_branch, d_gain, *d_heads = refs
    part = d_heads[0].shape[0]
    result[...] = (residual[...] + sum_near[...] + sum_far[...].astype(jnp.float32)).astype(jnp.bfloat16)
    z, inverse = norm_stats(residual[...])
    back, gain_part = norm_back(z, inverse, gain[...], grad_near[...] + grad_far[...].astype(jnp.float32))

    @pl.when(pl.program_id(0) == 0)
    def _():
        d_gain[...] = jnp.zeros_like(d_gain)

    d_gain[...] += gain_part
    d_residual[...] = cot[...].astype(jnp.float32) + back
    d_branch[...] = d_residual[...].astype(jnp.bfloat16)
    for s in range(4):
        d_heads[s][...] = dotg(w[rows_at(place, s, part), :], d_branch[...], 1, 1).astype(jnp.bfloat16)


def join_columns_body(place, *refs):
    pieces, out = refs[:4], refs[4]
    part = pieces[0].shape[1]

    def fill(me):
        for s in range(4):
            d = me ^ ORDER[s]
            out[:, d * part : (d + 1) * part] = pieces[s][...]

    for me in range(4):
        pl.when(place[0] == me)(functools.partial(fill, me))


def out_grad_body(place, *refs):
    came, (d_branch, *pieces, out) = refs[:-6], refs[-6:]
    part = len(came) // 4 * DH
    for s in range(4):
        heads = jnp.concatenate([p[...] for p in came[s::4]], axis=0)
        out[rows_at(place, s, part), :] = jnp.dot(
            heads, d_branch[...], preferred_element_type=jnp.float32
        ).astype(jnp.bfloat16)

    def fill(me):
        for s in range(4):
            d = me ^ ORDER[s]
            pieces[s][...] = out[:, d * part : (d + 1) * part]

    for me in range(4):
        pl.when(place[0] == me)(functools.partial(fill, me))


def rows_grad_body(place, *refs):
    *heads, w, out = refs
    for s in range(out.shape[0]):
        grad = jnp.concatenate([h[s] for h in heads], axis=0)
        out[s] = dotg(grad, w[:, : grad.shape[0]], 0, 1).astype(jnp.bfloat16)


def weight_grad_body(place, *refs):
    normed, heads, (*parts, out) = refs[:4], refs[4:-4], refs[-4:]
    total = 0.0
    for s in range(4):
        total += dotg(normed[s][...], jnp.concatenate([h[s] for h in heads], axis=0), 0, 1)
    rest = sum(p[...].astype(jnp.float32) for p in parts).astype(jnp.bfloat16)
    out[...] = jnp.concatenate((total.astype(jnp.bfloat16), rest), axis=1)


def pick_up_body(place, w, out, *, each):
    def fill(me):
        for g in range(out.shape[1] // each):
            out[:, g * each : (g + 1) * each] = w[:, (g * 4 + me) * each : (g * 4 + me + 1) * each]

    for me in range(4):
        pl.when(place[0] == me)(functools.partial(fill, me))


def place_up_body(place, grads, out, *, each):
    for p in range(4):
        for g in range(grads.shape[-1] // each):
            at = (g * 4 + p) * each
            out[:, at : at + each] = grads[p, :, g * each : (g + 1) * each].astype(jnp.float32)


def place_qkv_body(place, grads, qkv, out):
    width = out.shape[1]
    part = width // 4
    heads = part // DH
    for p in range(4):
        out[:, p * part : (p + 1) * part] = grads[p, :, 3 * part :].astype(jnp.float32)
        for h in range(heads):
            for which in range(3):
                at = which * width + (p * heads + h) * DH
                start = (h * 3 + which) * DH
                qkv[:, at : at + DH] = grads[p, :, start : start + DH].astype(jnp.float32)


def swap(value, axis, bit):
    count = lax.axis_size(axis)
    return lax.ppermute(value, axis, [(i, i ^ bit) for i in range(count)])


def bits_of(axis):
    count = lax.axis_size(axis)
    assert count & (count - 1) == 0, "axis size"
    return [1 << b for b in reversed(range(count.bit_length() - 1))]


def is_set(axis, bit):
    return (lax.axis_index(axis) & bit) != 0


def join(own, came, axis, bit, at):
    own, came = (jnp.expand_dims(a, at) for a in (own, came))
    shape = own.shape[:at] + (2,) + own.shape[at + 1 :]
    place = lax.broadcasted_iota(jnp.int32, shape, at)
    return jnp.where(place == is_set(axis, bit).astype(jnp.int32), own, came)


def gather(value, axis, bits, at=0):
    for k, bit in enumerate(bits):
        value = join(value, swap(value, axis, bit), axis, bit, at + k)
    return value


def spread(blocks, bit):
    return blocks | {r ^ bit: swap(b, "seq", bit) for r, b in blocks.items()}


def add(a, b):
    return (a.astype(jnp.float32) + b.astype(jnp.float32)).astype(a.dtype)


def fold(blocks, bit):
    return {r: add(b, swap(blocks[r ^ bit], "seq", bit)) for r, b in blocks.items() if not r & bit}


def halve(value, axis, bit, at, *more):
    mine = is_set(axis, bit).astype(jnp.int32)
    part = lambda which: functools.reduce(
        add, [lax.dynamic_index_in_dim(v, which, at, keepdims=False) for v in (value, *more)]
    )
    return part(mine), swap(part(1 - mine), axis, bit)


def norm_stats(values):
    centre = jnp.mean(values, axis=-1, keepdims=True)
    shifted = values - centre
    spread_of = jnp.mean(shifted * shifted, axis=-1, keepdims=True)
    inverse = lax.rsqrt(spread_of + EPSILON)
    return shifted * inverse, inverse


def norm_back(z, inverse, gain, grad):
    e = grad * gain
    back = (e - jnp.mean(e, axis=-1, keepdims=True) - z * jnp.mean(e * z, axis=-1, keepdims=True)) * inverse
    return back, jnp.sum(grad * z, axis=0, keepdims=True)


def pick_at(value, at):
    return lax.dynamic_index_in_dim(value, at, 1, keepdims=False)


def after(first, *values):
    return lax.optimization_barrier((first, values))[1]


def per_device(
    tokens, pass_index, lengths, table, gain_attn, w_qkv, w_out, gain_mlp, w_up, w_down, cotangent
):
    bf16, f32 = jnp.bfloat16, jnp.float32
    groups, parts = lax.axis_size("fsdp"), lax.axis_size("seq")
    local_len, seq_total, width = tokens.shape
    assert seq_total == groups and parts == 4
    heads = HEADS // parts
    part = width // parts
    ff = w_up.shape[1]
    own_rows = width // groups
    ff_each = ff // groups // parts
    me, group = lax.axis_index("seq"), lax.axis_index("fsdp")
    f_bits = bits_of("fsdp")
    last = len(f_bits) - 1
    top, low, between = f_bits[0], f_bits[-1], f_bits[1:-1]
    sizes = (2,) * len(f_bits)
    span = local_len * groups
    pick = lambda a, at: lax.dynamic_index_in_dim(a, me, at, keepdims=False)
    deal = lambda a: lax.all_to_all(a, "fsdp", split_axis=0, concat_axis=0, tiled=True)
    across = lambda a: [a[0]] + [swap(a[s], "seq", r) for s, r in enumerate(ORDER) if r]

    chooser = (pass_index[..., None] == jnp.arange(table.shape[0], dtype=jnp.int32)).astype(bf16)
    embedded = jnp.einsum("pnc,cd->npd", chooser, table, preferred_element_type=f32)
    summed = (jnp.swapaxes(tokens, 0, 1).astype(f32) + embedded).astype(bf16)
    inputs = deal(summed).reshape(span, width)
    qkv_slice = pick(w_qkv.reshape(own_rows, 3, parts, heads, DH), 2)
    qkv_slice = jnp.swapaxes(qkv_slice, 1, 2).reshape(own_rows, 3 * part)
    out_slice = pick(w_out.reshape(own_rows, parts, part), 1)
    gains = jnp.stack((gain_attn, gain_mlp), axis=1)
    qkv_slice, out_slice = after(summed, qkv_slice, out_slice)
    packet = jnp.concatenate((qkv_slice, out_slice, gains, jnp.zeros((own_rows, 126), bf16)), axis=1)
    packet_came = swap(packet, "fsdp", top)
    place = me.astype(jnp.int32)[None]
    (up,) = row_call(
        functools.partial(pick_up_body, each=ff_each), "pick_up",
        [jax.ShapeDtypeStruct((own_rows, ff // parts), bf16)], place, [w_up], [None], [None],
    )
    down = pick(w_down.reshape(parts, ff_each, width), 0)
    pair = jnp.stack((up, down))

    rows_2, rows_1 = swap(inputs, "seq", 2), swap(inputs, "seq", 1)
    rows = (inputs, rows_2, rows_1, swap(rows_2, "seq", 1))
    packet, packet_came, pair = after(inputs, packet, packet_came, pair)
    packet = gather(join(packet, packet_came, "fsdp", top, 0), "fsdp", between, 1)
    packet, pair = lax.optimization_barrier((packet, pair))
    packet = gather(packet, "fsdp", (low,), last).reshape(width, -1)
    wq = packet[:, : 3 * part]
    out_cols = packet[:, 3 * part : width]
    gain_one = packet[:, width].astype(f32)
    gain_two = packet[:, width + 1].astype(f32)
    pair_came = swap(pair, "fsdp", top)
    marks = jnp.swapaxes(pass_index, 0, 1)[..., None].astype(bf16)
    cot_packet = jnp.concatenate(
        (jnp.swapaxes(cotangent, 0, 1), jnp.broadcast_to(marks, marks.shape[:2] + (128,))), axis=2
    )

    normed = [(norm_stats(b.astype(f32))[0] * gain_one).astype(bf16) for b in rows]
    pair, pair_came, out_cols = after(rows[3], pair, pair_came, out_cols)
    pair = join(pair, pair_came, "fsdp", top, 1)
    pair = gather(pair, "fsdp", between, 2)
    out_2 = swap(out_cols, "seq", 2)
    qkv = jnp.stack([dotg(wq, b, 0, 1).astype(bf16) for b in normed])
    length = lax.dynamic_index_in_dim(lengths, group, 0, keepdims=False)
    slot = (me & 1) * 2 + (me >> 1)
    info = [jnp.stack((slot, length, jnp.int32(h))).astype(jnp.int32) for h in range(heads)]

    att, lse, crossed, many = [None] * heads, [None] * heads, [None] * heads, heads - 1
    att[1], lse[1] = attend(info[1], qkv)
    pair, out_cols, out_2, cot_packet = after(att[1], pair, out_cols, out_2, cot_packet)
    up, down = pair[0], pair[1]
    (qkv,) = after((up, down), qkv)
    cot_packet = deal(cot_packet).reshape(span, -1)
    up_came = swap(up, "fsdp", low)
    down_2 = swap(down, "seq", 2)
    out_1, out_3 = swap(out_cols, "seq", 1), swap(out_2, "seq", 1)
    for h in range(2, heads):
        att[h], lse[h] = attend(info[h], qkv)
    att[1:], out_1, out_3, down = lax.optimization_barrier((att[1:], out_1, out_3, down))
    square = jax.ShapeDtypeStruct((width, width), bf16)
    (w_out_full,) = row_call(
        join_columns_body, "join_columns", [square], place, [out_cols, out_2, out_1, out_3], [None] * 4, [None]
    )
    (qkv,) = after((att[1:], w_out_full), qkv)
    crossed[1:] = [across(a) for a in att[1:]]
    down_came = swap(down, "fsdp", low)
    att[0], lse[0] = attend(info[0], qkv)
    up, up_came, down_2, att[0], crossed[1:] = lax.optimization_barrier((up, up_came, down_2, att[0], crossed[1:]))
    crossed[0] = across(att[0])
    up = join(up, up_came, "fsdp", low, last).reshape(width, ff // parts)

    crossed[0], up, down, down_came, down_2, cot_packet = lax.optimization_barrier(
        (crossed[0], up, down, down_came, down_2, cot_packet)
    )
    crossed = [piece for pieces in crossed for piece in pieces]
    up_2 = swap(up, "seq", 2)
    cot = cot_packet[:, :width]
    passes = cot_packet[:, width]
    cot_far = swap(cot, "seq", 1)
    down_2_came = swap(down_2, "fsdp", low)
    down = join(down, down_came, "fsdp", low, last).reshape(ff // parts, width)
    rows_f32 = jax.ShapeDtypeStruct((span, width), f32)
    rows_bf16 = jax.ShapeDtypeStruct((span, width), bf16)
    residual, nm = row_call(
        project_out_body, "project_out", [rows_f32, rows_bf16], place,
        [*crossed, w_out_full, inputs, gain_two[None]], [1] * len(crossed) + [None, 0, None], [0, 0], parts,
    )
    nm_far = swap(nm, "seq", 1)
    *near, up_0, down_0 = mlp_part(nm, cot, up, down)
    *far, up_1, down_1 = mlp_part(nm_far, cot_far, up, down)
    down_2, down_2_came, up_2 = after(far[0], down_2, down_2_came, up_2)
    down_2 = join(down_2, down_2_came, "fsdp", low, last).reshape(ff // parts, width)
    *far, d_up_2, d_down_2 = mlp_part(nm_far, cot_far, up_2, down_2, far)
    far = [swap(a.astype(bf16), "seq", 1) for a in far]
    *near, up_2, down_2 = mlp_part(nm, cot, up_2, down_2, near)
    up_2 = add(up_2, d_up_2)
    down = jnp.stack((add(down_0, down_1), add(down_2, d_down_2))).reshape(2, *sizes, ff_each, width)
    down = halve(down, "fsdp", low, last + 1)
    head_rows = jax.ShapeDtypeStruct((part, span), bf16)
    result, d_residual, d_branch, d_gain_mlp, *d_heads = row_call(
        turn_body,
        "turn",
        [rows_bf16, rows_f32, rows_bf16, jax.ShapeDtypeStruct((1, width), f32)] + [head_rows] * parts,
        place,
        [residual, near[0], far[0], near[1], far[1], cot, gain_two[None], w_out_full],
        [0] * 6 + [None] * 2,
        [0, 0, 0, None] + [1] * parts,
        parts,
    )
    d_heads = across(d_heads)
    piece = jax.ShapeDtypeStruct((width, part), bf16)
    d_out, d_out_x, *d_out_far = row_call(
        out_grad_body, "out_grad", [piece] * 4, place, [*crossed, d_branch], [None] * (len(crossed) + 1), [None] * 4,
        scratch=[pltpu.VMEM((width, width), bf16)],
    )
    d_heads, d_out, d_out_x, d_out_far, up_0, up_1, up_2, result = lax.optimization_barrier(
        (d_heads, d_out, d_out_x, d_out_far, up_0, up_1, up_2, result)
    )

    up_came = swap(up_2, "seq", 2)
    out_back = deal(result.reshape(groups, local_len, width))
    d_out_1, d_out_3 = [swap(a, "seq", 1) for a in d_out_far]
    d_qkv = [attend_back(info[0], qkv, att[0], d_heads, lse[0])]
    down, d_out_x, d_out_3 = after(d_qkv, down, d_out_x, d_out_3)
    down = halve(down[0], "fsdp", f_bits[-2], last, down[1])
    d_out_x = add(d_out_x, d_out_3)
    d_heads = after((down[0], d_out_x), d_heads)[0]
    d_out_x = swap(d_out_x, "seq", 2)
    for h in range(1, many):
        d_qkv.append(attend_back(info[h], qkv, att[h], d_heads, lse[h]))
    up_0, up_1, up_came, down, d_out_x, out_back = after(d_qkv, up_0, up_1, up_came, down, d_out_x, out_back)
    split = lambda a: a.reshape(*sizes, own_rows, ff // parts)
    up = halve(split(up_0), "fsdp", low, last, split(up_1), split(up_came))
    for k in reversed(range(last - 1)):
        down = halve(down[0], "fsdp", f_bits[k], k + 1, down[1])
    (d_heads,) = after((up[0], down[0], out_back), d_heads)
    d_qkv.append(attend_back(info[many], qkv, att[many], d_heads, lse[many]))
    d_qkv, down, up = lax.optimization_barrier((d_qkv, down, up))

    half = jax.ShapeDtypeStruct((2, span, width), bf16)
    project_back = lambda a: row_call(rows_grad_body, "rows_grad", [half], place, [*a, packet], [None] * (heads + 1), [None])[0]
    d_far = swap(project_back([d[2:] for d in d_qkv]), "seq", 1)
    d_near = project_back([d[:2] for d in d_qkv])
    (d_tail,) = after(d_near, d_qkv)
    down = add(*down)
    up = halve(up[0], "fsdp", f_bits[-2], last - 1, up[1])
    (d_wq,) = row_call(
        weight_grad_body, "weight_grad", [square], place, [*normed, *d_tail, d_out, d_out_1, d_out_x],
        [None] * (7 + heads), [None],
    )
    d_near, d_wq, up = lax.optimization_barrier((d_near, d_wq, up))
    d_wq = halve(d_wq.reshape(*sizes, own_rows, width), "fsdp", low, last)
    for k in reversed(range(last - 1)):
        up = halve(up[0], "fsdp", f_bits[k], k, up[1])
    (d_near,) = after(up[0], d_near)
    d_near = add(d_near, d_far)
    d_came = swap(d_near[1], "seq", 2)
    d_wq = halve(d_wq[0], "fsdp", f_bits[-2], last - 1, d_wq[1])
    d_wq, down = after(d_came, d_wq, down)
    down_came = swap(down[1], "seq", 2)
    for k in reversed(range(last - 1)):
        d_wq = halve(d_wq[0], "fsdp", f_bits[k], k, d_wq[1])
    d_normed = d_near[0].astype(f32) + d_came.astype(f32)
    z_one, inverse_one = norm_stats(inputs.astype(f32))
    d_in_norm, d_gain_attn = norm_back(z_one, inverse_one, gain_one, d_normed)
    d_inputs = (d_residual + d_in_norm).astype(bf16)
    d_back = deal(d_inputs.reshape(groups, local_len, width))
    up, d_wq = after(d_inputs, up, d_wq)
    pair = jnp.stack((add(*up), add(down[0], down_came)))
    grads = gather(pair, "seq", (2, 1)).reshape(parts, 2, own_rows, width)
    (g_up,) = row_call(
        functools.partial(place_up_body, each=ff_each), "place_up",
        [jax.ShapeDtypeStruct((own_rows, ff), f32)], place, [grads[:, 0]], [None], [None],
    )
    g_down = grads[:, 1].reshape(ff // groups, width).astype(f32)

    count = table.shape[0]
    picks = (passes[None, :] == jnp.arange(count, dtype=jnp.int32)[:, None].astype(bf16)).astype(bf16)
    d_table = jnp.dot(picks, d_inputs, preferred_element_type=f32)
    small = jnp.concatenate((d_table, d_gain_attn, d_gain_mlp, jnp.zeros_like(d_gain_mlp)), axis=0)
    for bit in (1, 2):
        small = small + swap(small, "seq", bit)
    for bit in reversed(f_bits[1:]):
        small = small + swap(small, "fsdp", bit)
    (small,) = after(d_back, small)
    small = small + swap(small, "fsdp", top)
    owned_gain = lambda row: lax.dynamic_slice_in_dim(small[row], group * own_rows, own_rows)

    d_wq = gather(add(*d_wq), "seq", (2, 1)).reshape(parts, own_rows, width)
    g_qkv, g_out = row_call(
        place_qkv_body, "place_qkv",
        [jax.ShapeDtypeStruct((own_rows, 3 * width), f32), jax.ShapeDtypeStruct((own_rows, width), f32)],
        place, [d_wq], [None], [None] * 2,
    )
    return (
        jnp.swapaxes(out_back, 0, 1),
        jnp.swapaxes(d_back, 0, 1),
        small[:count],
        owned_gain(count),
        g_qkv,
        g_out,
        owned_gain(count + 1),
        g_up,
        g_down,
    )


def solution(mesh):
    return jax.shard_map(
        per_device,
        mesh=mesh,
        in_specs=(
            P(("seq", "fsdp"), None, None),
            P(("seq", "fsdp"), None),
            P(),
            P(),
            P("fsdp"),
            P("fsdp", None),
            P("fsdp", None),
            P("fsdp"),
            P("fsdp", None),
            P("fsdp", None),
            P(("seq", "fsdp"), None, None),
        ),
        out_specs=(
            P(("seq", "fsdp"), None, None),
            P(("seq", "fsdp"), None, None),
            P(),
            P("fsdp"),
            P("fsdp", None),
            P("fsdp", None),
            P("fsdp"),
            P("fsdp", None),
            P("fsdp", None),
        ),
        check_vma=False,
    )
```
